32 devices in a mesh: ctx: 8 (over y, x, core), fsdp: 4 (over z).
Axes of the slice: x: 2, y: 2, z: 4, core: 2. Of those that a mesh axis runs over, the one named last changes fastest.
Arguments:
- tokens: bfloat16 [4, 2, 8, 64, 2048], P('fsdp', None, 'ctx'), may hold values from -6 to 6
- segment_ids: int32 [4, 1024], P('fsdp'), may hold values from 0 to 2, never falling along the last dimension, each value on 1 to 512 neighbouring positions
- cotangent: bfloat16 [4, 2, 8, 64, 2048], P('fsdp', None, 'ctx'), may hold values from -6 to 6
- norm_attn: bfloat16 [2048], P('fsdp'), may hold values from 0.25 to 1.75
- w_query: bfloat16 [2048, 2048], P('fsdp'), may hold values from -0.125 to 0.125
- w_key: bfloat16 [2048, 1024], P('fsdp'), may hold values from -0.125 to 0.125
- w_value: bfloat16 [2048, 1024], P('fsdp'), may hold values from -0.125 to 0.125
- q_gain: bfloat16 [128], P('fsdp'), may hold values from 0.25 to 1.75
- k_gain: bfloat16 [128], P('fsdp'), may hold values from 0.25 to 1.75
- w_out: bfloat16 [2048, 2048], P('fsdp'), may hold values from -1 to 1
- norm_ffn: bfloat16 [2048], P('fsdp'), may hold values from 0.25 to 1.75
- w_gate: bfloat16 [2048, 6144], P('fsdp'), may hold values from -0.125 to 0.125
- w_up: bfloat16 [2048, 6144], P('fsdp'), may hold values from -0.125 to 0.125
- w_down: bfloat16 [6144, 2048], P('fsdp'), may hold values from -0.078125 to 0.078125
Outputs:
- block_out: bfloat16 [4, 2, 8, 64, 2048], P('fsdp', None, 'ctx')
- input_grad: float32 [4, 2, 8, 64, 2048], P('fsdp', None, 'ctx')
- grad_norm_attn: float32 [2048], P(('ctx', 'fsdp'))
- grad_query: float32 [2048, 2048], P(('ctx', 'fsdp'))
- grad_key: float32 [2048, 1024], P(('ctx', 'fsdp'))
- grad_value: float32 [2048, 1024], P(('ctx', 'fsdp'))
- grad_q_gain: float32 [128], P(('ctx', 'fsdp'))
- grad_k_gain: float32 [128], P(('ctx', 'fsdp'))
- grad_out_proj: float32 [2048, 2048], P(('ctx', 'fsdp'))
- grad_norm_ffn: float32 [2048], P(('ctx', 'fsdp'))
- grad_gate: float32 [2048, 6144], P(('ctx', 'fsdp'))
- grad_up: float32 [2048, 6144], P(('ctx', 'fsdp'))
- grad_down: float32 [6144, 2048], P(('ctx', 'fsdp'))
The draws below stay inside these ranges and needn't reach their ends.
All inputs are finite; a program needn't handle non-finite values.
Results may differ from the reference program's by a relative error of at most 0.02.
Values may be sent and summed in bfloat16 or wider, within the bound.
No kernel may reach another device: no remote copies, remote signals or barrier semaphores. Data moves between devices by JAX's collectives and lax.ppermute only.
A program may use at most 448 MiB of HBM per device.

```python
import math
import jax
import jax.numpy as jnp
import numpy as np
from jax import lax

D = 2048
H = 16
KVH = 8
HD = 128
FF = 6144
BLOCK = 64
DOCS = 3
QD = 2048
KVD = 1024
SEQ_LEN = 1024
NSEQ = 4
N_CTX = 8


def steps_of(stream_key, extent, shards, least, largest):
    level = 1.0
    for position, parts in shards:
        draws = jax.random.uniform(jax.random.fold_in(jax.random.fold_in(stream_key, 6), position), (parts,), jnp.float32, least / len(shards), largest / len(shards))
        level = level * jnp.repeat(jnp.exp(draws), extent[position] // parts).reshape((-1,) + (1,) * (len(extent) - 1 - position))
    return level


def split_up(number_of, total, bound, lean):
    loads = [(1 << 20) // math.isqrt(rank ** lean) + 1 for rank in range(2, number_of + 1)]
    surplus, given = total - bound - (number_of - 1), [1] * (number_of - 1)
    while surplus > 0:
        movable = [i for i in range(number_of - 1) if given[i] < bound]
        whole, left = sum([loads[i] for i in movable]), surplus
        for i in movable:
            more = min(bound - given[i], max(1, left * loads[i] // whole), surplus)
            given[i] = given[i] + more
            surplus = surplus - more
    return np.array([bound] + given)


def uneven(key, amount, total, most, slope):
    if amount == 2:
        one = jax.random.randint(key, (), max(1, total - most), min(most, total - 1) + 1)
        return jnp.stack([one, total - one])
    tallies = jnp.asarray(split_up(amount, total, most, slope), jnp.int32)
    couples = (amount - 1) // 2
    giver, taker = tallies[1:1 + 2 * couples:2], tallies[2:2 + 2 * couples:2]
    margin = jnp.minimum(giver - 1, most - taker)
    shifted = jax.random.randint(jax.random.fold_in(key, 1), (couples,), 0, 1 << 20) % (margin + 1)
    tallies = tallies.at[1:1 + 2 * couples:2].set(giver - shifted).at[2:2 + 2 * couples:2].set(taker + shifted)
    return tallies[jax.random.permutation(jax.random.fold_in(key, 2), amount)]


def scatter_about(stream_key, extent, deviation, most, pieces=(), kind=jnp.bfloat16):
    entries = jax.random.normal(stream_key, extent, jnp.float32) * deviation
    if len(pieces) > 0:
        entries = steps_of(stream_key, extent, pieces, -0.22, 0.18) * entries
    return jnp.clip(entries, min=-most, max=most).astype(kind)


def setup_inputs(seed: int = 0) -> dict:
    keys = jax.random.split(jax.random.key(seed), 15)
    return {
        "tokens": scatter_about(keys[0], (NSEQ, 2, N_CTX, BLOCK, D), 1.0, 6.0, ((0, 4), (2, 8))),
        "segment_ids": jax.vmap(lambda own: jnp.searchsorted(jnp.cumsum(uneven(own, DOCS, SEQ_LEN, SEQ_LEN // 2, 1)), jnp.arange(SEQ_LEN), side="right"))(jax.random.split(keys[1], NSEQ)).reshape((NSEQ, SEQ_LEN)).astype(jnp.int32),
        "cotangent": scatter_about(keys[2], (NSEQ, 2, N_CTX, BLOCK, D), 1.0, 6.0, ((0, 4), (2, 8))),
        "norm_attn": jnp.clip(1.0 + 0.15 * jax.random.normal(keys[3], (D,), jnp.float32), 0.25, 1.75).astype(jnp.bfloat16),
        "w_query": scatter_about(keys[4], (D, QD), D ** -0.5, 0.125, ((0, 4),)),
        "w_key": scatter_about(keys[5], (D, KVD), D ** -0.5, 0.125, ((0, 4),)),
        "w_value": scatter_about(keys[6], (D, KVD), D ** -0.5, 0.125, ((0, 4),)),
        "q_gain": jnp.clip(1.0 + 0.15 * jax.random.normal(keys[7], (HD,), jnp.float32), 0.25, 1.75).astype(jnp.bfloat16),
        "k_gain": jnp.clip(1.0 + 0.15 * jax.random.normal(keys[8], (HD,), jnp.float32), 0.25, 1.75).astype(jnp.bfloat16),
        "w_out": scatter_about(keys[9], (QD, D), (QD // 64) ** -0.5, 1.0, ((0, 4),)),
        "norm_ffn": jnp.clip(1.0 + 0.15 * jax.random.normal(keys[10], (D,), jnp.float32), 0.25, 1.75).astype(jnp.bfloat16),
        "w_gate": scatter_about(keys[11], (D, FF), D ** -0.5, 0.125, ((0, 4),)),
        "w_up": scatter_about(keys[12], (D, FF), D ** -0.5, 0.125, ((0, 4),)),
        "w_down": scatter_about(keys[13], (FF, D), FF ** -0.5, 0.078125, ((0, 4),)),
    }


@jax.custom_vjp
def low(v):
    return lax.optimization_barrier(v.astype(jnp.bfloat16)).astype(jnp.float32)

@jax.custom_vjp
def low_back(v):
    return v

def low_keep(v):
    return (low(v), None)

def low_pass(kept, grad):
    return (grad,)

def back_keep(v):
    return (v, None)

def back_low(kept, grad):
    return (low(grad),)
low.defvjp(low_keep, low_pass)
low_back.defvjp(back_keep, back_low)
epsilon = 1e-06
theta_base = 1000000.0
highest = lax.Precision.HIGHEST

def doc_places(segments):
    length = segments.shape[0]
    row_index = jnp.arange(length, dtype=jnp.int32)
    before = jnp.concatenate([jnp.full((1,), -1, jnp.int32), segments[:-1]])
    starts = jnp.where(segments != before, row_index, jnp.zeros_like(row_index))
    return row_index - lax.cummax(starts, axis=0)

def rope_tables(places):
    frequency = theta_base ** (-(jnp.arange(HD // 2, dtype=jnp.float32) * 2.0) / HD)
    angles = places.astype(jnp.float32)[:, None] * frequency[None, :]
    angles = jnp.concatenate([angles, angles], axis=-1)
    return (jnp.cos(angles), jnp.sin(angles))

def rotate_half(values):
    middle_index = values.shape[-1] // 2
    return jnp.concatenate([-values[..., middle_index:], values[..., :middle_index]], axis=-1)

def rms_scale(values, gain):
    factor = lax.rsqrt(lax.optimization_barrier(jnp.mean(values * values, axis=-1, keepdims=True)) + epsilon)
    return values * factor * gain

def product(left, right):
    return jnp.dot(left, right, precision=highest)

def one_sequence(params, inputs):
    features, segments = inputs
    gain_attn, query_w, key_w, value_w, query_gain, key_gain, out_w, gain_ffn, gate_w, up_w, down_w = params
    length = features.shape[0]
    group_size = H // KVH
    score_scale = HD ** (-0.5)
    cosine_table, sine_table = rope_tables(doc_places(segments))
    cosine_table = cosine_table[:, None, :]
    sine_table = sine_table[:, None, :]
    row_index = jnp.arange(length, dtype=jnp.int32)
    visible = (segments[:, None] == segments[None, :]) & (row_index[None, :] <= row_index[:, None])
    normed = low(rms_scale(features, gain_attn))
    query_raw = low_back(product(normed, query_w)).reshape(length, H, HD)
    key_raw = low_back(product(normed, key_w)).reshape(length, KVH, HD)
    values = low_back(low(product(normed, value_w))).reshape(length, KVH, HD)
    query_norm = rms_scale(query_raw, query_gain)
    key_norm = rms_scale(key_raw, key_gain)
    queries = low(query_norm * cosine_table + rotate_half(query_norm) * sine_table)
    key_rows = low(key_norm * cosine_table + rotate_half(key_norm) * sine_table)
    query_heads = queries.reshape(length, KVH, group_size, HD).transpose(1, 2, 0, 3)
    key_heads = key_rows.transpose(1, 0, 2)
    value_heads = values.transpose(1, 0, 2)

    def one_head(triple):
        query_block, key_block, value_block = triple
        scores = low_back(score_scale * jnp.einsum('gtd,kd->gtk', query_block, key_block, precision=highest))
        scores = jnp.where(visible[None], scores, -jnp.inf)
        row_peak = lax.optimization_barrier(jnp.max(scores, axis=-1, keepdims=True))
        powers = jnp.exp(scores - row_peak)
        attention_weights = low(powers / lax.optimization_barrier(jnp.sum(powers, axis=-1, keepdims=True)))
        return jnp.einsum('gtk,kd->tgd', attention_weights, value_block, precision=highest)
    mixed_heads = lax.map(jax.checkpoint(one_head), (query_heads, key_heads, value_heads))
    attended = low_back(low(mixed_heads.transpose(1, 0, 2, 3).reshape(length, H * HD)))
    branch = low_back(product(attended, out_w))
    middle = features + branch
    normed_ffn = low(rms_scale(middle, gain_ffn))
    gate_proj = low_back(product(normed_ffn, gate_w))
    up_proj = low_back(product(normed_ffn, up_w))
    hidden = low(jax.nn.silu(gate_proj) * up_proj)
    return middle + low_back(product(hidden, down_w))

def reference(tokens, segment_ids, cotangent, norm_attn, w_query, w_key, w_value, q_gain, k_gain, w_out, norm_ffn, w_gate, w_up, w_down):

    def natural(stacked):
        joined = jnp.concatenate([stacked[:, 0], stacked[:, 1, ::-1]], axis=1)
        return joined.reshape(joined.shape[0], -1, joined.shape[-1])

    def dealt_order(stacked):
        blocks = stacked.reshape(stacked.shape[0], 2 * N_CTX, BLOCK, stacked.shape[-1])
        return jnp.stack([blocks[:, :N_CTX], blocks[:, N_CTX:][:, ::-1]], axis=1)
    features = natural(tokens.astype(jnp.float32))
    incoming = natural(cotangent.astype(jnp.float32))
    params = tuple((weight.astype(jnp.float32) for weight in (norm_attn, w_query, w_key, w_value, q_gain, k_gain, w_out, norm_ffn, w_gate, w_up, w_down)))
    checked = jax.checkpoint(one_sequence)

    def forward(inputs, weights_all):
        return lax.map(lambda sequence: checked(weights_all, sequence), (inputs, segment_ids))
    outputs, pullback = jax.vjp(forward, features, params)
    input_grad, grads = pullback(incoming)
    return (dealt_order(outputs).astype(jnp.bfloat16), dealt_order(input_grad), grads[0], grads[1], grads[2], grads[3], grads[4], grads[5], grads[6], grads[7], grads[8], grads[9], grads[10])
```

```python
import functools

import jax
import jax.numpy as jnp
from jax import lax
from jax.experimental import pallas as pl
from jax.experimental.pallas import tpu as pltpu
from jax.sharding import PartitionSpec as P

H = 16
KVH = 8
HD = 128
BLOCK = 64
TILE = 256

epsilon = 1e-06
theta_base = 1000000.0
score_scale = HD ** (-0.5)
low = jnp.bfloat16
high = jnp.float32
vmem_bytes = 48 << 20


def dot(left, right):
    return jnp.dot(left, right, preferred_element_type=high)


def dot_t(left, right):
    return lax.dot_general(left, right, (((1,), (1,)), ((), ())), preferred_element_type=high)


def t_dot(left, right):
    return lax.dot_general(left, right, (((0,), (0,)), ((), ())), preferred_element_type=high)


def mean_last(values):
    return jnp.mean(values, axis=-1, keepdims=True)


def rms_factor(values):
    return lax.rsqrt(mean_last(values * values) + epsilon)


def head_cols(head):
    return slice(head * HD, (head + 1) * HD)


def visible_tile(segc_ref, segr_ref, first, keys):
    rows = lax.broadcasted_iota(jnp.int32, (TILE, keys), 0) + first
    cols = lax.broadcasted_iota(jnp.int32, (TILE, keys), 1)
    same = segc_ref[first : first + TILE, :] == segr_ref[:, :keys]
    return same & (cols <= rows)


def attend_kernel(
    sources_ref,
    places_ref,
    raw_ref,
    cos_ref,
    sin_ref,
    qg_ref,
    kg_ref,
    segc_ref,
    segr_ref,
    rel_ref,
    abs_ref,
    q_ref,
    k_ref,
    v_ref,
    log_ref,
):
    total = q_ref.shape[0]
    heads = q_ref.shape[1] // HD
    blocks = total // BLOCK

    def prepare(index, carry):
        source = pl.multiple_of(sources_ref[index] * BLOCK, BLOCK)
        target = pl.multiple_of(index * BLOCK, BLOCK)
        raw = raw_ref[pl.ds(source, BLOCK), :]
        cosine = cos_ref[pl.ds(target, BLOCK), :]
        sine = sin_ref[pl.ds(target, BLOCK), :]
        for head in range(heads + 1):
            values = raw[:, head_cols(head)]
            gain = qg_ref[...] if head < heads else kg_ref[...]
            normed = values * rms_factor(values) * gain
            turned = (normed * cosine + pltpu.roll(normed, HD // 2, 1) * sine).astype(low)
            if head < heads:
                q_ref[pl.ds(target, BLOCK), head_cols(head)] = turned
            else:
                k_ref[pl.ds(target, BLOCK), :] = turned
        v_ref[pl.ds(target, BLOCK), :] = raw[:, head_cols(heads + 1)].astype(low)
        return carry

    lax.fori_loop(0, blocks, prepare, 0)
    for tile in range(total // TILE):
        first = tile * TILE
        keys = first + TILE
        visible = visible_tile(segc_ref, segr_ref, first, keys)
        for head in range(heads):
            scores = dot_t(q_ref[first : first + TILE, head_cols(head)], k_ref[:keys, :])
            scores = jnp.where(visible, scores * score_scale, -jnp.inf)
            peak = jnp.max(scores, axis=-1, keepdims=True)
            powers = jnp.exp(scores - peak)
            sums = jnp.sum(powers, axis=-1, keepdims=True)
            probs = (powers / sums).astype(low)
            mixed = dot(probs, v_ref[:keys, :]).astype(low)
            log_ref[first : first + TILE, head : head + 1] = peak + jnp.log(sums)
            for part in range(TILE // BLOCK):
                index = first // BLOCK + part
                piece = mixed[part * BLOCK : (part + 1) * BLOCK, :]
                target = pl.multiple_of(sources_ref[index] * BLOCK, BLOCK)
                rel_ref[pl.ds(target, BLOCK), head_cols(head)] = piece
                target = pl.multiple_of(places_ref[index] * BLOCK, BLOCK)
                abs_ref[pl.ds(target, BLOCK), head_cols(head)] = piece


def attend_back_kernel(
    sources_ref,
    places_ref,
    raw_ref,
    cos_ref,
    sin_ref,
    qg_ref,
    kg_ref,
    segc_ref,
    segr_ref,
    q_ref,
    k_ref,
    v_ref,
    log_ref,
    up_ref,
    out_ref,
    gains_ref,
    dq_ref,
    dk_ref,
    dv_ref,
):
    total = q_ref.shape[0]
    heads = q_ref.shape[1] // HD
    blocks = total // BLOCK
    dk_ref[...] = jnp.zeros_like(dk_ref)
    dv_ref[...] = jnp.zeros_like(dv_ref)
    for tile in range(total // TILE):
        first = tile * TILE
        keys = first + TILE
        visible = visible_tile(segc_ref, segr_ref, first, keys)
        for head in range(heads):
            pieces = []
            for part in range(TILE // BLOCK):
                source = pl.multiple_of(places_ref[first // BLOCK + part] * BLOCK, BLOCK)
                pieces.append(up_ref[pl.ds(source, BLOCK), head_cols(head)])
            upstream = jnp.concatenate(pieces, axis=0)
            query = q_ref[first : first + TILE, head_cols(head)]
            key = k_ref[:keys, :]
            scores = dot_t(query, key) * score_scale
            shifted = scores - log_ref[first : first + TILE, head : head + 1]
            probs = jnp.exp(jnp.where(visible, shifted, -jnp.inf))
            dprobs = dot_t(upstream, v_ref[:keys, :])
            inner = jnp.sum(probs * dprobs, axis=-1, keepdims=True)
            dscores = (probs * (dprobs - inner)).astype(low)
            dq_ref[first : first + TILE, head_cols(head)] = dot(dscores, key) * score_scale
            dk_ref[:keys, :] += t_dot(dscores, query) * score_scale
            dv_ref[:keys, :] += t_dot(probs.astype(low), upstream)

    def finish(index, carry):
        target = pl.multiple_of(sources_ref[index] * BLOCK, BLOCK)
        source = pl.multiple_of(index * BLOCK, BLOCK)
        raw = raw_ref[pl.ds(target, BLOCK), :]
        cosine = cos_ref[pl.ds(source, BLOCK), :]
        sine = sin_ref[pl.ds(source, BLOCK), :]
        gains = list(carry)
        for head in range(heads + 1):
            values = raw[:, head_cols(head)]
            if head < heads:
                upstream, gain, slot = dq_ref[pl.ds(source, BLOCK), head_cols(head)], qg_ref[...], 0
            else:
                upstream, gain, slot = dk_ref[pl.ds(source, BLOCK), :], kg_ref[...], 1
            upstream = upstream * cosine - pltpu.roll(upstream, HD // 2, 1) * sine
            factor = rms_factor(values)
            gains[slot] = gains[slot] + jnp.sum(upstream * values * factor, axis=0, keepdims=True)
            scaled = gain * upstream
            inner = mean_last(values * scaled)
            back = factor * scaled - values * (factor * factor * factor) * inner
            out_ref[pl.ds(target, BLOCK), head_cols(head)] = back.astype(low)
        out_ref[pl.ds(target, BLOCK), head_cols(heads + 1)] = dv_ref[pl.ds(source, BLOCK), :].astype(low)
        return tuple(gains)

    zero = jnp.zeros((1, HD), high)
    query_gain, key_gain = lax.fori_loop(0, blocks, finish, (zero, zero))
    gains_ref[0:1, :] = query_gain
    gains_ref[1:2, :] = key_gain


def in_memory(kinds):
    return [pl.BlockSpec(memory_space=kind) for kind in kinds]


def attend(total, heads, *operands):
    shapes = (
        jax.ShapeDtypeStruct((total, heads * HD), low),
        jax.ShapeDtypeStruct((total, heads * HD), low),
        jax.ShapeDtypeStruct((total, heads * HD), low),
        jax.ShapeDtypeStruct((total, HD), low),
        jax.ShapeDtypeStruct((total, HD), low),
        jax.ShapeDtypeStruct((total, HD), high),
    )
    return pl.pallas_call(
        attend_kernel,
        out_shape=shapes,
        in_specs=in_memory([pltpu.SMEM] * 2 + [pltpu.VMEM] * (len(operands) - 2)),
        out_specs=in_memory([pltpu.VMEM] * len(shapes)),
        compiler_params=pltpu.CompilerParams(vmem_limit_bytes=vmem_bytes),
        name="attend",
    )(*operands)


def attend_back(total, heads, *operands):
    shapes = (
        jax.ShapeDtypeStruct((total, (heads + 2) * HD), low),
        jax.ShapeDtypeStruct((2, HD), high),
    )
    return pl.pallas_call(
        attend_back_kernel,
        out_shape=shapes,
        in_specs=in_memory([pltpu.SMEM] * 2 + [pltpu.VMEM] * (len(operands) - 2)),
        out_specs=in_memory([pltpu.VMEM] * len(shapes)),
        scratch_shapes=[
            pltpu.VMEM((total, heads * HD), high),
            pltpu.VMEM((total, HD), high),
            pltpu.VMEM((total, HD), high),
        ],
        compiler_params=pltpu.CompilerParams(vmem_limit_bytes=vmem_bytes),
        name="attend_back",
    )(*operands)


def swap(values, mask):
    size = lax.axis_size("ctx")
    return lax.ppermute(values, "ctx", [(i, i ^ mask) for i in range(size)])


def gather_ctx(values):
    size = lax.axis_size("ctx")
    half = [values] + [swap(values, mask) for mask in range(2, size, 2)]
    half = jnp.concatenate(half, axis=0)
    return jnp.concatenate([half, swap(half, 1)], axis=0)


def scatter_ctx(keep, give):
    size = lax.axis_size("ctx")
    chips = size // 2
    rows = keep.shape[0] // chips
    got = swap(give, 1)
    keep = keep.reshape(chips, rows, -1)
    got = got.reshape(chips, rows, -1)
    sums = [keep[i].astype(high) + got[i].astype(high) for i in range(chips)]
    total = sums[0]
    for i in range(1, chips):
        total = total + swap(sums[i].astype(low), 2 * i).astype(high)
    return total


def halves(values):
    middle = values.shape[0] // 2
    return values[:middle], values[middle:]


def partial_rows(left, right, product):
    keep, give = halves(left)
    give = product(give, right).astype(low)
    keep = product(keep, right).astype(low)
    return scatter_ctx(keep, give)


def columns_of(values, index, width):
    return lax.dynamic_slice_in_dim(values, index * width, width, axis=1)


def gather_rows(values):
    return lax.all_gather(values, "fsdp", axis=0, tiled=True)


def scatter_rows(values):
    return lax.psum_scatter(values.astype(low), "fsdp", scatter_dimension=0, tiled=True)


def local(
    tokens,
    segment_ids,
    cotangent,
    norm_attn,
    w_query,
    w_key,
    w_value,
    q_gain,
    k_gain,
    w_out,
    norm_ffn,
    w_gate,
    w_up,
    w_down,
):
    n = lax.axis_size("ctx")
    m = lax.axis_size("fsdp")
    me = lax.axis_index("ctx")
    layer = lax.axis_index("fsdp")
    width = tokens.shape[-1]
    own = 2 * BLOCK
    total = n * own
    heads = H // n
    repeat = n // KVH
    qw = heads * HD
    hidden = w_gate.shape[1] // n
    piece = hidden // m
    assert tokens.shape[0] == 1 and heads * n == H and repeat * KVH == n

    own_tokens = tokens.reshape(own, width)
    own_cotangent = cotangent.reshape(own, width)
    all_tokens = gather_ctx(own_tokens)

    small = jnp.concatenate([norm_attn, norm_ffn, q_gain, k_gain]).reshape(1, -1)
    small = lax.all_to_all(jnp.broadcast_to(small, (m, small.shape[1])), "fsdp", 0, 0, tiled=True)
    part, gain_part = norm_attn.shape[0], q_gain.shape[0]
    small = small.astype(high)
    gain_attn = small[:, :part].reshape(-1)
    gain_ffn = small[:, part : 2 * part].reshape(-1)
    query_gain = small[:, 2 * part : 2 * part + gain_part].reshape(1, HD)
    key_gain = small[:, 2 * part + gain_part :].reshape(1, HD)

    qkv_w = gather_rows(
        jnp.concatenate(
            [
                columns_of(w_query, me, qw),
                columns_of(w_key, me // repeat, HD),
                columns_of(w_value, me // repeat, HD),
            ],
            axis=1,
        )
    )
    out_cols = width // n
    out_w = gather_rows(columns_of(w_out, me, out_cols))

    def hidden_columns(weights):
        starts = [i * n * piece + me * piece for i in range(m)]
        return [lax.dynamic_slice_in_dim(weights, start, piece, axis=1) for start in starts]

    gate_up_w = gather_rows(jnp.concatenate(hidden_columns(w_gate) + hidden_columns(w_up), axis=1))
    down_w = gather_rows(lax.dynamic_slice_in_dim(w_down, me * piece, piece, axis=0))

    def slot_of(owner):
        mask = owner ^ me
        return (mask >> 1) + (mask & 1) * (n // 2)

    out_w = gather_ctx(out_w).reshape(n, -1, out_cols)

    natural = jnp.arange(2 * n, dtype=jnp.int32)
    side = (natural >= n).astype(jnp.int32)
    owner = jnp.where(side == 0, natural, 2 * n - 1 - natural)
    sources = 2 * slot_of(owner) + side
    places = 2 * owner + side

    segments = segment_ids.reshape(total)
    starts = jnp.sum((segments[None, :] < segments[:, None]).astype(jnp.int32), axis=1)
    place = jnp.arange(total, dtype=jnp.int32) - starts
    frequency = theta_base ** (-(jnp.arange(HD // 2, dtype=high) * 2.0) / HD)
    angles = place.astype(high)[:, None] * frequency
    cosine = jnp.cos(angles)
    sine = jnp.sin(angles)
    cosine = jnp.concatenate([cosine, cosine], axis=1)
    sine = jnp.concatenate([-sine, sine], axis=1)
    segment_column = segments.reshape(total, 1)
    segment_row = segments.reshape(1, total)

    features = all_tokens.astype(high)
    normed_low = (features * rms_factor(features) * gain_attn).astype(low)
    qkv_raw = dot(normed_low, qkv_w)
    tables = (cosine, sine, query_gain, key_gain, segment_column, segment_row)
    mixed_rel, mixed_abs, query, key, value, logs = attend(
        total, heads, sources, places, qkv_raw, *tables
    )
    mixed = lax.all_to_all(mixed_abs.reshape(n, own, qw), "ctx", 0, 0, tiled=True)
    mixed = mixed.transpose(1, 0, 2).reshape(own, n * qw)
    own_features = own_tokens.astype(high)
    branch = [dot(mixed, out_w[i]) for i in range(n)]
    branch = jnp.stack(branch)
    branch = [lax.dynamic_index_in_dim(branch, slot_of(i), axis=0, keepdims=False) for i in range(n)]
    middle = own_features + jnp.concatenate(branch, axis=1)
    factor_ffn = rms_factor(middle)
    ffn_low = gather_ctx((middle * factor_ffn * gain_ffn).astype(low))
    upstream_low = gather_ctx(own_cotangent)

    gate_up = dot(ffn_low, gate_up_w)
    gate, up = gate_up[:, :hidden], gate_up[:, hidden:]
    sigmoid = jax.nn.sigmoid(gate)
    silu = gate * sigmoid
    hidden_low = (silu * up).astype(low)
    block_sum = middle + partial_rows(hidden_low, down_w, dot)
    block_out = block_sum.astype(low).reshape(tokens.shape)

    grad_hidden = dot_t(upstream_low, down_w)
    slope = sigmoid * (1.0 + gate * (1.0 - sigmoid))
    gate_up_grad = jnp.concatenate(
        [(grad_hidden * up * slope).astype(low), (grad_hidden * silu).astype(low)], axis=1
    )
    grad_ffn = partial_rows(gate_up_grad, gate_up_w, dot_t)
    upstream = own_cotangent.astype(high)
    scaled = gain_ffn * grad_ffn
    inner = mean_last(middle * scaled)
    grad_middle = upstream + factor_ffn * scaled - middle * factor_ffn**3 * inner
    grad_gain_ffn = jnp.sum(grad_ffn * middle * factor_ffn, axis=0)
    middle_low = grad_middle.astype(low)

    mixed_grad = 0.0
    for mask in range(n):
        slot = (mask >> 1) + (mask & 1) * (n // 2)
        mixed_grad = mixed_grad + dot_t(columns_of(middle_low, me ^ mask, out_cols), out_w[slot])
    mixed_grad = mixed_grad.astype(low).reshape(own, n, qw).transpose(1, 0, 2)
    mixed_grad = lax.all_to_all(mixed_grad, "ctx", 0, 0, tiled=True).reshape(total, qw)
    qkv_grad, grad_gains = attend_back(
        total, heads, sources, places, qkv_raw, *tables, query, key, value, logs, mixed_grad
    )
    grad_attn = partial_rows(qkv_grad, qkv_w, dot_t)
    factor_attn = rms_factor(own_features)
    scaled = gain_attn * grad_attn
    inner = mean_last(own_features * scaled)
    input_grad = grad_middle + factor_attn * scaled - own_features * factor_attn**3 * inner
    grad_gain_attn = jnp.sum(grad_attn * own_features * factor_attn, axis=0)
    input_grad = input_grad.reshape(tokens.shape)

    strip = width // (n * m)

    def grad_rows(left, right):
        grads = t_dot(left, right).astype(low).reshape(n, m, strip, right.shape[1])
        grads = grads.transpose(1, 0, 2, 3).reshape(width, right.shape[1])
        grads = scatter_rows(grads).reshape(n, strip, right.shape[1])
        return lax.all_to_all(grads, "ctx", 0, 0, tiled=True).astype(high)

    grad_down = scatter_rows(t_dot(hidden_low, upstream_low))
    targets = []
    for device in range(n * m):
        block = (device % m) * n + device // m
        targets.append((device, block))
    grad_down = lax.ppermute(grad_down, ("ctx", "fsdp"), targets).astype(high)
    grad_gate_up = grad_rows(ffn_low, gate_up_grad).reshape(n, strip, 2, m, piece)
    grad_gate_up = grad_gate_up.transpose(2, 1, 3, 0, 4).reshape(2, strip, -1)
    grad_out = scatter_rows(t_dot(mixed_rel, gather_ctx(middle_low))).astype(high)
    grad_qkv = grad_rows(normed_low, qkv_grad)
    grad_query = grad_qkv[:, :, :qw].transpose(1, 0, 2).reshape(strip, -1)

    def grad_of_kv(grads):
        grads = jnp.sum(grads.reshape(KVH, repeat, strip, HD), axis=1)
        return grads.transpose(1, 0, 2).reshape(strip, -1)

    grad_key = grad_of_kv(grad_qkv[:, :, qw : qw + HD])
    grad_value = grad_of_kv(grad_qkv[:, :, qw + HD :])

    devices = n * m
    partial = jnp.concatenate(
        [
            grad_gain_attn.reshape(devices, -1),
            grad_gain_ffn.reshape(devices, -1),
            grad_gains[0].reshape(devices, -1),
            grad_gains[1].reshape(devices, -1),
        ],
        axis=1,
    )
    gains = jnp.sum(lax.all_to_all(partial, ("ctx", "fsdp"), 0, 0, tiled=True), axis=0)
    end = 2 * strip + HD // devices
    return (
        block_out,
        input_grad,
        gains[:strip],
        grad_query,
        grad_key,
        grad_value,
        gains[2 * strip : end],
        gains[end:],
        grad_out,
        gains[strip : 2 * strip],
        grad_gate_up[0],
        grad_gate_up[1],
        grad_down,
    )


def solution(mesh):
    rows = P("fsdp", None)
    line = P("fsdp")
    blocks = P("fsdp", None, "ctx", None, None)
    both = P(("ctx", "fsdp"), None)
    both_line = P(("ctx", "fsdp"))
    in_specs = (blocks, rows, blocks, line, rows, rows, rows, line, line, rows, line, rows, rows, rows)
    out_specs = (
        blocks,
        blocks,
        both_line,
        both,
        both,
        both,
        both_line,
        both_line,
        both,
        both_line,
        both,
        both,
        both,
    )
    return jax.shard_map(local, mesh=mesh, in_specs=in_specs, out_specs=out_specs, check_vma=False)
```

```python
import math

import jax
import jax.numpy as jnp
from jax import lax
from jax.experimental import pallas as pl
from jax.experimental.pallas import tpu as pltpu
from jax.sharding import Mesh
from jax.sharding import PartitionSpec as P

H = 16
KVH = 8
HD = 128
BLOCK = 64
TILE = 256

epsilon = 1e-06
theta_base = 1000000.0
score_scale = HD ** (-0.5)
low = jnp.bfloat16
high = jnp.float32
vmem_bytes = 48 << 20


def dot(left, right):
    return jnp.dot(left, right, preferred_element_type=high)


def dot_t(left, right):
    return lax.dot_general(left, right, (((1,), (1,)), ((), ())), preferred_element_type=high)


def t_dot(left, right):
    return lax.dot_general(left, right, (((0,), (0,)), ((), ())), preferred_element_type=high)


def mean_last(values):
    return jnp.mean(values, axis=-1, keepdims=True)


def rms_factor(values):
    return lax.rsqrt(mean_last(values * values) + epsilon)


def head_cols(head):
    return slice(head * HD, (head + 1) * HD)


def visible_tile(segc_ref, segr_ref, first, keys):
    rows = lax.broadcasted_iota(jnp.int32, (TILE, keys), 0) + first
    cols = lax.broadcasted_iota(jnp.int32, (TILE, keys), 1)
    same = segc_ref[first : first + TILE, :] == segr_ref[:, :keys]
    return same & (cols <= rows)


def attend_kernel(
    sources_ref,
    places_ref,
    raw_ref,
    cos_ref,
    sin_ref,
    qg_ref,
    kg_ref,
    segc_ref,
    segr_ref,
    rel_ref,
    abs_ref,
    q_ref,
    k_ref,
    v_ref,
    log_ref,
):
    total = q_ref.shape[0]
    heads = q_ref.shape[1] // HD
    blocks = total // BLOCK

    def prepare(index, carry):
        source = pl.multiple_of(sources_ref[index] * BLOCK, BLOCK)
        target = pl.multiple_of(index * BLOCK, BLOCK)
        raw = raw_ref[pl.ds(source, BLOCK), :]
        cosine = cos_ref[pl.ds(target, BLOCK), :]
        sine = sin_ref[pl.ds(target, BLOCK), :]
        for head in range(heads + 1):
            values = raw[:, head_cols(head)]
            gain = qg_ref[...] if head < heads else kg_ref[...]
            normed = values * rms_factor(values) * gain
            turned = (normed * cosine + pltpu.roll(normed, HD // 2, 1) * sine).astype(low)
            if head < heads:
                q_ref[pl.ds(target, BLOCK), head_cols(head)] = turned
            else:
                k_ref[pl.ds(target, BLOCK), :] = turned
        v_ref[pl.ds(target, BLOCK), :] = raw[:, head_cols(heads + 1)].astype(low)
        return carry

    lax.fori_loop(0, blocks, prepare, 0)
    for tile in range(total // TILE):
        first = tile * TILE
        keys = first + TILE
        visible = visible_tile(segc_ref, segr_ref, first, keys)
        for head in range(heads):
            scores = dot_t(q_ref[first : first + TILE, head_cols(head)], k_ref[:keys, :])
            scores = jnp.where(visible, scores * score_scale, -jnp.inf)
            peak = jnp.max(scores, axis=-1, keepdims=True)
            powers = jnp.exp(scores - peak)
            sums = jnp.sum(powers, axis=-1, keepdims=True)
            probs = (powers / sums).astype(low)
            mixed = dot(probs, v_ref[:keys, :]).astype(low)
            log_ref[first : first + TILE, head : head + 1] = peak + jnp.log(sums)
            for part in range(TILE // BLOCK):
                index = first // BLOCK + part
                piece = mixed[part * BLOCK : (part + 1) * BLOCK, :]
                target = pl.multiple_of(sources_ref[index] * BLOCK, BLOCK)
                rel_ref[pl.ds(target, BLOCK), head_cols(head)] = piece
                target = pl.multiple_of(places_ref[index] * BLOCK, BLOCK)
                abs_ref[pl.ds(target, BLOCK), head_cols(head)] = piece


def attend_back_kernel(
    sources_ref,
    places_ref,
    raw_ref,
    cos_ref,
    sin_ref,
    qg_ref,
    kg_ref,
    segc_ref,
    segr_ref,
    q_ref,
    k_ref,
    v_ref,
    log_ref,
    up_ref,
    out_ref,
    gains_ref,
    dq_ref,
    dk_ref,
    dv_ref,
):
    total = q_ref.shape[0]
    heads = q_ref.shape[1] // HD
    blocks = total // BLOCK
    dk_ref[...] = jnp.zeros_like(dk_ref)
    dv_ref[...] = jnp.zeros_like(dv_ref)
    for tile in range(total // TILE):
        first = tile * TILE
        keys = first + TILE
        visible = visible_tile(segc_ref, segr_ref, first, keys)
        for head in range(heads):
            pieces = []
            for part in range(TILE // BLOCK):
                source = pl.multiple_of(places_ref[first // BLOCK + part] * BLOCK, BLOCK)
                pieces.append(up_ref[pl.ds(source, BLOCK), head_cols(head)])
            upstream = jnp.concatenate(pieces, axis=0)
            query = q_ref[first : first + TILE, head_cols(head)]
            key = k_ref[:keys, :]
            scores = dot_t(query, key) * score_scale
            shifted = scores - log_ref[first : first + TILE, head : head + 1]
            probs = jnp.exp(jnp.where(visible, shifted, -jnp.inf))
            dprobs = dot_t(upstream, v_ref[:keys, :])
            inner = jnp.sum(probs * dprobs, axis=-1, keepdims=True)
            dscores = (probs * (dprobs - inner)).astype(low)
            dq_ref[first : first + TILE, head_cols(head)] = dot(dscores, key) * score_scale
            dk_ref[:keys, :] += t_dot(dscores, query) * score_scale
            dv_ref[:keys, :] += t_dot(probs.astype(low), upstream)

    def finish(index, carry):
        target = pl.multiple_of(sources_ref[index] * BLOCK, BLOCK)
        source = pl.multiple_of(index * BLOCK, BLOCK)
        raw = raw_ref[pl.ds(target, BLOCK), :]
        cosine = cos_ref[pl.ds(source, BLOCK), :]
        sine = sin_ref[pl.ds(source, BLOCK), :]
        gains = list(carry)
        for head in range(heads + 1):
            values = raw[:, head_cols(head)]
            if head < heads:
                upstream, gain, slot = dq_ref[pl.ds(source, BLOCK), head_cols(head)], qg_ref[...], 0
            else:
                upstream, gain, slot = dk_ref[pl.ds(source, BLOCK), :], kg_ref[...], 1
            upstream = upstream * cosine - pltpu.roll(upstream, HD // 2, 1) * sine
            factor = rms_factor(values)
            gains[slot] = gains[slot] + jnp.sum(upstream * values * factor, axis=0, keepdims=True)
            scaled = gain * upstream
            inner = mean_last(values * scaled)
            back = factor * scaled - values * (factor * factor * factor) * inner
            out_ref[pl.ds(target, BLOCK), head_cols(head)] = back.astype(low)
        out_ref[pl.ds(target, BLOCK), head_cols(heads + 1)] = dv_ref[pl.ds(source, BLOCK), :].astype(low)
        return tuple(gains)

    zero = jnp.zeros((1, HD), high)
    query_gain, key_gain = lax.fori_loop(0, blocks, finish, (zero, zero))
    gains_ref[0:1, :] = query_gain
    gains_ref[1:2, :] = key_gain


def in_memory(kinds):
    return [pl.BlockSpec(memory_space=kind) for kind in kinds]


def attend(total, heads, *operands):
    shapes = (
        jax.ShapeDtypeStruct((total, heads * HD), low),
        jax.ShapeDtypeStruct((total, heads * HD), low),
        jax.ShapeDtypeStruct((total, heads * HD), low),
        jax.ShapeDtypeStruct((total, HD), low),
        jax.ShapeDtypeStruct((total, HD), low),
        jax.ShapeDtypeStruct((total, HD), high),
    )
    return pl.pallas_call(
        attend_kernel,
        out_shape=shapes,
        in_specs=in_memory([pltpu.SMEM] * 2 + [pltpu.VMEM] * (len(operands) - 2)),
        out_specs=in_memory([pltpu.VMEM] * len(shapes)),
        compiler_params=pltpu.CompilerParams(vmem_limit_bytes=vmem_bytes),
        name="attend",
    )(*operands)


def attend_back(total, heads, *operands):
    shapes = (
        jax.ShapeDtypeStruct((total, (heads + 2) * HD), low),
        jax.ShapeDtypeStruct((2, HD), high),
    )
    return pl.pallas_call(
        attend_back_kernel,
        out_shape=shapes,
        in_specs=in_memory([pltpu.SMEM] * 2 + [pltpu.VMEM] * (len(operands) - 2)),
        out_specs=in_memory([pltpu.VMEM] * len(shapes)),
        scratch_shapes=[
            pltpu.VMEM((total, heads * HD), high),
            pltpu.VMEM((total, HD), high),
            pltpu.VMEM((total, HD), high),
        ],
        compiler_params=pltpu.CompilerParams(vmem_limit_bytes=vmem_bytes),
        name="attend_back",
    )(*operands)


CTX = ("chip", "core")
LAYER = ("hi", "lo")


def swap(values, axis, mask=1):
    size = lax.axis_size(axis)
    return lax.ppermute(values, axis, [(i, i ^ mask) for i in range(size)])


def exchange(values, axis):
    return lax.all_to_all(values, axis, 0, 0, tiled=True)


def gather(values):
    copies = jnp.broadcast_to(values[None], (lax.axis_size("chip"),) + values.shape)
    half = exchange(copies, "chip").reshape(-1, values.shape[-1])
    return half, swap(half, "core")


def scatter(keep, give):
    size = lax.axis_size("chip")
    sums = (keep.astype(high) + swap(give, "core").astype(high)).astype(low)
    sums = exchange(sums.reshape(size, keep.shape[0] // size, -1), "chip")
    return jnp.sum(sums.astype(high), axis=0)


def spread(values, axis):
    return [values] + [swap(values, axis, mask) for mask in range(1, lax.axis_size(axis))]


def in_order(pieces, index):
    rows = pieces[0].shape[0]
    whole = jnp.zeros((len(pieces) * rows,) + pieces[0].shape[1:], pieces[0].dtype)
    for mask, piece in enumerate(pieces):
        whole = lax.dynamic_update_slice_in_dim(whole, piece, (index ^ mask) * rows, axis=0)
    return whole


def halves(values):
    middle = values.shape[0] // 2
    return values[:middle], values[middle:]


def after(values, *others):
    return lax.optimization_barrier((values,) + others)


def columns_of(values, index, width):
    return lax.dynamic_slice_in_dim(values, index * width, width, axis=1)


def rows_of(values, index, height):
    return lax.dynamic_slice_in_dim(values, index * height, height, axis=0)


def sum_parts(lefts, rights):
    return sum(t_dot(left, right) for left, right in zip(lefts, rights)).astype(low)


def gather_rows(values):
    return lax.all_gather(values, LAYER, axis=0, tiled=True)


def scatter_rows(values):
    return lax.psum_scatter(values, LAYER, scatter_dimension=0, tiled=True)


def local(
    tokens,
    segment_ids,
    cotangent,
    norm_attn,
    w_query,
    w_key,
    w_value,
    q_gain,
    k_gain,
    w_out,
    norm_ffn,
    w_gate,
    w_up,
    w_down,
):
    n = lax.axis_size(CTX)
    m = lax.axis_size(LAYER)
    me = lax.axis_index(CTX)
    chip = lax.axis_index("chip")
    core = lax.axis_index("core")
    chips = n // 2
    width = tokens.shape[-1]
    own = 2 * BLOCK
    total = n * own
    heads = H // n
    repeat = n // KVH
    qw = heads * HD
    hidden = w_gate.shape[1] // n
    piece = hidden // m
    strip = width // (n * m)
    assert tokens.shape[0] == 1 and heads * n == H and repeat * KVH == n

    own_tokens = tokens.reshape(own, width)
    own_cotangent = cotangent.reshape(own, width)
    out_cols = width // n
    attn_w = jnp.concatenate(
        [
            columns_of(w_out, me, out_cols),
            columns_of(w_query, me, qw),
            columns_of(w_key, me // repeat, HD),
            columns_of(w_value, me // repeat, HD),
        ],
        axis=1,
    )
    own_tokens, attn_w = after(own_tokens, attn_w)
    layer = lax.axis_index(LAYER)
    attn_w = gather_rows(attn_w)
    out_w, qkv_w = attn_w[:, :out_cols], attn_w[:, out_cols:]

    small = jnp.concatenate([norm_attn, norm_ffn, q_gain, k_gain]).reshape(1, -1)
    small = in_order(spread(small, LAYER), layer).astype(high)
    part, gain_part = norm_attn.shape[0], q_gain.shape[0]
    gain_attn = small[:, :part].reshape(-1)
    gain_ffn = small[:, part : 2 * part].reshape(-1)
    query_gain = small[:, 2 * part : 2 * part + gain_part].reshape(1, HD)
    key_gain = small[:, 2 * part + gain_part :].reshape(1, HD)

    def hidden_columns(weights):
        starts = [(i * n + me) * piece for i in range(m)]
        return [lax.dynamic_slice_in_dim(weights, start, piece, axis=1) for start in starts]

    gate_up_w = jnp.concatenate(hidden_columns(w_gate) + hidden_columns(w_up), axis=1)
    down_w = rows_of(w_down, me, piece)
    token_half = exchange(jnp.broadcast_to(own_tokens, (chips, own, width)), "chip").reshape(-1, width)
    token_half, gate_up_w, down_w = after(token_half, gate_up_w, down_w)
    token_parts = (token_half, swap(token_half, "core"))
    gate_up_w = gather_rows(gate_up_w)
    down_w = gather_rows(down_w)

    out_half = spread(out_w, "chip")
    owners = [me ^ (2 * mask) for mask in range(chips)]
    owners = owners + [owner ^ 1 for owner in owners]

    def by_layer(grads):
        return grads.reshape(n, m, strip, -1).transpose(1, 0, 2, 3).reshape(width, -1)

    def own_hidden(grads):
        whole = jnp.zeros_like(grads)
        for step in range(m):
            targets = [(i, ((step + i) % m * n + i) // m) for i in range(n)]
            rows = lax.ppermute(rows_of(grads, (step + me) % m, piece), CTX, targets)
            place = (me // (n // m) - step) % m * piece
            whole = lax.dynamic_update_slice_in_dim(whole, rows, place, axis=0)
        return whole

    natural = jnp.arange(2 * n, dtype=jnp.int32)
    side = (natural >= n).astype(jnp.int32)
    owner = jnp.where(side == 0, natural, 2 * n - 1 - natural)
    sources = 2 * (((owner & 1) ^ core) * chips + (owner >> 1)) + side
    places = 2 * owner + side

    segments = segment_ids.reshape(total)
    starts = jnp.sum((segments[None, :] < segments[:, None]).astype(jnp.int32), axis=1)
    place = jnp.arange(total, dtype=jnp.int32) - starts
    frequency = theta_base ** (-(jnp.arange(HD // 2, dtype=high) * 2.0) / HD)
    angles = place.astype(high)[:, None] * frequency
    cosine = jnp.cos(angles)
    sine = jnp.sin(angles)
    cosine = jnp.concatenate([cosine, cosine], axis=1)
    sine = jnp.concatenate([-sine, sine], axis=1)
    segment_column = segments.reshape(total, 1)
    segment_row = segments.reshape(1, total)

    normed_parts = []
    for tokens_part in token_parts:
        features = tokens_part.astype(high)
        normed_parts.append((features * rms_factor(features) * gain_attn).astype(low))
    qkv_raw = jnp.concatenate([dot(normed, qkv_w) for normed in normed_parts], axis=0)
    tables = (cosine, sine, query_gain, key_gain, segment_column, segment_row)
    mixed_rel, mixed_abs, query, key, value, logs = attend(
        total, heads, sources, places, qkv_raw, *tables
    )
    mixed = exchange(mixed_abs.reshape(n, own, qw), CTX)
    mixed, own_cotangent, *out_half = after(mixed, own_cotangent, *out_half)
    out_blocks = out_half + [swap(block, "core") for block in out_half]
    upstream_half = in_order(spread(own_cotangent, "chip"), chip)
    mixed = mixed.transpose(1, 0, 2).reshape(own, n * qw)
    own_features = own_tokens.astype(high)
    branch = jnp.zeros((own, width), high)
    for block_owner, block in zip(owners, out_blocks):
        branch = lax.dynamic_update_slice_in_dim(branch, dot(mixed, block), block_owner * out_cols, axis=1)
    middle = own_features + branch
    factor_ffn = rms_factor(middle)
    ffn_own = (middle * factor_ffn * gain_ffn).astype(low)
    ffn_parts = gather(ffn_own)
    upstream_parts = (upstream_half, swap(upstream_half, "core"))

    hidden_parts, gates = [], []
    for ffn_low in ffn_parts:
        gate_up = dot(ffn_low, gate_up_w)
        gate, up = gate_up[:, :hidden], gate_up[:, hidden:]
        sigmoid = jax.nn.sigmoid(gate)
        silu = gate * sigmoid
        hidden_parts.append((silu * up).astype(low))
        gates.append((up * sigmoid * (1.0 + gate * (1.0 - sigmoid)), silu))
    grad_down = own_hidden(sum_parts(hidden_parts, upstream_parts))
    grad_down, *upstream_parts = after(grad_down, *upstream_parts)
    gate_up_grads = []
    for upstream_low, (gate_slope, silu) in zip(upstream_parts, gates):
        grad_hidden = dot_t(upstream_low, down_w)
        grads = [(grad_hidden * gate_slope).astype(low), (grad_hidden * silu).astype(low)]
        gate_up_grads.append(jnp.concatenate(grads, axis=1))
    grad_ffn = [dot_t(grads, gate_up_w).astype(low) for grads in gate_up_grads]
    grad_gate_up = by_layer(sum_parts(ffn_parts, gate_up_grads))
    grad_ffn = scatter(grad_ffn[0], grad_ffn[1])
    grad_down = scatter_rows(grad_down)
    grad_ffn, grad_gate_up, grad_down = after(grad_ffn, grad_gate_up, grad_down)
    grad_gate_up = scatter_rows(grad_gate_up)

    upstream = own_cotangent.astype(high)
    scaled = gain_ffn * grad_ffn
    inner = mean_last(middle * scaled)
    grad_middle = upstream + factor_ffn * scaled - middle * factor_ffn**3 * inner
    grad_gain_ffn = jnp.sum(grad_ffn * middle * factor_ffn, axis=0)
    middle_low = grad_middle.astype(low)

    mixed_grad = 0.0
    for block_owner, block in zip(owners, out_blocks):
        mixed_grad = mixed_grad + dot_t(columns_of(middle_low, block_owner, out_cols), block)
    mixed_grad = mixed_grad.astype(low).reshape(own, n, qw).transpose(1, 0, 2)
    mixed_grad = exchange(mixed_grad, CTX).reshape(total, qw)
    mixed_grad, late_low = after(mixed_grad, middle_low)
    late_half = in_order(spread(late_low, "chip"), chip)
    grad_out = sum_parts(halves(mixed_rel), (late_half, swap(late_half, "core")))
    qkv_grad, grad_gains = attend_back(
        total, heads, sources, places, qkv_raw, *tables, query, key, value, logs, mixed_grad
    )
    qkv_grads = halves(qkv_grad)
    grad_attn = [dot_t(grads, qkv_w).astype(low) for grads in qkv_grads]
    grad_attn = scatter(grad_attn[0], grad_attn[1])
    factor_attn = rms_factor(own_features)
    scaled = gain_attn * grad_attn
    inner = mean_last(own_features * scaled)
    input_grad = grad_middle + factor_attn * scaled - own_features * factor_attn**3 * inner
    grad_gain_attn = jnp.sum(grad_attn * own_features * factor_attn, axis=0)
    input_grad = input_grad.reshape(tokens.shape)

    lanes = math.gcd((heads + 2) * HD, width)
    grad_qkv = by_layer(sum_parts(normed_parts, qkv_grads))
    grad_late = [grad_qkv.reshape(m, -1, lanes), grad_out.reshape(m, -1, lanes)]
    grad_late = jnp.concatenate(grad_late, axis=1)
    grad_attn, grad_gate_up, grad_late, *hidden_late = after(
        grad_attn, grad_gate_up, grad_late, *hidden_parts
    )
    grad_late = scatter_rows(grad_late.reshape(-1, lanes))
    block_parts = [dot(values, down_w).astype(low) for values in hidden_late]
    block_out = middle + scatter(block_parts[0], block_parts[1])
    block_out = block_out.astype(low).reshape(tokens.shape)

    grad_down = grad_down.astype(high)
    grad_gate_up = exchange(grad_gate_up.reshape(n, strip, -1), CTX).astype(high)
    grad_gate_up = grad_gate_up.reshape(n, strip, 2, m, piece).transpose(2, 1, 3, 0, 4)
    grad_gate_up = grad_gate_up.reshape(2, strip, -1)

    late_rows = n * strip * (heads + 2) * HD // lanes
    grad_qkv, grad_out = grad_late[:late_rows], grad_late[late_rows:]
    grad_out = grad_out.reshape(-1, width).astype(high)
    grad_qkv = exchange(grad_qkv.reshape(n, strip, -1), CTX).astype(high)
    grad_query = grad_qkv[:, :, :qw].transpose(1, 0, 2).reshape(strip, -1)

    def grad_of_kv(grads):
        grads = jnp.sum(grads.reshape(KVH, repeat, strip, HD), axis=1)
        return grads.transpose(1, 0, 2).reshape(strip, -1)

    grad_key = grad_of_kv(grad_qkv[:, :, qw : qw + HD])
    grad_value = grad_of_kv(grad_qkv[:, :, qw + HD :])

    devices = n * m
    partial = jnp.concatenate(
        [
            grad_gain_attn.reshape(devices, -1),
            grad_gain_ffn.reshape(devices, -1),
            grad_gains[0].reshape(devices, -1),
            grad_gains[1].reshape(devices, -1),
        ],
        axis=1,
    )
    gains = jnp.sum(exchange(partial, CTX + LAYER), axis=0)
    end = 2 * strip + HD // devices
    return (
        block_out,
        input_grad,
        gains[:strip],
        grad_query,
        grad_key,
        grad_value,
        gains[2 * strip : end],
        gains[end:],
        grad_out,
        gains[strip : 2 * strip],
        grad_gate_up[0],
        grad_gate_up[1],
        grad_down,
    )


def solution(mesh):
    n, m = mesh.shape["ctx"], mesh.shape["fsdp"]
    mesh = Mesh(mesh.devices.reshape(n // 2, 2, m // 2, 2), CTX + LAYER)
    rows = P(LAYER, None)
    line = P(LAYER)
    blocks = P(LAYER, None, CTX, None, None)
    both = P(CTX + LAYER, None)
    both_line = P(CTX + LAYER)
    in_specs = (blocks, rows, blocks, line, rows, rows, rows, line, line, rows, line, rows, rows, rows)
    out_specs = (
        blocks,
        blocks,
        both_line,
        both,
        both,
        both,
        both_line,
        both_line,
        both,
        both_line,
        both,
        both,
        both,
    )
    return jax.shard_map(local, mesh=mesh, in_specs=in_specs, out_specs=out_specs, check_vma=False)
```

```python
import functools

import jax
import jax.numpy as jnp
from jax import lax
from jax.experimental import pallas as pl
from jax.experimental.pallas import tpu as pltpu
from jax.sharding import Mesh
from jax.sharding import PartitionSpec as P

H = 16
KVH = 8
HD = 128
BLOCK = 64
TILE = 256

epsilon = 1e-06
theta_base = 1000000.0
score_scale = HD ** (-0.5)
low = jnp.bfloat16
high = jnp.float32
vmem_bytes = 48 << 20


def dot(left, right):
    return jnp.dot(left, right, preferred_element_type=high)


def dot_t(left, right):
    return lax.dot_general(left, right, (((1,), (1,)), ((), ())), preferred_element_type=high)


def t_dot(left, right):
    return lax.dot_general(left, right, (((0,), (0,)), ((), ())), preferred_element_type=high)


def mean_last(values):
    return jnp.mean(values, axis=-1, keepdims=True)


def rms_factor(values):
    return lax.rsqrt(mean_last(values * values) + epsilon)


def head_cols(head):
    return slice(head * HD, (head + 1) * HD)


def visible_tile(segc_ref, segr_ref, first, keys):
    rows = lax.broadcasted_iota(jnp.int32, (TILE, keys), 0) + first
    cols = lax.broadcasted_iota(jnp.int32, (TILE, keys), 1)
    same = segc_ref[first : first + TILE, :] == segr_ref[:, :keys]
    return same & (cols <= rows)


def attend_kernel(
    sources_ref,
    places_ref,
    raw_ref,
    cos_ref,
    sin_ref,
    qg_ref,
    kg_ref,
    segc_ref,
    segr_ref,
    rel_ref,
    abs_ref,
    q_ref,
    k_ref,
    v_ref,
    log_ref,
):
    total = q_ref.shape[0]
    heads = q_ref.shape[1] // HD
    blocks = total // BLOCK

    def prepare(index, carry):
        source = pl.multiple_of(sources_ref[index] * BLOCK, BLOCK)
        target = pl.multiple_of(index * BLOCK, BLOCK)
        raw = raw_ref[pl.ds(source, BLOCK), :]
        cosine = cos_ref[pl.ds(target, BLOCK), :]
        sine = sin_ref[pl.ds(target, BLOCK), :]
        for head in range(heads + 1):
            values = raw[:, head_cols(head)]
            gain = qg_ref[...] if head < heads else kg_ref[...]
            normed = values * rms_factor(values) * gain
            turned = (normed * cosine + pltpu.roll(normed, HD // 2, 1) * sine).astype(low)
            if head < heads:
                q_ref[pl.ds(target, BLOCK), head_cols(head)] = turned
            else:
                k_ref[pl.ds(target, BLOCK), :] = turned
        v_ref[pl.ds(target, BLOCK), :] = raw[:, head_cols(heads + 1)].astype(low)
        return carry

    lax.fori_loop(0, blocks, prepare, 0)
    for tile in range(total // TILE):
        first = tile * TILE
        keys = first + TILE
        visible = visible_tile(segc_ref, segr_ref, first, keys)
        for head in range(heads):
            scores = dot_t(q_ref[first : first + TILE, head_cols(head)], k_ref[:keys, :])
            scores = jnp.where(visible, scores * score_scale, -jnp.inf)
            peak = jnp.max(scores, axis=-1, keepdims=True)
            powers = jnp.exp(scores - peak)
            sums = jnp.sum(powers, axis=-1, keepdims=True)
            probs = (powers / sums).astype(low)
            mixed = dot(probs, v_ref[:keys, :]).astype(low)
            log_ref[first : first + TILE, head : head + 1] = peak + jnp.log(sums)
            for part in range(TILE // BLOCK):
                index = first // BLOCK + part
                piece = mixed[part * BLOCK : (part + 1) * BLOCK, :]
                target = pl.multiple_of(sources_ref[index] * BLOCK, BLOCK)
                rel_ref[pl.ds(target, BLOCK), head_cols(head)] = piece
                target = pl.multiple_of(places_ref[index] * BLOCK, BLOCK)
                abs_ref[pl.ds(target, BLOCK), head_cols(head)] = piece


def attend_back_kernel(
    sources_ref,
    places_ref,
    raw_ref,
    cos_ref,
    sin_ref,
    qg_ref,
    kg_ref,
    segc_ref,
    segr_ref,
    q_ref,
    k_ref,
    v_ref,
    log_ref,
    up_ref,
    out_ref,
    gains_ref,
    dq_ref,
    dk_ref,
    dv_ref,
):
    total = q_ref.shape[0]
    heads = q_ref.shape[1] // HD
    blocks = total // BLOCK
    dk_ref[...] = jnp.zeros_like(dk_ref)
    dv_ref[...] = jnp.zeros_like(dv_ref)
    for tile in range(total // TILE):
        first = tile * TILE
        keys = first + TILE
        visible = visible_tile(segc_ref, segr_ref, first, keys)
        for head in range(heads):
            pieces = []
            for part in range(TILE // BLOCK):
                source = pl.multiple_of(places_ref[first // BLOCK + part] * BLOCK, BLOCK)
                pieces.append(up_ref[pl.ds(source, BLOCK), head_cols(head)])
            upstream = jnp.concatenate(pieces, axis=0)
            query = q_ref[first : first + TILE, head_cols(head)]
            key = k_ref[:keys, :]
            scores = dot_t(query, key) * score_scale
            shifted = scores - log_ref[first : first + TILE, head : head + 1]
            probs = jnp.exp(jnp.where(visible, shifted, -jnp.inf))
            dprobs = dot_t(upstream, v_ref[:keys, :])
            inner = jnp.sum(probs * dprobs, axis=-1, keepdims=True)
            dscores = (probs * (dprobs - inner)).astype(low)
            dq_ref[first : first + TILE, head_cols(head)] = dot(dscores, key) * score_scale
            dk_ref[:keys, :] += t_dot(dscores, query) * score_scale
            dv_ref[:keys, :] += t_dot(probs.astype(low), upstream)

    def finish(index, carry):
        target = pl.multiple_of(sources_ref[index] * BLOCK, BLOCK)
        source = pl.multiple_of(index * BLOCK, BLOCK)
        raw = raw_ref[pl.ds(target, BLOCK), :]
        cosine = cos_ref[pl.ds(source, BLOCK), :]
        sine = sin_ref[pl.ds(source, BLOCK), :]
        gains = list(carry)
        for head in range(heads + 1):
            values = raw[:, head_cols(head)]
            if head < heads:
                upstream, gain, slot = dq_ref[pl.ds(source, BLOCK), head_cols(head)], qg_ref[...], 0
            else:
                upstream, gain, slot = dk_ref[pl.ds(source, BLOCK), :], kg_ref[...], 1
            upstream = upstream * cosine - pltpu.roll(upstream, HD // 2, 1) * sine
            factor = rms_factor(values)
            gains[slot] = gains[slot] + jnp.sum(upstream * values * factor, axis=0, keepdims=True)
            scaled = gain * upstream
            inner = mean_last(values * scaled)
            back = factor * scaled - values * (factor * factor * factor) * inner
            out_ref[pl.ds(target, BLOCK), head_cols(head)] = back.astype(low)
        out_ref[pl.ds(target, BLOCK), head_cols(heads + 1)] = dv_ref[pl.ds(source, BLOCK), :].astype(low)
        return tuple(gains)

    zero = jnp.zeros((1, HD), high)
    query_gain, key_gain = lax.fori_loop(0, blocks, finish, (zero, zero))
    gains_ref[0:1, :] = query_gain
    gains_ref[1:2, :] = key_gain


def in_memory(kinds):
    return [pl.BlockSpec(memory_space=kind) for kind in kinds]


def attend(total, heads, *operands):
    shapes = (
        jax.ShapeDtypeStruct((total, heads * HD), low),
        jax.ShapeDtypeStruct((total, heads * HD), low),
        jax.ShapeDtypeStruct((total, heads * HD), low),
        jax.ShapeDtypeStruct((total, HD), low),
        jax.ShapeDtypeStruct((total, HD), low),
        jax.ShapeDtypeStruct((total, HD), high),
    )
    return pl.pallas_call(
        attend_kernel,
        out_shape=shapes,
        in_specs=in_memory([pltpu.SMEM] * 2 + [pltpu.VMEM] * (len(operands) - 2)),
        out_specs=in_memory([pltpu.VMEM] * len(shapes)),
        compiler_params=pltpu.CompilerParams(vmem_limit_bytes=vmem_bytes),
        name="attend",
    )(*operands)


def attend_back(total, heads, *operands):
    shapes = (
        jax.ShapeDtypeStruct((total, (heads + 2) * HD), low),
        jax.ShapeDtypeStruct((2, HD), high),
    )
    return pl.pallas_call(
        attend_back_kernel,
        out_shape=shapes,
        in_specs=in_memory([pltpu.SMEM] * 2 + [pltpu.VMEM] * (len(operands) - 2)),
        out_specs=in_memory([pltpu.VMEM] * len(shapes)),
        scratch_shapes=[
            pltpu.VMEM((total, heads * HD), high),
            pltpu.VMEM((total, HD), high),
            pltpu.VMEM((total, HD), high),
        ],
        compiler_params=pltpu.CompilerParams(vmem_limit_bytes=vmem_bytes),
        name="attend_back",
    )(*operands)


def project_back_kernel(chips, *refs):
    owners_ref, sums_ref, middle_ref, up_ref, gain_ref = refs[:5]
    (grad_ref, low_ref, gain_grad_ref, out_ref, weights_ref, sems) = refs[-6:]
    blocks = refs[5:-6]
    copies = [
        pltpu.make_async_copy(block, weights_ref.at[i], sems.at[i]) for i, block in enumerate(blocks)
    ]
    for copy in copies:
        copy.start()
    upstream = sums_ref[0].astype(high)
    for chip in range(1, chips):
        upstream = upstream + sums_ref[chip].astype(high)
    values = middle_ref[...]
    factor = rms_factor(values)
    gain_grad_ref[...] = jnp.sum(upstream * values * factor, axis=0, keepdims=True)
    scaled = gain_ref[...] * upstream
    inner = mean_last(values * scaled)
    back = factor * scaled - values * (factor * factor * factor) * inner
    grad = up_ref[...].astype(high) + back
    grad_ref[...] = grad
    low_ref[...] = grad.astype(low)
    cols = weights_ref.shape[2]
    total = 0.0
    for i, copy in enumerate(copies):
        start = pl.multiple_of(owners_ref[i] * cols, cols)
        copy.wait()
        total = total + dot_t(low_ref[:, pl.ds(start, cols)], weights_ref[i])
    total = total.astype(low)
    width = out_ref.shape[2]
    for i in range(out_ref.shape[0]):
        out_ref[i] = total[:, i * width : (i + 1) * width]


def project_back(owners, sums, middle, upstream, gain, blocks):
    rows, width = middle.shape
    count = len(blocks)
    depth, cols = blocks[0].shape
    shapes = (
        jax.ShapeDtypeStruct((rows, width), high),
        jax.ShapeDtypeStruct((rows, width), low),
        jax.ShapeDtypeStruct((1, width), high),
        jax.ShapeDtypeStruct((count, rows, depth // count), low),
    )
    return pl.pallas_call(
        functools.partial(project_back_kernel, sums.shape[0]),
        out_shape=shapes,
        in_specs=in_memory([pltpu.SMEM] + [pltpu.VMEM] * 4 + [pl.ANY] * count),
        out_specs=in_memory([pltpu.VMEM] * len(shapes)),
        scratch_shapes=[pltpu.VMEM((count, depth, cols), low), pltpu.SemaphoreType.DMA((count,))],
        compiler_params=pltpu.CompilerParams(vmem_limit_bytes=vmem_bytes),
        name="project_back",
    )(owners, sums, middle, upstream, gain, *blocks)


def arrange_kernel(piece, in_ref, gate_ref, up_ref):
    count, _, width = in_ref.shape
    hidden = width // 2
    for half, out_ref in enumerate((gate_ref, up_ref)):
        for layer in range(hidden // piece):
            start = half * hidden + layer * piece
            parts = [in_ref[i, :, start : start + piece].astype(high) for i in range(count)]
            target = layer * count * piece
            out_ref[:, target : target + count * piece] = jnp.concatenate(parts, axis=1)


def arrange(grads, piece):
    count, rows, width = grads.shape
    shape = jax.ShapeDtypeStruct((rows, count * width // 2), high)
    return pl.pallas_call(
        functools.partial(arrange_kernel, piece),
        out_shape=(shape, shape),
        in_specs=in_memory([pltpu.VMEM]),
        out_specs=in_memory([pltpu.VMEM] * 2),
        compiler_params=pltpu.CompilerParams(vmem_limit_bytes=vmem_bytes),
        name="arrange",
    )(grads)


CTX = ("chip", "core")
LAYER = ("hi", "lo")


def swap(values, axis, mask=1):
    size = lax.axis_size(axis)
    return lax.ppermute(values, axis, [(i, i ^ mask) for i in range(size)])


def exchange(values, axis):
    return lax.all_to_all(values, axis, 0, 0, tiled=True)


def gather(values):
    copies = jnp.broadcast_to(values[None], (lax.axis_size("chip"),) + values.shape)
    half = exchange(copies, "chip").reshape(-1, values.shape[-1])
    return half, swap(half, "core")


def sum_cores(keep, give):
    return (keep.astype(high) + swap(give, "core").astype(high)).astype(low)


def sum_chips(half):
    return jnp.sum(send_chips(half).astype(high), axis=0)


def send_chips(half):
    size = lax.axis_size("chip")
    return exchange(half.reshape(size, half.shape[0] // size, -1), "chip")


def spread(values, axis):
    return [values] + [swap(values, axis, mask) for mask in range(1, lax.axis_size(axis))]


def in_order(pieces, index):
    rows = pieces[0].shape[0]
    whole = jnp.zeros((len(pieces) * rows,) + pieces[0].shape[1:], pieces[0].dtype)
    for mask, piece in enumerate(pieces):
        whole = lax.dynamic_update_slice_in_dim(whole, piece, (index ^ mask) * rows, axis=0)
    return whole


def halves(values):
    middle = values.shape[0] // 2
    return values[:middle], values[middle:]


def after(values, *others):
    return lax.optimization_barrier((values,) + others)


def columns_of(values, index, width):
    return lax.dynamic_slice_in_dim(values, index * width, width, axis=1)


def rows_of(values, index, height):
    return lax.dynamic_slice_in_dim(values, index * height, height, axis=0)


def sum_parts(lefts, rights):
    return sum(t_dot(left, right) for left, right in zip(lefts, rights)).astype(low)


def gather_rows(values):
    return lax.all_gather(values, LAYER, axis=0, tiled=True)


def scatter_rows(values):
    return lax.psum_scatter(values, LAYER, scatter_dimension=0, tiled=True)


def local(
    tokens,
    segment_ids,
    cotangent,
    norm_attn,
    w_query,
    w_key,
    w_value,
    q_gain,
    k_gain,
    w_out,
    norm_ffn,
    w_gate,
    w_up,
    w_down,
):
    n = lax.axis_size(CTX)
    m = lax.axis_size(LAYER)
    me = lax.axis_index(CTX)
    chip = lax.axis_index("chip")
    core = lax.axis_index("core")
    chips = n // 2
    width = tokens.shape[-1]
    own = 2 * BLOCK
    total = n * own
    heads = H // n
    repeat = n // KVH
    qw = heads * HD
    hidden = w_gate.shape[1] // n
    piece = hidden // m
    strip = width // (n * m)
    assert tokens.shape[0] == 1 and heads * n == H and repeat * KVH == n

    own_tokens = tokens.reshape(own, width)
    own_cotangent = cotangent.reshape(own, width)
    out_cols = width // n
    attn_w = jnp.concatenate(
        [
            columns_of(w_out, me, out_cols),
            columns_of(w_query, me, qw),
            columns_of(w_key, me // repeat, HD),
            columns_of(w_value, me // repeat, HD),
        ],
        axis=1,
    )
    own_tokens, attn_w = after(own_tokens, attn_w)
    layer = lax.axis_index(LAYER)
    attn_w = gather_rows(attn_w)

    small = jnp.concatenate([norm_attn, norm_ffn, q_gain, k_gain]).reshape(1, -1)
    small = in_order(spread(small, LAYER), layer).astype(high)
    part, gain_part = norm_attn.shape[0], q_gain.shape[0]
    gain_attn = small[:, :part].reshape(-1)
    gain_ffn = small[:, part : 2 * part].reshape(-1)
    query_gain = small[:, 2 * part : 2 * part + gain_part].reshape(1, HD)
    key_gain = small[:, 2 * part + gain_part :].reshape(1, HD)

    def hidden_columns(weights):
        starts = [(i * n + me) * piece for i in range(m)]
        return [lax.dynamic_slice_in_dim(weights, start, piece, axis=1) for start in starts]

    gate_up_w = jnp.concatenate(hidden_columns(w_gate) + hidden_columns(w_up), axis=1)
    down_w = rows_of(w_down, me, piece)
    token_half = exchange(jnp.broadcast_to(own_tokens, (chips, own, width)), "chip").reshape(-1, width)
    token_half, own_cotangent, gate_up_w, down_w = after(
        token_half, own_cotangent, gate_up_w, down_w
    )
    upstream_half = in_order(spread(own_cotangent, "chip"), chip)
    upstream_half, attn_w = after(upstream_half, attn_w)
    out_w, qkv_w = attn_w[:, :out_cols], attn_w[:, out_cols:]
    token_parts = (token_half, swap(token_half, "core"))
    gate_up_w = gather_rows(gate_up_w)
    down_w = gather_rows(down_w)

    out_half = spread(out_w, "chip")
    owners = [me ^ (2 * mask) for mask in range(chips)]
    owners = owners + [owner ^ 1 for owner in owners]

    def by_layer(grads):
        return grads.reshape(n, m, strip, -1).transpose(1, 0, 2, 3).reshape(width, -1)

    def own_hidden(grads):
        whole = jnp.zeros_like(grads)
        for step in range(m):
            targets = [(i, ((step + i) % m * n + i) // m) for i in range(n)]
            rows = lax.ppermute(rows_of(grads, (step + me) % m, piece), CTX, targets)
            place = (me // (n // m) - step) % m * piece
            whole = lax.dynamic_update_slice_in_dim(whole, rows, place, axis=0)
        return whole

    natural = jnp.arange(2 * n, dtype=jnp.int32)
    side = (natural >= n).astype(jnp.int32)
    owner = jnp.where(side == 0, natural, 2 * n - 1 - natural)
    sources = 2 * (((owner & 1) ^ core) * chips + (owner >> 1)) + side
    places = 2 * owner + side

    segments = segment_ids.reshape(total)
    starts = jnp.sum((segments[None, :] < segments[:, None]).astype(jnp.int32), axis=1)
    place = jnp.arange(total, dtype=jnp.int32) - starts
    frequency = theta_base ** (-(jnp.arange(HD // 2, dtype=high) * 2.0) / HD)
    angles = place.astype(high)[:, None] * frequency
    cosine = jnp.cos(angles)
    sine = jnp.sin(angles)
    cosine = jnp.concatenate([cosine, cosine], axis=1)
    sine = jnp.concatenate([-sine, sine], axis=1)
    segment_column = segments.reshape(total, 1)
    segment_row = segments.reshape(1, total)

    normed_parts = []
    for tokens_part in token_parts:
        features = tokens_part.astype(high)
        normed_parts.append((features * rms_factor(features) * gain_attn).astype(low))
    qkv_raw = jnp.concatenate([dot(normed, qkv_w) for normed in normed_parts], axis=0)
    tables = (cosine, sine, query_gain, key_gain, segment_column, segment_row)
    mixed_rel, mixed_abs, query, key, value, logs = attend(
        total, heads, sources, places, qkv_raw, *tables
    )
    mixed = exchange(mixed_abs.reshape(n, own, qw), CTX)
    out_blocks = out_half + [swap(block, "core") for block in out_half]
    mixed = mixed.transpose(1, 0, 2).reshape(own, n * qw)
    own_features = own_tokens.astype(high)
    branch = jnp.zeros((own, width), high)
    for block_owner, block in zip(owners, out_blocks):
        branch = lax.dynamic_update_slice_in_dim(branch, dot(mixed, block), block_owner * out_cols, axis=1)
    middle = own_features + branch
    factor_ffn = rms_factor(middle)
    ffn_own = (middle * factor_ffn * gain_ffn).astype(low)
    ffn_parts = gather(ffn_own)
    upstream_parts = (upstream_half, swap(upstream_half, "core"))

    hidden_parts, gates = [], []
    for ffn_low in ffn_parts:
        gate_up = dot(ffn_low, gate_up_w)
        gate, up = gate_up[:, :hidden], gate_up[:, hidden:]
        sigmoid = jax.nn.sigmoid(gate)
        silu = gate * sigmoid
        hidden_parts.append((silu * up).astype(low))
        gates.append((up * sigmoid * (1.0 + gate * (1.0 - sigmoid)), silu))
    grad_down = own_hidden(sum_parts(hidden_parts, upstream_parts))
    grad_down, down_w = after(grad_down, down_w)
    gate_up_grads = []
    for upstream_low, (gate_slope, silu) in zip(upstream_parts, gates):
        grad_hidden = dot_t(upstream_low, down_w)
        grads = [(grad_hidden * gate_slope).astype(low), (grad_hidden * silu).astype(low)]
        gate_up_grads.append(jnp.concatenate(grads, axis=1))
    grad_ffn = [dot_t(grads, gate_up_w).astype(low) for grads in gate_up_grads]
    grad_gate_up = by_layer(sum_parts(ffn_parts, gate_up_grads))
    grad_ffn = send_chips(sum_cores(grad_ffn[0], grad_ffn[1]))
    grad_down = scatter_rows(grad_down)
    grad_ffn, grad_gate_up, grad_down = after(grad_ffn, grad_gate_up, grad_down)
    grad_gate_up = scatter_rows(grad_gate_up)

    grad_middle, middle_low, grad_gain_ffn, mixed_grad = project_back(
        jnp.stack(owners), grad_ffn, middle, own_cotangent, gain_ffn.reshape(1, -1), out_blocks
    )
    mixed_grad = exchange(mixed_grad, CTX).reshape(total, qw)
    late_half = in_order(spread(middle_low, "chip"), chip)
    qkv_grad, grad_gains = attend_back(
        total, heads, sources, places, qkv_raw, *tables, query, key, value, logs, mixed_grad
    )
    qkv_grad, late_half = after(qkv_grad, late_half)
    grad_out = sum_parts(halves(mixed_rel), (late_half, swap(late_half, "core")))
    qkv_grads = halves(qkv_grad)
    grad_attn = [dot_t(grads, qkv_w).astype(low) for grads in qkv_grads]
    grad_attn = sum_chips(sum_cores(grad_attn[0], grad_attn[1]))
    grad_qkv = sum_parts(normed_parts, qkv_grads).reshape(n, m * strip, -1)
    grad_qkv = exchange(grad_qkv, CTX).reshape(n, m, strip, -1)

    def all_heads(grads):
        return grads.transpose(1, 2, 0, 3).reshape(m, strip, -1)

    def grad_of_kv(grads):
        grads = jnp.sum(grads.reshape(KVH, repeat, m, strip, HD).astype(high), axis=1)
        return all_heads(grads.astype(low))

    grad_late = [
        all_heads(grad_qkv[..., :qw]),
        grad_of_kv(grad_qkv[..., qw : qw + HD]),
        grad_of_kv(grad_qkv[..., qw + HD :]),
        grad_out.reshape(m, strip, width),
    ]
    grad_late = jnp.concatenate(grad_late, axis=2).reshape(m * strip, -1)
    grad_late, *hidden_parts = after(grad_late, *hidden_parts)
    block_parts = [dot(values, down_w).astype(low) for values in hidden_parts]
    block_half = sum_cores(block_parts[0], block_parts[1])
    block_sum = rows_of(block_half, chip, own).astype(high)
    for mask in range(1, chips):
        block_sum = block_sum + swap(rows_of(block_half, chip ^ mask, own), "chip", mask).astype(high)
    block_out = (middle + block_sum).astype(low).reshape(tokens.shape)
    grad_late = scatter_rows(grad_late)

    grad_attn, grad_gate_up = after(grad_attn, grad_gate_up)
    grad_gate_up = exchange(grad_gate_up.reshape(n, strip, -1), CTX)
    factor_attn = rms_factor(own_features)
    scaled = gain_attn * grad_attn
    inner = mean_last(own_features * scaled)
    input_grad = grad_middle + factor_attn * scaled - own_features * factor_attn**3 * inner
    grad_gain_attn = jnp.sum(grad_attn * own_features * factor_attn, axis=0)
    input_grad = input_grad.reshape(tokens.shape)

    devices = n * m
    partial = jnp.concatenate(
        [
            grad_gain_attn.reshape(devices, -1),
            grad_gain_ffn.reshape(devices, -1),
            grad_gains[0].reshape(devices, -1),
            grad_gains[1].reshape(devices, -1),
        ],
        axis=1,
    )
    grad_gate_up, partial = after(grad_gate_up, partial)
    gains = exchange(partial, CTX + LAYER)
    gains = jnp.sum(gains, axis=0)
    grad_down = grad_down.astype(high)
    grad_gate, grad_up = arrange(grad_gate_up, piece)
    grad_late, gains = after(grad_late, gains)
    ends = [0, n * qw, n * qw + KVH * HD, n * qw + 2 * KVH * HD, grad_late.shape[1]]
    grad_query, grad_key, grad_value, grad_out = [
        grad_late[:, start:end].astype(high) for start, end in zip(ends, ends[1:])
    ]

    end = 2 * strip + HD // devices
    return (
        block_out,
        input_grad,
        gains[:strip],
        grad_query,
        grad_key,
        grad_value,
        gains[2 * strip : end],
        gains[end:],
        grad_out,
        gains[strip : 2 * strip],
        grad_gate,
        grad_up,
        grad_down,
    )


def solution(mesh):
    n, m = mesh.shape["ctx"], mesh.shape["fsdp"]
    mesh = Mesh(mesh.devices.reshape(n // 2, 2, m // 2, 2), CTX + LAYER)
    rows = P(LAYER, None)
    line = P(LAYER)
    blocks = P(LAYER, None, CTX, None, None)
    both = P(CTX + LAYER, None)
    both_line = P(CTX + LAYER)
    in_specs = (blocks, rows, blocks, line, rows, rows, rows, line, line, rows, line, rows, rows, rows)
    out_specs = (
        blocks,
        blocks,
        both_line,
        both,
        both,
        both,
        both_line,
        both_line,
        both,
        both_line,
        both,
        both,
        both,
    )
    return jax.shard_map(local, mesh=mesh, in_specs=in_specs, out_specs=out_specs, check_vma=False)
```

```python
import functools

import jax
import jax.numpy as jnp
from jax import lax
from jax.experimental import pallas as pl
from jax.experimental.pallas import tpu as pltpu
from jax.sharding import Mesh
from jax.sharding import PartitionSpec as P

H = 16
KVH = 8
HD = 128
BLOCK = 64
TILE = 256

epsilon = 1e-06
theta_base = 1000000.0
score_scale = HD ** (-0.5)
low = jnp.bfloat16
high = jnp.float32
vmem_bytes = 48 << 20


def dot(left, right):
    return jnp.dot(left, right, preferred_element_type=high)


def dot_t(left, right):
    return lax.dot_general(left, right, (((1,), (1,)), ((), ())), preferred_element_type=high)


def t_dot(left, right):
    return lax.dot_general(left, right, (((0,), (0,)), ((), ())), preferred_element_type=high)


def mean_last(values):
    return jnp.mean(values, axis=-1, keepdims=True)


def rms_factor(values):
    return lax.rsqrt(mean_last(values * values) + epsilon)


def head_cols(head):
    return slice(head * HD, (head + 1) * HD)


def visible_tile(segc_ref, segr_ref, first, keys):
    rows = lax.broadcasted_iota(jnp.int32, (TILE, keys), 0) + first
    cols = lax.broadcasted_iota(jnp.int32, (TILE, keys), 1)
    same = segc_ref[first : first + TILE, :] == segr_ref[:, :keys]
    return same & (cols <= rows)


def attend_kernel(
    sources_ref,
    places_ref,
    raw_ref,
    cos_ref,
    sin_ref,
    qg_ref,
    kg_ref,
    segc_ref,
    segr_ref,
    rel_ref,
    abs_ref,
    q_ref,
    k_ref,
    v_ref,
    log_ref,
):
    total = q_ref.shape[0]
    heads = q_ref.shape[1] // HD
    blocks = total // BLOCK

    def prepare(index, carry):
        source = pl.multiple_of(sources_ref[index] * BLOCK, BLOCK)
        target = pl.multiple_of(index * BLOCK, BLOCK)
        raw = raw_ref[pl.ds(source, BLOCK), :]
        cosine = cos_ref[pl.ds(target, BLOCK), :]
        sine = sin_ref[pl.ds(target, BLOCK), :]
        for head in range(heads + 1):
            values = raw[:, head_cols(head)]
            gain = qg_ref[...] if head < heads else kg_ref[...]
            normed = values * rms_factor(values) * gain
            turned = (normed * cosine + pltpu.roll(normed, HD // 2, 1) * sine).astype(low)
            if head < heads:
                q_ref[pl.ds(target, BLOCK), head_cols(head)] = turned
            else:
                k_ref[pl.ds(target, BLOCK), :] = turned
        v_ref[pl.ds(target, BLOCK), :] = raw[:, head_cols(heads + 1)].astype(low)
        return carry

    lax.fori_loop(0, blocks, prepare, 0)
    for tile in range(total // TILE):
        first = tile * TILE
        keys = first + TILE
        visible = visible_tile(segc_ref, segr_ref, first, keys)
        for head in range(heads):
            scores = dot_t(q_ref[first : first + TILE, head_cols(head)], k_ref[:keys, :])
            scores = jnp.where(visible, scores * score_scale, -jnp.inf)
            peak = jnp.max(scores, axis=-1, keepdims=True)
            powers = jnp.exp(scores - peak)
            sums = jnp.sum(powers, axis=-1, keepdims=True)
            probs = (powers / sums).astype(low)
            mixed = dot(probs, v_ref[:keys, :]).astype(low)
            log_ref[first : first + TILE, head : head + 1] = peak + jnp.log(sums)
            for part in range(TILE // BLOCK):
                index = first // BLOCK + part
                piece = mixed[part * BLOCK : (part + 1) * BLOCK, :]
                target = pl.multiple_of(sources_ref[index] * BLOCK, BLOCK)
                rel_ref[pl.ds(target, BLOCK), head_cols(head)] = piece
                target = pl.multiple_of(places_ref[index] * BLOCK, BLOCK)
                abs_ref[pl.ds(target, BLOCK), head_cols(head)] = piece


def attend_back_kernel(
    sources_ref,
    places_ref,
    raw_ref,
    cos_ref,
    sin_ref,
    qg_ref,
    kg_ref,
    segc_ref,
    segr_ref,
    q_ref,
    k_ref,
    v_ref,
    log_ref,
    up_ref,
    out_ref,
    gains_ref,
    dq_ref,
    dk_ref,
    dv_ref,
):
    total = q_ref.shape[0]
    heads = q_ref.shape[1] // HD
    blocks = total // BLOCK
    dk_ref[...] = jnp.zeros_like(dk_ref)
    dv_ref[...] = jnp.zeros_like(dv_ref)
    for tile in range(total // TILE):
        first = tile * TILE
        keys = first + TILE
        visible = visible_tile(segc_ref, segr_ref, first, keys)
        for head in range(heads):
            pieces = []
            for part in range(TILE // BLOCK):
                source = pl.multiple_of(places_ref[first // BLOCK + part] * BLOCK, BLOCK)
                pieces.append(up_ref[pl.ds(source, BLOCK), head_cols(head)])
            upstream = jnp.concatenate(pieces, axis=0)
            query = q_ref[first : first + TILE, head_cols(head)]
            key = k_ref[:keys, :]
            scores = dot_t(query, key) * score_scale
            shifted = scores - log_ref[first : first + TILE, head : head + 1]
            probs = jnp.exp(jnp.where(visible, shifted, -jnp.inf))
            dprobs = dot_t(upstream, v_ref[:keys, :])
            inner = jnp.sum(probs * dprobs, axis=-1, keepdims=True)
            dscores = (probs * (dprobs - inner)).astype(low)
            dq_ref[first : first + TILE, head_cols(head)] = dot(dscores, key) * score_scale
            dk_ref[:keys, :] += t_dot(dscores, query) * score_scale
            dv_ref[:keys, :] += t_dot(probs.astype(low), upstream)

    def finish(index, carry):
        target = pl.multiple_of(sources_ref[index] * BLOCK, BLOCK)
        source = pl.multiple_of(index * BLOCK, BLOCK)
        raw = raw_ref[pl.ds(target, BLOCK), :]
        cosine = cos_ref[pl.ds(source, BLOCK), :]
        sine = sin_ref[pl.ds(source, BLOCK), :]
        gains = list(carry)
        for head in range(heads + 1):
            values = raw[:, head_cols(head)]
            if head < heads:
                upstream, gain, slot = dq_ref[pl.ds(source, BLOCK), head_cols(head)], qg_ref[...], 0
            else:
                upstream, gain, slot = dk_ref[pl.ds(source, BLOCK), :], kg_ref[...], 1
            upstream = upstream * cosine - pltpu.roll(upstream, HD // 2, 1) * sine
            factor = rms_factor(values)
            gains[slot] = gains[slot] + jnp.sum(upstream * values * factor, axis=0, keepdims=True)
            scaled = gain * upstream
            inner = mean_last(values * scaled)
            back = factor * scaled - values * (factor * factor * factor) * inner
            out_ref[pl.ds(target, BLOCK), head_cols(head)] = back.astype(low)
        out_ref[pl.ds(target, BLOCK), head_cols(heads + 1)] = dv_ref[pl.ds(source, BLOCK), :].astype(low)
        return tuple(gains)

    zero = jnp.zeros((1, HD), high)
    query_gain, key_gain = lax.fori_loop(0, blocks, finish, (zero, zero))
    gains_ref[0:1, :] = query_gain
    gains_ref[1:2, :] = key_gain


def in_memory(kinds):
    return [pl.BlockSpec(memory_space=kind) for kind in kinds]


def attend(total, heads, *operands):
    shapes = (
        jax.ShapeDtypeStruct((total, heads * HD), low),
        jax.ShapeDtypeStruct((total, heads * HD), low),
        jax.ShapeDtypeStruct((total, heads * HD), low),
        jax.ShapeDtypeStruct((total, HD), low),
        jax.ShapeDtypeStruct((total, HD), low),
        jax.ShapeDtypeStruct((total, HD), high),
    )
    return pl.pallas_call(
        attend_kernel,
        out_shape=shapes,
        in_specs=in_memory([pltpu.SMEM] * 2 + [pltpu.VMEM] * (len(operands) - 2)),
        out_specs=in_memory([pltpu.VMEM] * len(shapes)),
        compiler_params=pltpu.CompilerParams(vmem_limit_bytes=vmem_bytes),
        name="attend",
    )(*operands)


def attend_back(total, heads, *operands):
    shapes = (
        jax.ShapeDtypeStruct((total, (heads + 2) * HD), low),
        jax.ShapeDtypeStruct((2, HD), high),
    )
    return pl.pallas_call(
        attend_back_kernel,
        out_shape=shapes,
        in_specs=in_memory([pltpu.SMEM] * 2 + [pltpu.VMEM] * (len(operands) - 2)),
        out_specs=in_memory([pltpu.VMEM] * len(shapes)),
        scratch_shapes=[
            pltpu.VMEM((total, heads * HD), high),
            pltpu.VMEM((total, HD), high),
            pltpu.VMEM((total, HD), high),
        ],
        compiler_params=pltpu.CompilerParams(vmem_limit_bytes=vmem_bytes),
        name="attend_back",
    )(*operands)


def project_back_kernel(chips, *refs):
    owners_ref, sums_ref, middle_ref, up_ref, gain_ref = refs[:5]
    (grad_ref, low_ref, gain_grad_ref, out_ref, weights_ref, sems) = refs[-6:]
    blocks = refs[5:-6]
    copies = [
        pltpu.make_async_copy(block, weights_ref.at[i], sems.at[i]) for i, block in enumerate(blocks)
    ]
    for copy in copies:
        copy.start()
    upstream = sums_ref[0].astype(high)
    for chip in range(1, chips):
        upstream = upstream + sums_ref[chip].astype(high)
    values = middle_ref[...]
    factor = rms_factor(values)
    gain_grad_ref[...] = jnp.sum(upstream * values * factor, axis=0, keepdims=True)
    scaled = gain_ref[...] * upstream
    inner = mean_last(values * scaled)
    back = factor * scaled - values * (factor * factor * factor) * inner
    grad = up_ref[...].astype(high) + back
    grad_ref[...] = grad
    low_ref[...] = grad.astype(low)
    cols = weights_ref.shape[2]
    total = 0.0
    for i, copy in enumerate(copies):
        start = pl.multiple_of(owners_ref[i] * cols, cols)
        copy.wait()
        total = total + dot_t(low_ref[:, pl.ds(start, cols)], weights_ref[i])
    total = total.astype(low)
    width = out_ref.shape[2]
    for i in range(out_ref.shape[0]):
        out_ref[i] = total[:, i * width : (i + 1) * width]


def project_back(owners, sums, middle, upstream, gain, blocks):
    rows, width = middle.shape
    count = len(blocks)
    depth, cols = blocks[0].shape
    shapes = (
        jax.ShapeDtypeStruct((rows, width), high),
        jax.ShapeDtypeStruct((rows, width), low),
        jax.ShapeDtypeStruct((1, width), high),
        jax.ShapeDtypeStruct((count, rows, depth // count), low),
    )
    return pl.pallas_call(
        functools.partial(project_back_kernel, sums.shape[0]),
        out_shape=shapes,
        in_specs=in_memory([pltpu.SMEM] + [pltpu.VMEM] * 4 + [pl.ANY] * count),
        out_specs=in_memory([pltpu.VMEM] * len(shapes)),
        scratch_shapes=[pltpu.VMEM((count, depth, cols), low), pltpu.SemaphoreType.DMA((count,))],
        compiler_params=pltpu.CompilerParams(vmem_limit_bytes=vmem_bytes),
        name="project_back",
    )(owners, sums, middle, upstream, gain, *blocks)


def arrange_kernel(piece, in_ref, gate_ref, up_ref):
    count, _, width = in_ref.shape
    hidden = width // 2
    for half, out_ref in enumerate((gate_ref, up_ref)):
        for layer in range(hidden // piece):
            start = half * hidden + layer * piece
            parts = [in_ref[i, :, start : start + piece].astype(high) for i in range(count)]
            target = layer * count * piece
            out_ref[:, target : target + count * piece] = jnp.concatenate(parts, axis=1)


def arrange(grads, piece):
    count, rows, width = grads.shape
    shape = jax.ShapeDtypeStruct((rows, count * width // 2), high)
    return pl.pallas_call(
        functools.partial(arrange_kernel, piece),
        out_shape=(shape, shape),
        in_specs=in_memory([pltpu.VMEM]),
        out_specs=in_memory([pltpu.VMEM] * 2),
        compiler_params=pltpu.CompilerParams(vmem_limit_bytes=vmem_bytes),
        name="arrange",
    )(grads)


CTX = ("chip", "core")
LAYER = ("hi", "lo")


def swap(values, axis, mask=1):
    size = lax.axis_size(axis)
    return lax.ppermute(values, axis, [(i, i ^ mask) for i in range(size)])


def exchange(values, axis):
    return lax.all_to_all(values, axis, 0, 0, tiled=True)


def gather(values):
    copies = jnp.broadcast_to(values[None], (lax.axis_size("chip"),) + values.shape)
    half = exchange(copies, "chip").reshape(-1, values.shape[-1])
    return half, swap(half, "core")


def sum_cores(keep, give):
    return (keep.astype(high) + swap(give, "core").astype(high)).astype(low)


def sum_chips(half):
    size = lax.axis_size("chip")
    chip = lax.axis_index("chip")
    rows = half.shape[0] // size
    total = rows_of(half, chip, rows).astype(high)
    for mask in range(1, size):
        total = total + swap(rows_of(half, chip ^ mask, rows), "chip", mask).astype(high)
    return total


def send_chips(half):
    size = lax.axis_size("chip")
    return exchange(half.reshape(size, half.shape[0] // size, -1), "chip")


def spread(values, axis):
    return [values] + [swap(values, axis, mask) for mask in range(1, lax.axis_size(axis))]


def in_order(pieces, index):
    rows = pieces[0].shape[0]
    whole = jnp.zeros((len(pieces) * rows,) + pieces[0].shape[1:], pieces[0].dtype)
    for mask, piece in enumerate(pieces):
        whole = lax.dynamic_update_slice_in_dim(whole, piece, (index ^ mask) * rows, axis=0)
    return whole


def halves(values):
    middle = values.shape[0] // 2
    return values[:middle], values[middle:]


def after(values, *others):
    return lax.optimization_barrier((values,) + others)


def columns_of(values, index, width):
    return lax.dynamic_slice_in_dim(values, index * width, width, axis=1)


def rows_of(values, index, height):
    return lax.dynamic_slice_in_dim(values, index * height, height, axis=0)


def sum_parts(lefts, rights):
    return sum(t_dot(left, right) for left, right in zip(lefts, rights)).astype(low)


def gather_rows(values):
    return lax.all_gather(values, LAYER, axis=0, tiled=True)


def scatter_rows(values):
    return lax.psum_scatter(values, LAYER, scatter_dimension=0, tiled=True)


def local(
    tokens,
    segment_ids,
    cotangent,
    norm_attn,
    w_query,
    w_key,
    w_value,
    q_gain,
    k_gain,
    w_out,
    norm_ffn,
    w_gate,
    w_up,
    w_down,
):
    n = lax.axis_size(CTX)
    m = lax.axis_size(LAYER)
    me = lax.axis_index(CTX)
    chip = lax.axis_index("chip")
    core = lax.axis_index("core")
    chips = n // 2
    width = tokens.shape[-1]
    own = 2 * BLOCK
    total = n * own
    heads = H // n
    repeat = n // KVH
    qw = heads * HD
    hidden = w_gate.shape[1] // n
    piece = hidden // m
    strip = width // (n * m)
    assert tokens.shape[0] == 1 and heads * n == H and repeat * KVH == n

    own_tokens = tokens.reshape(own, width)
    own_cotangent = cotangent.reshape(own, width)
    out_cols = width // n
    attn_w = jnp.concatenate(
        [
            columns_of(w_out, me, out_cols),
            columns_of(w_query, me, qw),
            columns_of(w_key, me // repeat, HD),
            columns_of(w_value, me // repeat, HD),
        ],
        axis=1,
    )
    own_tokens, attn_w = after(own_tokens, attn_w)
    layer = lax.axis_index(LAYER)
    attn_w = gather_rows(attn_w)

    small = jnp.concatenate([norm_attn, norm_ffn, q_gain, k_gain]).reshape(1, -1)
    small = in_order(spread(small, LAYER), layer).astype(high)
    part, gain_part = norm_attn.shape[0], q_gain.shape[0]
    gain_attn = small[:, :part].reshape(-1)
    gain_ffn = small[:, part : 2 * part].reshape(-1)
    query_gain = small[:, 2 * part : 2 * part + gain_part].reshape(1, HD)
    key_gain = small[:, 2 * part + gain_part :].reshape(1, HD)

    def hidden_columns(weights):
        starts = [(i * n + me) * piece for i in range(m)]
        return [lax.dynamic_slice_in_dim(weights, start, piece, axis=1) for start in starts]

    gate_up_w = jnp.concatenate(hidden_columns(w_gate) + hidden_columns(w_up), axis=1)
    down_w = rows_of(w_down, me, piece)
    token_half = exchange(jnp.broadcast_to(own_tokens, (chips, own, width)), "chip").reshape(-1, width)
    token_half, own_cotangent, gate_up_w, down_w = after(
        token_half, own_cotangent, gate_up_w, down_w
    )
    upstream_half = in_order(spread(own_cotangent, "chip"), chip)
    upstream_half, attn_w = after(upstream_half, attn_w)
    out_w, qkv_w = attn_w[:, :out_cols], attn_w[:, out_cols:]
    token_parts = (token_half, swap(token_half, "core"))
    gate_up_w = gather_rows(gate_up_w)
    down_w = gather_rows(down_w)

    out_half = spread(out_w, "chip")
    owners = [me ^ (2 * mask) for mask in range(chips)]
    owners = owners + [owner ^ 1 for owner in owners]

    def by_layer(grads):
        return grads.reshape(n, m, strip, -1).transpose(1, 0, 2, 3).reshape(width, -1)

    def own_hidden(grads):
        whole = jnp.zeros_like(grads)
        for step in range(m):
            targets = [(i, ((step + i) % m * n + i) // m) for i in range(n)]
            rows = lax.ppermute(rows_of(grads, (step + me) % m, piece), CTX, targets)
            place = (me // (n // m) - step) % m * piece
            whole = lax.dynamic_update_slice_in_dim(whole, rows, place, axis=0)
        return whole

    natural = jnp.arange(2 * n, dtype=jnp.int32)
    side = (natural >= n).astype(jnp.int32)
    owner = jnp.where(side == 0, natural, 2 * n - 1 - natural)
    sources = 2 * (((owner & 1) ^ core) * chips + (owner >> 1)) + side
    places = 2 * owner + side

    segments = segment_ids.reshape(total)
    starts = jnp.sum((segments[None, :] < segments[:, None]).astype(jnp.int32), axis=1)
    place = jnp.arange(total, dtype=jnp.int32) - starts
    frequency = theta_base ** (-(jnp.arange(HD // 2, dtype=high) * 2.0) / HD)
    angles = place.astype(high)[:, None] * frequency
    cosine = jnp.cos(angles)
    sine = jnp.sin(angles)
    cosine = jnp.concatenate([cosine, cosine], axis=1)
    sine = jnp.concatenate([-sine, sine], axis=1)
    segment_column = segments.reshape(total, 1)
    segment_row = segments.reshape(1, total)

    normed_parts = []
    for tokens_part in token_parts:
        features = tokens_part.astype(high)
        normed_parts.append((features * rms_factor(features) * gain_attn).astype(low))
    qkv_raw = jnp.concatenate([dot(normed, qkv_w) for normed in normed_parts], axis=0)
    tables = (cosine, sine, query_gain, key_gain, segment_column, segment_row)
    mixed_rel, mixed_abs, query, key, value, logs = attend(
        total, heads, sources, places, qkv_raw, *tables
    )
    mixed = exchange(mixed_abs.reshape(n, own, qw), CTX)
    out_blocks = out_half + [swap(block, "core") for block in out_half]
    mixed = mixed.transpose(1, 0, 2).reshape(own, n * qw)
    own_features = own_tokens.astype(high)
    branch = jnp.zeros((own, width), high)
    for block_owner, block in zip(owners, out_blocks):
        branch = lax.dynamic_update_slice_in_dim(branch, dot(mixed, block), block_owner * out_cols, axis=1)
    middle = own_features + branch
    factor_ffn = rms_factor(middle)
    ffn_own = (middle * factor_ffn * gain_ffn).astype(low)
    ffn_parts = gather(ffn_own)
    upstream_parts = (upstream_half, swap(upstream_half, "core"))

    hidden_parts, gates = [], []
    for ffn_low in ffn_parts:
        gate_up = dot(ffn_low, gate_up_w)
        gate, up = gate_up[:, :hidden], gate_up[:, hidden:]
        sigmoid = jax.nn.sigmoid(gate)
        silu = gate * sigmoid
        hidden_parts.append((silu * up).astype(low))
        gates.append((up * sigmoid * (1.0 + gate * (1.0 - sigmoid)), silu))
    grad_down = own_hidden(sum_parts(hidden_parts, upstream_parts))
    grad_down, down_w = after(grad_down, down_w)
    gate_up_grads = []
    for upstream_low, (gate_slope, silu) in zip(upstream_parts, gates):
        grad_hidden = dot_t(upstream_low, down_w)
        grads = [(grad_hidden * gate_slope).astype(low), (grad_hidden * silu).astype(low)]
        gate_up_grads.append(jnp.concatenate(grads, axis=1))
    grad_ffn = [dot_t(grads, gate_up_w).astype(low) for grads in gate_up_grads]
    grad_gate_up = by_layer(sum_parts(ffn_parts, gate_up_grads))
    grad_ffn = send_chips(sum_cores(grad_ffn[0], grad_ffn[1]))
    grad_down = scatter_rows(grad_down)
    grad_ffn, grad_gate_up, grad_down = after(grad_ffn, grad_gate_up, grad_down)
    grad_gate_up = scatter_rows(grad_gate_up)

    grad_middle, middle_low, grad_gain_ffn, mixed_grad = project_back(
        jnp.stack(owners), grad_ffn, middle, own_cotangent, gain_ffn.reshape(1, -1), out_blocks
    )
    mixed_grad = exchange(mixed_grad, CTX).reshape(total, qw)
    late_half = in_order(spread(middle_low, "chip"), chip)
    qkv_grad, grad_gains = attend_back(
        total, heads, sources, places, qkv_raw, *tables, query, key, value, logs, mixed_grad
    )
    qkv_grad, late_half = after(qkv_grad, late_half)
    grad_out = sum_parts(halves(mixed_rel), (late_half, swap(late_half, "core")))
    qkv_grads = halves(qkv_grad)
    grad_attn = [dot_t(grads, qkv_w).astype(low) for grads in qkv_grads]
    grad_attn = sum_chips(sum_cores(grad_attn[0], grad_attn[1]))
    grad_qkv = sum_parts(normed_parts, qkv_grads).reshape(n, m * strip, -1)
    grad_qkv = exchange(grad_qkv, CTX).reshape(n, m, strip, -1)

    def all_heads(grads):
        return grads.transpose(1, 2, 0, 3).reshape(m, strip, -1)

    def grad_of_kv(grads):
        grads = jnp.sum(grads.reshape(KVH, repeat, m, strip, HD).astype(high), axis=1)
        return all_heads(grads.astype(low))

    grad_late = [
        all_heads(grad_qkv[..., :qw]),
        grad_of_kv(grad_qkv[..., qw : qw + HD]),
        grad_of_kv(grad_qkv[..., qw + HD :]),
        grad_out.reshape(m, strip, width),
    ]
    grad_late = jnp.concatenate(grad_late, axis=2).reshape(m * strip, -1)
    grad_late, *hidden_parts = after(grad_late, *hidden_parts)
    block_parts = [dot(values, down_w).astype(low) for values in hidden_parts]
    block_half = sum_cores(block_parts[0], block_parts[1])
    block_out = (middle + sum_chips(block_half)).astype(low).reshape(tokens.shape)
    grad_late = scatter_rows(grad_late)

    grad_attn, grad_gate_up = after(grad_attn, grad_gate_up)
    grad_gate_up = exchange(grad_gate_up.reshape(n, strip, -1), CTX)
    factor_attn = rms_factor(own_features)
    scaled = gain_attn * grad_attn
    inner = mean_last(own_features * scaled)
    input_grad = grad_middle + factor_attn * scaled - own_features * factor_attn**3 * inner
    grad_gain_attn = jnp.sum(grad_attn * own_features * factor_attn, axis=0)
    input_grad = input_grad.reshape(tokens.shape)

    devices = n * m
    partial = jnp.concatenate(
        [
            grad_gain_attn.reshape(devices, -1),
            grad_gain_ffn.reshape(devices, -1),
            grad_gains[0].reshape(devices, -1),
            grad_gains[1].reshape(devices, -1),
        ],
        axis=1,
    )
    grad_gate_up, partial = after(grad_gate_up, partial)
    gains = exchange(partial, CTX + LAYER)
    gains = jnp.sum(gains, axis=0)
    grad_down = grad_down.astype(high)
    grad_gate, grad_up = arrange(grad_gate_up, piece)
    grad_late, gains = after(grad_late, gains)
    ends = [0, n * qw, n * qw + KVH * HD, n * qw + 2 * KVH * HD, grad_late.shape[1]]
    grad_query, grad_key, grad_value, grad_out = [
        grad_late[:, start:end].astype(high) for start, end in zip(ends, ends[1:])
    ]

    end = 2 * strip + HD // devices
    return (
        block_out,
        input_grad,
        gains[:strip],
        grad_query,
        grad_key,
        grad_value,
        gains[2 * strip : end],
        gains[end:],
        grad_out,
        gains[strip : 2 * strip],
        grad_gate,
        grad_up,
        grad_down,
    )


def solution(mesh):
    n, m = mesh.shape["ctx"], mesh.shape["fsdp"]
    mesh = Mesh(mesh.devices.reshape(n // 2, 2, m // 2, 2), CTX + LAYER)
    rows = P(LAYER, None)
    line = P(LAYER)
    blocks = P(LAYER, None, CTX, None, None)
    both = P(CTX + LAYER, None)
    both_line = P(CTX + LAYER)
    in_specs = (blocks, rows, blocks, line, rows, rows, rows, line, line, rows, line, rows, rows, rows)
    out_specs = (
        blocks,
        blocks,
        both_line,
        both,
        both,
        both,
        both_line,
        both_line,
        both,
        both_line,
        both,
        both,
        both,
    )
    return jax.shard_map(local, mesh=mesh, in_specs=in_specs, out_specs=out_specs, check_vma=False)
```

```python
import functools

import jax
import jax.numpy as jnp
from jax import lax
from jax.experimental import pallas as pl
from jax.experimental.pallas import tpu as pltpu
from jax.sharding import Mesh
from jax.sharding import PartitionSpec as P

H = 16
KVH = 8
HD = 128
BLOCK = 64
TILE = 256

epsilon = 1e-06
theta_base = 1000000.0
score_scale = HD ** (-0.5)
low = jnp.bfloat16
high = jnp.float32
vmem_bytes = 48 << 20


def dot(left, right):
    return jnp.dot(left, right, preferred_element_type=high)


def dot_t(left, right):
    return lax.dot_general(left, right, (((1,), (1,)), ((), ())), preferred_element_type=high)


def t_dot(left, right):
    return lax.dot_general(left, right, (((0,), (0,)), ((), ())), preferred_element_type=high)


def mean_last(values):
    return jnp.mean(values, axis=-1, keepdims=True)


def rms_factor(values):
    return lax.rsqrt(mean_last(values * values) + epsilon)


def head_cols(head):
    return slice(head * HD, (head + 1) * HD)


def visible_tile(segc_ref, segr_ref, first, keys):
    rows = lax.broadcasted_iota(jnp.int32, (TILE, keys), 0) + first
    cols = lax.broadcasted_iota(jnp.int32, (TILE, keys), 1)
    same = segc_ref[first : first + TILE, :] == segr_ref[:, :keys]
    return same & (cols <= rows)


def attend_kernel(
    sources_ref,
    places_ref,
    raw_ref,
    cos_ref,
    sin_ref,
    qg_ref,
    kg_ref,
    segc_ref,
    segr_ref,
    rel_ref,
    abs_ref,
    q_ref,
    k_ref,
    v_ref,
    log_ref,
):
    total = q_ref.shape[0]
    heads = q_ref.shape[1] // HD
    blocks = total // BLOCK

    def prepare(index, carry):
        source = pl.multiple_of(sources_ref[index] * BLOCK, BLOCK)
        target = pl.multiple_of(index * BLOCK, BLOCK)
        raw = raw_ref[pl.ds(source, BLOCK), :]
        cosine = cos_ref[pl.ds(target, BLOCK), :]
        sine = sin_ref[pl.ds(target, BLOCK), :]
        for head in range(heads + 1):
            values = raw[:, head_cols(head)]
            gain = qg_ref[...] if head < heads else kg_ref[...]
            normed = values * rms_factor(values) * gain
            turned = (normed * cosine + pltpu.roll(normed, HD // 2, 1) * sine).astype(low)
            if head < heads:
                q_ref[pl.ds(target, BLOCK), head_cols(head)] = turned
            else:
                k_ref[pl.ds(target, BLOCK), :] = turned
        v_ref[pl.ds(target, BLOCK), :] = raw[:, head_cols(heads + 1)].astype(low)
        return carry

    lax.fori_loop(0, blocks, prepare, 0)
    for tile in range(total // TILE):
        first = tile * TILE
        keys = first + TILE
        visible = visible_tile(segc_ref, segr_ref, first, keys)
        for head in range(heads):
            scores = dot_t(q_ref[first : first + TILE, head_cols(head)], k_ref[:keys, :])
            scores = jnp.where(visible, scores * score_scale, -jnp.inf)
            peak = jnp.max(scores, axis=-1, keepdims=True)
            powers = jnp.exp(scores - peak)
            sums = jnp.sum(powers, axis=-1, keepdims=True)
            probs = (powers / sums).astype(low)
            mixed = dot(probs, v_ref[:keys, :]).astype(low)
            log_ref[first : first + TILE, head : head + 1] = peak + jnp.log(sums)
            for part in range(TILE // BLOCK):
                index = first // BLOCK + part
                piece = mixed[part * BLOCK : (part + 1) * BLOCK, :]
                target = pl.multiple_of(sources_ref[index] * BLOCK, BLOCK)
                rel_ref[pl.ds(target, BLOCK), head_cols(head)] = piece
                target = pl.multiple_of(places_ref[index] * BLOCK, BLOCK)
                abs_ref[pl.ds(target, BLOCK), head_cols(head)] = piece


def attend_back_kernel(
    sources_ref,
    places_ref,
    raw_ref,
    cos_ref,
    sin_ref,
    qg_ref,
    kg_ref,
    segc_ref,
    segr_ref,
    q_ref,
    k_ref,
    v_ref,
    log_ref,
    up_ref,
    out_ref,
    gains_ref,
    dq_ref,
    dk_ref,
    dv_ref,
):
    total = q_ref.shape[0]
    heads = q_ref.shape[1] // HD
    blocks = total // BLOCK
    dk_ref[...] = jnp.zeros_like(dk_ref)
    dv_ref[...] = jnp.zeros_like(dv_ref)
    for tile in range(total // TILE):
        first = tile * TILE
        keys = first + TILE
        visible = visible_tile(segc_ref, segr_ref, first, keys)
        for head in range(heads):
            pieces = []
            for part in range(TILE // BLOCK):
                source = pl.multiple_of(places_ref[first // BLOCK + part] * BLOCK, BLOCK)
                pieces.append(up_ref[pl.ds(source, BLOCK), head_cols(head)])
            upstream = jnp.concatenate(pieces, axis=0)
            query = q_ref[first : first + TILE, head_cols(head)]
            key = k_ref[:keys, :]
            scores = dot_t(query, key) * score_scale
            shifted = scores - log_ref[first : first + TILE, head : head + 1]
            probs = jnp.exp(jnp.where(visible, shifted, -jnp.inf))
            dprobs = dot_t(upstream, v_ref[:keys, :])
            inner = jnp.sum(probs * dprobs, axis=-1, keepdims=True)
            dscores = (probs * (dprobs - inner)).astype(low)
            dq_ref[first : first + TILE, head_cols(head)] = dot(dscores, key) * score_scale
            dk_ref[:keys, :] += t_dot(dscores, query) * score_scale
            dv_ref[:keys, :] += t_dot(probs.astype(low), upstream)

    def finish(index, carry):
        target = pl.multiple_of(sources_ref[index] * BLOCK, BLOCK)
        source = pl.multiple_of(index * BLOCK, BLOCK)
        raw = raw_ref[pl.ds(target, BLOCK), :]
        cosine = cos_ref[pl.ds(source, BLOCK), :]
        sine = sin_ref[pl.ds(source, BLOCK), :]
        gains = list(carry)
        for head in range(heads + 1):
            values = raw[:, head_cols(head)]
            if head < heads:
                upstream, gain, slot = dq_ref[pl.ds(source, BLOCK), head_cols(head)], qg_ref[...], 0
            else:
                upstream, gain, slot = dk_ref[pl.ds(source, BLOCK), :], kg_ref[...], 1
            upstream = upstream * cosine - pltpu.roll(upstream, HD // 2, 1) * sine
            factor = rms_factor(values)
            gains[slot] = gains[slot] + jnp.sum(upstream * values * factor, axis=0, keepdims=True)
            scaled = gain * upstream
            inner = mean_last(values * scaled)
            back = factor * scaled - values * (factor * factor * factor) * inner
            out_ref[pl.ds(target, BLOCK), head_cols(head)] = back.astype(low)
        out_ref[pl.ds(target, BLOCK), head_cols(heads + 1)] = dv_ref[pl.ds(source, BLOCK), :].astype(low)
        return tuple(gains)

    zero = jnp.zeros((1, HD), high)
    query_gain, key_gain = lax.fori_loop(0, blocks, finish, (zero, zero))
    gains_ref[0:1, :] = query_gain
    gains_ref[1:2, :] = key_gain


def in_memory(kinds):
    return [pl.BlockSpec(memory_space=kind) for kind in kinds]


def attend(total, heads, *operands):
    shapes = (
        jax.ShapeDtypeStruct((total, heads * HD), low),
        jax.ShapeDtypeStruct((total, heads * HD), low),
        jax.ShapeDtypeStruct((total, heads * HD), low),
        jax.ShapeDtypeStruct((total, HD), low),
        jax.ShapeDtypeStruct((total, HD), low),
        jax.ShapeDtypeStruct((total, HD), high),
    )
    return pl.pallas_call(
        attend_kernel,
        out_shape=shapes,
        in_specs=in_memory([pltpu.SMEM] * 2 + [pltpu.VMEM] * (len(operands) - 2)),
        out_specs=in_memory([pltpu.VMEM] * len(shapes)),
        compiler_params=pltpu.CompilerParams(vmem_limit_bytes=vmem_bytes),
        name="attend",
    )(*operands)


def attend_back(total, heads, *operands):
    shapes = (
        jax.ShapeDtypeStruct((total, (heads + 2) * HD), low),
        jax.ShapeDtypeStruct((2, HD), high),
    )
    return pl.pallas_call(
        attend_back_kernel,
        out_shape=shapes,
        in_specs=in_memory([pltpu.SMEM] * 2 + [pltpu.VMEM] * (len(operands) - 2)),
        out_specs=in_memory([pltpu.VMEM] * len(shapes)),
        scratch_shapes=[
            pltpu.VMEM((total, heads * HD), high),
            pltpu.VMEM((total, HD), high),
            pltpu.VMEM((total, HD), high),
        ],
        compiler_params=pltpu.CompilerParams(vmem_limit_bytes=vmem_bytes),
        name="attend_back",
    )(*operands)


def project_back_kernel(chips, *refs):
    owners_ref, sums_ref, middle_ref, up_ref, gain_ref = refs[:5]
    (grad_ref, low_ref, gain_grad_ref, out_ref, weights_ref, sems) = refs[-6:]
    blocks = refs[5:-6]
    copies = [
        pltpu.make_async_copy(block, weights_ref.at[i], sems.at[i]) for i, block in enumerate(blocks)
    ]
    for copy in copies:
        copy.start()
    upstream = sums_ref[0].astype(high)
    for chip in range(1, chips):
        upstream = upstream + sums_ref[chip].astype(high)
    values = middle_ref[...]
    factor = rms_factor(values)
    gain_grad_ref[...] = jnp.sum(upstream * values * factor, axis=0, keepdims=True)
    scaled = gain_ref[...] * upstream
    inner = mean_last(values * scaled)
    back = factor * scaled - values * (factor * factor * factor) * inner
    grad = up_ref[...].astype(high) + back
    grad_ref[...] = grad
    low_ref[...] = grad.astype(low)
    cols = weights_ref.shape[2]
    total = 0.0
    for i, copy in enumerate(copies):
        start = pl.multiple_of(owners_ref[i] * cols, cols)
        copy.wait()
        total = total + dot_t(low_ref[:, pl.ds(start, cols)], weights_ref[i])
    total = total.astype(low)
    width = out_ref.shape[2]
    for i in range(out_ref.shape[0]):
        out_ref[i] = total[:, i * width : (i + 1) * width]


def project_back(owners, sums, middle, upstream, gain, blocks):
    rows, width = middle.shape
    count = len(blocks)
    depth, cols = blocks[0].shape
    shapes = (
        jax.ShapeDtypeStruct((rows, width), high),
        jax.ShapeDtypeStruct((rows, width), low),
        jax.ShapeDtypeStruct((1, width), high),
        jax.ShapeDtypeStruct((count, rows, depth // count), low),
    )
    return pl.pallas_call(
        functools.partial(project_back_kernel, sums.shape[0]),
        out_shape=shapes,
        in_specs=in_memory([pltpu.SMEM] + [pltpu.VMEM] * 4 + [pl.ANY] * count),
        out_specs=in_memory([pltpu.VMEM] * len(shapes)),
        scratch_shapes=[pltpu.VMEM((count, depth, cols), low), pltpu.SemaphoreType.DMA((count,))],
        compiler_params=pltpu.CompilerParams(vmem_limit_bytes=vmem_bytes),
        name="project_back",
    )(owners, sums, middle, upstream, gain, *blocks)


def arrange_kernel(piece, in_ref, gate_ref, up_ref):
    count, _, width = in_ref.shape
    hidden = width // 2
    for half, out_ref in enumerate((gate_ref, up_ref)):
        for layer in range(hidden // piece):
            start = half * hidden + layer * piece
            parts = [in_ref[i, :, start : start + piece].astype(high) for i in range(count)]
            target = layer * count * piece
            out_ref[:, target : target + count * piece] = jnp.concatenate(parts, axis=1)


def arrange(grads, piece):
    count, rows, width = grads.shape
    shape = jax.ShapeDtypeStruct((rows, count * width // 2), high)
    return pl.pallas_call(
        functools.partial(arrange_kernel, piece),
        out_shape=(shape, shape),
        in_specs=in_memory([pltpu.VMEM]),
        out_specs=in_memory([pltpu.VMEM] * 2),
        compiler_params=pltpu.CompilerParams(vmem_limit_bytes=vmem_bytes),
        name="arrange",
    )(grads)


CTX = ("chip", "core")
LAYER = ("hi", "lo")


def swap(values, axis, mask=1):
    size = lax.axis_size(axis)
    return lax.ppermute(values, axis, [(i, i ^ mask) for i in range(size)])


def exchange(values, axis):
    return lax.all_to_all(values, axis, 0, 0, tiled=True)


def gather(values):
    copies = jnp.broadcast_to(values[None], (lax.axis_size("chip"),) + values.shape)
    half = exchange(copies, "chip").reshape(-1, values.shape[-1])
    return half, swap(half, "core")


def sum_cores(keep, give):
    return (keep.astype(high) + swap(give, "core").astype(high)).astype(low)


def sum_chips(half):
    size = lax.axis_size("chip")
    chip = lax.axis_index("chip")
    rows = half.shape[0] // size
    total = rows_of(half, chip, rows).astype(high)
    for mask in range(1, size):
        total = total + swap(rows_of(half, chip ^ mask, rows), "chip", mask).astype(high)
    return total


def send_chips(half):
    size = lax.axis_size("chip")
    return exchange(half.reshape(size, half.shape[0] // size, -1), "chip")


def spread(values, axis):
    return [values] + [swap(values, axis, mask) for mask in range(1, lax.axis_size(axis))]


def in_order(pieces, index):
    rows = pieces[0].shape[0]
    whole = jnp.zeros((len(pieces) * rows,) + pieces[0].shape[1:], pieces[0].dtype)
    for mask, piece in enumerate(pieces):
        whole = lax.dynamic_update_slice_in_dim(whole, piece, (index ^ mask) * rows, axis=0)
    return whole


def halves(values):
    middle = values.shape[0] // 2
    return values[:middle], values[middle:]


def after(values, *others):
    return lax.optimization_barrier((values,) + others)


def columns_of(values, index, width):
    return lax.dynamic_slice_in_dim(values, index * width, width, axis=1)


def rows_of(values, index, height):
    return lax.dynamic_slice_in_dim(values, index * height, height, axis=0)


def sum_parts(lefts, rights):
    return sum(t_dot(left, right) for left, right in zip(lefts, rights)).astype(low)


def gather_rows(values):
    return lax.all_gather(values, LAYER, axis=0, tiled=True)


def scatter_rows(values):
    return lax.psum_scatter(values, LAYER, scatter_dimension=0, tiled=True)


def local(
    tokens,
    segment_ids,
    cotangent,
    norm_attn,
    w_query,
    w_key,
    w_value,
    q_gain,
    k_gain,
    w_out,
    norm_ffn,
    w_gate,
    w_up,
    w_down,
):
    n = lax.axis_size(CTX)
    m = lax.axis_size(LAYER)
    me = lax.axis_index(CTX)
    chip = lax.axis_index("chip")
    core = lax.axis_index("core")
    chips = n // 2
    width = tokens.shape[-1]
    own = 2 * BLOCK
    total = n * own
    heads = H // n
    repeat = n // KVH
    qw = heads * HD
    hidden = w_gate.shape[1] // n
    piece = hidden // m
    strip = width // (n * m)
    assert tokens.shape[0] == 1 and heads * n == H and repeat * KVH == n

    own_tokens = tokens.reshape(own, width)
    own_cotangent = cotangent.reshape(own, width)
    out_cols = width // n
    attn_w = jnp.concatenate(
        [
            columns_of(w_out, me, out_cols),
            columns_of(w_query, me, qw),
            columns_of(w_key, me // repeat, HD),
            columns_of(w_value, me // repeat, HD),
        ],
        axis=1,
    )
    own_tokens, attn_w = after(own_tokens, attn_w)
    layer = lax.axis_index(LAYER)
    attn_w = gather_rows(attn_w)

    small = jnp.concatenate([norm_attn, norm_ffn, q_gain, k_gain]).reshape(1, -1)
    small = in_order(spread(small, LAYER), layer).astype(high)
    part, gain_part = norm_attn.shape[0], q_gain.shape[0]
    gain_attn = small[:, :part].reshape(-1)
    gain_ffn = small[:, part : 2 * part].reshape(-1)
    query_gain = small[:, 2 * part : 2 * part + gain_part].reshape(1, HD)
    key_gain = small[:, 2 * part + gain_part :].reshape(1, HD)

    def hidden_columns(weights):
        starts = [(i * n + me) * piece for i in range(m)]
        return [lax.dynamic_slice_in_dim(weights, start, piece, axis=1) for start in starts]

    gate_up_w = jnp.concatenate(hidden_columns(w_gate) + hidden_columns(w_up), axis=1)
    down_w = rows_of(w_down, me, piece)
    token_half = exchange(jnp.broadcast_to(own_tokens, (chips, own, width)), "chip").reshape(-1, width)
    token_half, own_cotangent, gate_up_w, down_w = after(
        token_half, own_cotangent, gate_up_w, down_w
    )
    upstream_half = in_order(spread(own_cotangent, "chip"), chip)
    upstream_half, attn_w = after(upstream_half, attn_w)
    out_w, qkv_w = attn_w[:, :out_cols], attn_w[:, out_cols:]
    token_parts = (token_half, swap(token_half, "core"))
    gate_up_w = gather_rows(gate_up_w)
    down_w = gather_rows(down_w)

    out_half = spread(out_w, "chip")
    owners = [me ^ (2 * mask) for mask in range(chips)]
    owners = owners + [owner ^ 1 for owner in owners]

    def by_layer(grads):
        return grads.reshape(n, m, strip, -1).transpose(1, 0, 2, 3).reshape(width, -1)

    def own_hidden(grads):
        whole = jnp.zeros_like(grads)
        for step in range(m):
            targets = [(i, ((step + i) % m * n + i) // m) for i in range(n)]
            rows = lax.ppermute(rows_of(grads, (step + me) % m, piece), CTX, targets)
            place = (me // (n // m) - step) % m * piece
            whole = lax.dynamic_update_slice_in_dim(whole, rows, place, axis=0)
        return whole

    natural = jnp.arange(2 * n, dtype=jnp.int32)
    side = (natural >= n).astype(jnp.int32)
    owner = jnp.where(side == 0, natural, 2 * n - 1 - natural)
    sources = 2 * (((owner & 1) ^ core) * chips + (owner >> 1)) + side
    places = 2 * owner + side

    segments = segment_ids.reshape(total)
    starts = jnp.sum((segments[None, :] < segments[:, None]).astype(jnp.int32), axis=1)
    place = jnp.arange(total, dtype=jnp.int32) - starts
    frequency = theta_base ** (-(jnp.arange(HD // 2, dtype=high) * 2.0) / HD)
    angles = place.astype(high)[:, None] * frequency
    cosine = jnp.cos(angles)
    sine = jnp.sin(angles)
    cosine = jnp.concatenate([cosine, cosine], axis=1)
    sine = jnp.concatenate([-sine, sine], axis=1)
    segment_column = segments.reshape(total, 1)
    segment_row = segments.reshape(1, total)

    normed_parts = []
    for tokens_part in token_parts:
        features = tokens_part.astype(high)
        normed_parts.append((features * rms_factor(features) * gain_attn).astype(low))
    qkv_raw = jnp.concatenate([dot(normed, qkv_w) for normed in normed_parts], axis=0)
    tables = (cosine, sine, query_gain, key_gain, segment_column, segment_row)
    mixed_rel, mixed_abs, query, key, value, logs = attend(
        total, heads, sources, places, qkv_raw, *tables
    )
    mixed = exchange(mixed_abs.reshape(n, own, qw), CTX)
    out_blocks = out_half + [swap(block, "core") for block in out_half]
    mixed = mixed.transpose(1, 0, 2).reshape(own, n * qw)
    own_features = own_tokens.astype(high)
    branch = jnp.zeros((own, width), high)
    for block_owner, block in zip(owners, out_blocks):
        branch = lax.dynamic_update_slice_in_dim(branch, dot(mixed, block), block_owner * out_cols, axis=1)
    middle = own_features + branch
    factor_ffn = rms_factor(middle)
    ffn_own = (middle * factor_ffn * gain_ffn).astype(low)
    ffn_parts = gather(ffn_own)
    upstream_parts = (upstream_half, swap(upstream_half, "core"))

    hidden_parts, gates = [], []
    for ffn_low in ffn_parts:
        gate_up = dot(ffn_low, gate_up_w)
        gate, up = gate_up[:, :hidden], gate_up[:, hidden:]
        sigmoid = jax.nn.sigmoid(gate)
        silu = gate * sigmoid
        hidden_parts.append((silu * up).astype(low))
        gates.append((up * sigmoid * (1.0 + gate * (1.0 - sigmoid)), silu))
    grad_down = own_hidden(sum_parts(hidden_parts, upstream_parts))
    grad_down, down_w = after(grad_down, down_w)
    gate_up_grads = []
    for upstream_low, (gate_slope, silu) in zip(upstream_parts, gates):
        grad_hidden = dot_t(upstream_low, down_w)
        grads = [(grad_hidden * gate_slope).astype(low), (grad_hidden * silu).astype(low)]
        gate_up_grads.append(jnp.concatenate(grads, axis=1))
    grad_ffn = [dot_t(grads, gate_up_w).astype(low) for grads in gate_up_grads]
    grad_gate_up = by_layer(sum_parts(ffn_parts, gate_up_grads))
    grad_ffn = send_chips(sum_cores(grad_ffn[0], grad_ffn[1]))
    grad_down = scatter_rows(grad_down)
    grad_ffn, grad_gate_up, grad_down = after(grad_ffn, grad_gate_up, grad_down)
    grad_gate_up = scatter_rows(grad_gate_up)

    grad_middle, middle_low, grad_gain_ffn, mixed_grad = project_back(
        jnp.stack(owners), grad_ffn, middle, own_cotangent, gain_ffn.reshape(1, -1), out_blocks
    )
    mixed_grad, *hidden_parts = after(mixed_grad, *hidden_parts)
    block_parts = [dot(values, down_w).astype(low) for values in hidden_parts]
    block_half = sum_cores(block_parts[0], block_parts[1])
    mixed_grad, block_half = after(exchange(mixed_grad, CTX), block_half)
    block_sum = sum_chips(block_half)
    mixed_grad = mixed_grad.reshape(total, qw)
    late_half = in_order(spread(middle_low, "chip"), chip)
    qkv_grad, grad_gains = attend_back(
        total, heads, sources, places, qkv_raw, *tables, query, key, value, logs, mixed_grad
    )
    qkv_grad, late_half = after(qkv_grad, late_half)
    grad_out = sum_parts(halves(mixed_rel), (late_half, swap(late_half, "core")))
    qkv_grads = halves(qkv_grad)
    grad_attn = [dot_t(grads, qkv_w).astype(low) for grads in qkv_grads]
    attn_half = sum_cores(grad_attn[0], grad_attn[1])
    grad_qkv = sum_parts(normed_parts, qkv_grads).reshape(n, m * strip, -1)
    block_sum, grad_qkv = after(block_sum, grad_qkv)
    block_out = (middle + block_sum).astype(low).reshape(tokens.shape)
    grad_qkv = exchange(grad_qkv, CTX).reshape(n, m, strip, -1)

    def all_heads(grads):
        return grads.transpose(1, 2, 0, 3).reshape(m, strip, -1)

    def grad_of_kv(grads):
        grads = jnp.sum(grads.reshape(KVH, repeat, m, strip, HD).astype(high), axis=1)
        return all_heads(grads.astype(low))

    grad_late = [
        all_heads(grad_qkv[..., :qw]),
        grad_of_kv(grad_qkv[..., qw : qw + HD]),
        grad_of_kv(grad_qkv[..., qw + HD :]),
        grad_out.reshape(m, strip, width),
    ]
    grad_late = jnp.concatenate(grad_late, axis=2).reshape(m * strip, -1)
    grad_late, attn_half = after(grad_late, attn_half)
    grad_attn = sum_chips(attn_half)
    grad_late = scatter_rows(grad_late)

    grad_attn, grad_gate_up = after(grad_attn, grad_gate_up)
    grad_gate_up = exchange(grad_gate_up.reshape(n, strip, -1), CTX)
    factor_attn = rms_factor(own_features)
    scaled = gain_attn * grad_attn
    inner = mean_last(own_features * scaled)
    input_grad = grad_middle + factor_attn * scaled - own_features * factor_attn**3 * inner
    grad_gain_attn = jnp.sum(grad_attn * own_features * factor_attn, axis=0)
    input_grad = input_grad.reshape(tokens.shape)

    devices = n * m
    partial = jnp.concatenate(
        [
            grad_gain_attn.reshape(devices, -1),
            grad_gain_ffn.reshape(devices, -1),
            grad_gains[0].reshape(devices, -1),
            grad_gains[1].reshape(devices, -1),
        ],
        axis=1,
    )
    grad_gate_up, partial = after(grad_gate_up, partial)
    gains = exchange(partial, CTX + LAYER)
    gains = jnp.sum(gains, axis=0)
    grad_down = grad_down.astype(high)
    grad_gate, grad_up = arrange(grad_gate_up, piece)
    grad_late, gains = after(grad_late, gains)
    ends = [0, n * qw, n * qw + KVH * HD, n * qw + 2 * KVH * HD, grad_late.shape[1]]
    grad_query, grad_key, grad_value, grad_out = [
        grad_late[:, start:end].astype(high) for start, end in zip(ends, ends[1:])
    ]

    end = 2 * strip + HD // devices
    return (
        block_out,
        input_grad,
        gains[:strip],
        grad_query,
        grad_key,
        grad_value,
        gains[2 * strip : end],
        gains[end:],
        grad_out,
        gains[strip : 2 * strip],
        grad_gate,
        grad_up,
        grad_down,
    )


def solution(mesh):
    n, m = mesh.shape["ctx"], mesh.shape["fsdp"]
    mesh = Mesh(mesh.devices.reshape(n // 2, 2, m // 2, 2), CTX + LAYER)
    rows = P(LAYER, None)
    line = P(LAYER)
    blocks = P(LAYER, None, CTX, None, None)
    both = P(CTX + LAYER, None)
    both_line = P(CTX + LAYER)
    in_specs = (blocks, rows, blocks, line, rows, rows, rows, line, line, rows, line, rows, rows, rows)
    out_specs = (
        blocks,
        blocks,
        both_line,
        both,
        both,
        both,
        both_line,
        both_line,
        both,
        both_line,
        both,
        both,
        both,
    )
    return jax.shard_map(local, mesh=mesh, in_specs=in_specs, out_specs=out_specs, check_vma=False)
```

```python
import functools

import jax
import jax.numpy as jnp
from jax import lax
from jax.experimental import pallas as pl
from jax.experimental.pallas import tpu as pltpu
from jax.sharding import Mesh
from jax.sharding import PartitionSpec as P

H = 16
KVH = 8
HD = 128
BLOCK = 64
TILE = 256

epsilon = 1e-06
theta_base = 1000000.0
score_scale = HD ** (-0.5)
low = jnp.bfloat16
high = jnp.float32
vmem_bytes = 48 << 20


def dot(left, right):
    return jnp.dot(left, right, preferred_element_type=high)


def dot_t(left, right):
    return lax.dot_general(left, right, (((1,), (1,)), ((), ())), preferred_element_type=high)


def t_dot(left, right):
    return lax.dot_general(left, right, (((0,), (0,)), ((), ())), preferred_element_type=high)


def mean_last(values):
    return jnp.mean(values, axis=-1, keepdims=True)


def rms_factor(values):
    return lax.rsqrt(mean_last(values * values) + epsilon)


def head_cols(head):
    return slice(head * HD, (head + 1) * HD)


def visible_tile(segc_ref, segr_ref, first, keys):
    rows = lax.broadcasted_iota(jnp.int32, (TILE, keys), 0) + first
    cols = lax.broadcasted_iota(jnp.int32, (TILE, keys), 1)
    same = segc_ref[first : first + TILE, :] == segr_ref[:, :keys]
    return same & (cols <= rows)


def attend_kernel(
    sources_ref,
    places_ref,
    raw_ref,
    cos_ref,
    sin_ref,
    qg_ref,
    kg_ref,
    segc_ref,
    segr_ref,
    rel_ref,
    abs_ref,
    q_ref,
    k_ref,
    v_ref,
    log_ref,
):
    total = q_ref.shape[0]
    heads = q_ref.shape[1] // HD
    blocks = total // BLOCK

    def prepare(index, carry):
        source = pl.multiple_of(sources_ref[index] * BLOCK, BLOCK)
        target = pl.multiple_of(index * BLOCK, BLOCK)
        raw = raw_ref[pl.ds(source, BLOCK), :]
        cosine = cos_ref[pl.ds(target, BLOCK), :]
        sine = sin_ref[pl.ds(target, BLOCK), :]
        for head in range(heads + 1):
            values = raw[:, head_cols(head)]
            gain = qg_ref[...] if head < heads else kg_ref[...]
            normed = values * rms_factor(values) * gain
            turned = (normed * cosine + pltpu.roll(normed, HD // 2, 1) * sine).astype(low)
            if head < heads:
                q_ref[pl.ds(target, BLOCK), head_cols(head)] = turned
            else:
                k_ref[pl.ds(target, BLOCK), :] = turned
        v_ref[pl.ds(target, BLOCK), :] = raw[:, head_cols(heads + 1)].astype(low)
        return carry

    lax.fori_loop(0, blocks, prepare, 0)
    for tile in range(total // TILE):
        first = tile * TILE
        keys = first + TILE
        visible = visible_tile(segc_ref, segr_ref, first, keys)
        for head in range(heads):
            scores = dot_t(q_ref[first : first + TILE, head_cols(head)], k_ref[:keys, :])
            scores = jnp.where(visible, scores * score_scale, -jnp.inf)
            peak = jnp.max(scores, axis=-1, keepdims=True)
            powers = jnp.exp(scores - peak)
            sums = jnp.sum(powers, axis=-1, keepdims=True)
            probs = (powers / sums).astype(low)
            mixed = dot(probs, v_ref[:keys, :]).astype(low)
            log_ref[first : first + TILE, head : head + 1] = peak + jnp.log(sums)
            for part in range(TILE // BLOCK):
                index = first // BLOCK + part
                piece = mixed[part * BLOCK : (part + 1) * BLOCK, :]
                target = pl.multiple_of(sources_ref[index] * BLOCK, BLOCK)
                rel_ref[pl.ds(target, BLOCK), head_cols(head)] = piece
                target = pl.multiple_of(places_ref[index] * BLOCK, BLOCK)
                abs_ref[pl.ds(target, BLOCK), head_cols(head)] = piece


def attend_back_kernel(
    sources_ref,
    places_ref,
    raw_ref,
    cos_ref,
    sin_ref,
    qg_ref,
    kg_ref,
    segc_ref,
    segr_ref,
    q_ref,
    k_ref,
    v_ref,
    log_ref,
    up_ref,
    out_ref,
    gains_ref,
    dq_ref,
    dk_ref,
    dv_ref,
):
    total = q_ref.shape[0]
    heads = q_ref.shape[1] // HD
    blocks = total // BLOCK
    dk_ref[...] = jnp.zeros_like(dk_ref)
    dv_ref[...] = jnp.zeros_like(dv_ref)
    for tile in range(total // TILE):
        first = tile * TILE
        keys = first + TILE
        visible = visible_tile(segc_ref, segr_ref, first, keys)
        for head in range(heads):
            pieces = []
            for part in range(TILE // BLOCK):
                source = pl.multiple_of(places_ref[first // BLOCK + part] * BLOCK, BLOCK)
                pieces.append(up_ref[pl.ds(source, BLOCK), head_cols(head)])
            upstream = jnp.concatenate(pieces, axis=0)
            query = q_ref[first : first + TILE, head_cols(head)]
            key = k_ref[:keys, :]
            scores = dot_t(query, key) * score_scale
            shifted = scores - log_ref[first : first + TILE, head : head + 1]
            probs = jnp.exp(jnp.where(visible, shifted, -jnp.inf))
            dprobs = dot_t(upstream, v_ref[:keys, :])
            inner = jnp.sum(probs * dprobs, axis=-1, keepdims=True)
            dscores = (probs * (dprobs - inner)).astype(low)
            dq_ref[first : first + TILE, head_cols(head)] = dot(dscores, key) * score_scale
            dk_ref[:keys, :] += t_dot(dscores, query) * score_scale
            dv_ref[:keys, :] += t_dot(probs.astype(low), upstream)

    def finish(index, carry):
        target = pl.multiple_of(sources_ref[index] * BLOCK, BLOCK)
        source = pl.multiple_of(index * BLOCK, BLOCK)
        raw = raw_ref[pl.ds(target, BLOCK), :]
        cosine = cos_ref[pl.ds(source, BLOCK), :]
        sine = sin_ref[pl.ds(source, BLOCK), :]
        gains = list(carry)
        for head in range(heads + 1):
            values = raw[:, head_cols(head)]
            if head < heads:
                upstream, gain, slot = dq_ref[pl.ds(source, BLOCK), head_cols(head)], qg_ref[...], 0
            else:
                upstream, gain, slot = dk_ref[pl.ds(source, BLOCK), :], kg_ref[...], 1
            upstream = upstream * cosine - pltpu.roll(upstream, HD // 2, 1) * sine
            factor = rms_factor(values)
            gains[slot] = gains[slot] + jnp.sum(upstream * values * factor, axis=0, keepdims=True)
            scaled = gain * upstream
            inner = mean_last(values * scaled)
            back = factor * scaled - values * (factor * factor * factor) * inner
            out_ref[pl.ds(target, BLOCK), head_cols(head)] = back.astype(low)
        out_ref[pl.ds(target, BLOCK), head_cols(heads + 1)] = dv_ref[pl.ds(source, BLOCK), :].astype(low)
        return tuple(gains)

    zero = jnp.zeros((1, HD), high)
    query_gain, key_gain = lax.fori_loop(0, blocks, finish, (zero, zero))
    gains_ref[0:1, :] = query_gain
    gains_ref[1:2, :] = key_gain


def in_memory(kinds):
    return [pl.BlockSpec(memory_space=kind) for kind in kinds]


def attend(total, heads, *operands):
    shapes = (
        jax.ShapeDtypeStruct((total, heads * HD), low),
        jax.ShapeDtypeStruct((total, heads * HD), low),
        jax.ShapeDtypeStruct((total, heads * HD), low),
        jax.ShapeDtypeStruct((total, HD), low),
        jax.ShapeDtypeStruct((total, HD), low),
        jax.ShapeDtypeStruct((total, HD), high),
    )
    return pl.pallas_call(
        attend_kernel,
        out_shape=shapes,
        in_specs=in_memory([pltpu.SMEM] * 2 + [pltpu.VMEM] * (len(operands) - 2)),
        out_specs=in_memory([pltpu.VMEM] * len(shapes)),
        compiler_params=pltpu.CompilerParams(vmem_limit_bytes=vmem_bytes),
        name="attend",
    )(*operands)


def attend_back(total, heads, *operands):
    shapes = (
        jax.ShapeDtypeStruct((total, (heads + 2) * HD), low),
        jax.ShapeDtypeStruct((2, HD), high),
    )
    return pl.pallas_call(
        attend_back_kernel,
        out_shape=shapes,
        in_specs=in_memory([pltpu.SMEM] * 2 + [pltpu.VMEM] * (len(operands) - 2)),
        out_specs=in_memory([pltpu.VMEM] * len(shapes)),
        scratch_shapes=[
            pltpu.VMEM((total, heads * HD), high),
            pltpu.VMEM((total, HD), high),
            pltpu.VMEM((total, HD), high),
        ],
        compiler_params=pltpu.CompilerParams(vmem_limit_bytes=vmem_bytes),
        name="attend_back",
    )(*operands)


def project_back_kernel(chips, *refs):
    owners_ref, sums_ref, middle_ref, up_ref, gain_ref = refs[:5]
    (grad_ref, low_ref, gain_grad_ref, out_ref, weights_ref, sems) = refs[-6:]
    blocks = refs[5:-6]
    copies = [
        pltpu.make_async_copy(block, weights_ref.at[i], sems.at[i]) for i, block in enumerate(blocks)
    ]
    for copy in copies:
        copy.start()
    upstream = sums_ref[0].astype(high)
    for chip in range(1, chips):
        upstream = upstream + sums_ref[chip].astype(high)
    values = middle_ref[...]
    factor = rms_factor(values)
    gain_grad_ref[...] = jnp.sum(upstream * values * factor, axis=0, keepdims=True)
    scaled = gain_ref[...] * upstream
    inner = mean_last(values * scaled)
    back = factor * scaled - values * (factor * factor * factor) * inner
    grad = up_ref[...].astype(high) + back
    grad_ref[...] = grad
    low_ref[...] = grad.astype(low)
    cols = weights_ref.shape[2]
    total = 0.0
    for i, copy in enumerate(copies):
        start = pl.multiple_of(owners_ref[i] * cols, cols)
        copy.wait()
        total = total + dot_t(low_ref[:, pl.ds(start, cols)], weights_ref[i])
    total = total.astype(low)
    width = out_ref.shape[2]
    for i in range(out_ref.shape[0]):
        out_ref[i] = total[:, i * width : (i + 1) * width]


def project_back(owners, sums, middle, upstream, gain, blocks):
    rows, width = middle.shape
    count = len(blocks)
    depth, cols = blocks[0].shape
    shapes = (
        jax.ShapeDtypeStruct((rows, width), high),
        jax.ShapeDtypeStruct((rows, width), low),
        jax.ShapeDtypeStruct((1, width), high),
        jax.ShapeDtypeStruct((count, rows, depth // count), low),
    )
    return pl.pallas_call(
        functools.partial(project_back_kernel, sums.shape[0]),
        out_shape=shapes,
        in_specs=in_memory([pltpu.SMEM] + [pltpu.VMEM] * 4 + [pl.ANY] * count),
        out_specs=in_memory([pltpu.VMEM] * len(shapes)),
        scratch_shapes=[pltpu.VMEM((count, depth, cols), low), pltpu.SemaphoreType.DMA((count,))],
        compiler_params=pltpu.CompilerParams(vmem_limit_bytes=vmem_bytes),
        name="project_back",
    )(owners, sums, middle, upstream, gain, *blocks)


def arrange_kernel(piece, in_ref, gate_ref, up_ref):
    count, _, width = in_ref.shape
    hidden = width // 2
    for half, out_ref in enumerate((gate_ref, up_ref)):
        for layer in range(hidden // piece):
            start = half * hidden + layer * piece
            parts = [in_ref[i, :, start : start + piece].astype(high) for i in range(count)]
            target = layer * count * piece
            out_ref[:, target : target + count * piece] = jnp.concatenate(parts, axis=1)


def arrange(grads, piece):
    count, rows, width = grads.shape
    shape = jax.ShapeDtypeStruct((rows, count * width // 2), high)
    return pl.pallas_call(
        functools.partial(arrange_kernel, piece),
        out_shape=(shape, shape),
        in_specs=in_memory([pltpu.VMEM]),
        out_specs=in_memory([pltpu.VMEM] * 2),
        compiler_params=pltpu.CompilerParams(vmem_limit_bytes=vmem_bytes),
        name="arrange",
    )(grads)


CTX = ("chip", "core")
LAYER = ("hi", "lo")


def swap(values, axis, mask=1):
    size = lax.axis_size(axis)
    return lax.ppermute(values, axis, [(i, i ^ mask) for i in range(size)])


def exchange(values, axis):
    return lax.all_to_all(values, axis, 0, 0, tiled=True)


def gather(values):
    copies = jnp.broadcast_to(values[None], (lax.axis_size("chip"),) + values.shape)
    half = exchange(copies, "chip").reshape(-1, values.shape[-1])
    return half, swap(half, "core")


def sum_cores(keep, give):
    return (keep.astype(high) + swap(give, "core").astype(high)).astype(low)


def sum_chips(half):
    size = lax.axis_size("chip")
    chip = lax.axis_index("chip")
    rows = half.shape[0] // size
    total = rows_of(half, chip, rows).astype(high)
    for mask in range(1, size):
        total = total + swap(rows_of(half, chip ^ mask, rows), "chip", mask).astype(high)
    return total


def send_chips(half):
    size = lax.axis_size("chip")
    return exchange(half.reshape(size, half.shape[0] // size, -1), "chip")


def spread(values, axis):
    return [values] + [swap(values, axis, mask) for mask in range(1, lax.axis_size(axis))]


def in_order(pieces, index):
    rows = pieces[0].shape[0]
    whole = jnp.zeros((len(pieces) * rows,) + pieces[0].shape[1:], pieces[0].dtype)
    for mask, piece in enumerate(pieces):
        whole = lax.dynamic_update_slice_in_dim(whole, piece, (index ^ mask) * rows, axis=0)
    return whole


def halves(values):
    middle = values.shape[0] // 2
    return values[:middle], values[middle:]


def after(values, *others):
    return lax.optimization_barrier((values,) + others)


def columns_of(values, index, width):
    return lax.dynamic_slice_in_dim(values, index * width, width, axis=1)


def rows_of(values, index, height):
    return lax.dynamic_slice_in_dim(values, index * height, height, axis=0)


def sum_parts(lefts, rights):
    return sum(t_dot(left, right) for left, right in zip(lefts, rights)).astype(low)


def gather_rows(values):
    return lax.all_gather(values, LAYER, axis=0, tiled=True)


def scatter_rows(values):
    return lax.psum_scatter(values, LAYER, scatter_dimension=0, tiled=True)


def local(
    tokens,
    segment_ids,
    cotangent,
    norm_attn,
    w_query,
    w_key,
    w_value,
    q_gain,
    k_gain,
    w_out,
    norm_ffn,
    w_gate,
    w_up,
    w_down,
):
    n = lax.axis_size(CTX)
    m = lax.axis_size(LAYER)
    me = lax.axis_index(CTX)
    chip = lax.axis_index("chip")
    core = lax.axis_index("core")
    chips = n // 2
    width = tokens.shape[-1]
    own = 2 * BLOCK
    total = n * own
    heads = H // n
    repeat = n // KVH
    qw = heads * HD
    hidden = w_gate.shape[1] // n
    piece = hidden // m
    strip = width // (n * m)
    assert tokens.shape[0] == 1 and heads * n == H and repeat * KVH == n

    own_tokens = tokens.reshape(own, width)
    own_cotangent = cotangent.reshape(own, width)
    out_cols = width // n
    attn_w = jnp.concatenate(
        [
            columns_of(w_out, me, out_cols),
            columns_of(w_query, me, qw),
            columns_of(w_key, me // repeat, HD),
            columns_of(w_value, me // repeat, HD),
        ],
        axis=1,
    )
    own_tokens, attn_w = after(own_tokens, attn_w)
    layer = lax.axis_index(LAYER)
    attn_w = gather_rows(attn_w)

    small = jnp.concatenate([norm_attn, norm_ffn, q_gain, k_gain]).reshape(1, -1)
    small = in_order(spread(small, LAYER), layer).astype(high)
    part, gain_part = norm_attn.shape[0], q_gain.shape[0]
    gain_attn = small[:, :part].reshape(-1)
    gain_ffn = small[:, part : 2 * part].reshape(-1)
    query_gain = small[:, 2 * part : 2 * part + gain_part].reshape(1, HD)
    key_gain = small[:, 2 * part + gain_part :].reshape(1, HD)

    def hidden_columns(weights):
        starts = [(i * n + me) * piece for i in range(m)]
        return [lax.dynamic_slice_in_dim(weights, start, piece, axis=1) for start in starts]

    gate_up_w = jnp.concatenate(hidden_columns(w_gate) + hidden_columns(w_up), axis=1)
    down_w = rows_of(w_down, me, piece)
    token_half = exchange(jnp.broadcast_to(own_tokens, (chips, own, width)), "chip").reshape(-1, width)
    token_half, own_cotangent, gate_up_w, down_w = after(
        token_half, own_cotangent, gate_up_w, down_w
    )
    upstream_half = in_order(spread(own_cotangent, "chip"), chip)
    upstream_half, attn_w = after(upstream_half, attn_w)
    out_w, qkv_w = attn_w[:, :out_cols], attn_w[:, out_cols:]
    token_parts = (token_half, swap(token_half, "core"))
    gate_up_w = gather_rows(gate_up_w)
    down_w = gather_rows(down_w)

    out_half = spread(out_w, "chip")
    owners = [me ^ (2 * mask) for mask in range(chips)]
    owners = owners + [owner ^ 1 for owner in owners]

    def by_layer(grads):
        return grads.reshape(n, m, strip, -1).transpose(1, 0, 2, 3).reshape(width, -1)

    def own_hidden(grads):
        whole = jnp.zeros_like(grads)
        for step in range(m):
            targets = [(i, ((step + i) % m * n + i) // m) for i in range(n)]
            rows = lax.ppermute(rows_of(grads, (step + me) % m, piece), CTX, targets)
            place = (me // (n // m) - step) % m * piece
            whole = lax.dynamic_update_slice_in_dim(whole, rows, place, axis=0)
        return whole

    natural = jnp.arange(2 * n, dtype=jnp.int32)
    side = (natural >= n).astype(jnp.int32)
    owner = jnp.where(side == 0, natural, 2 * n - 1 - natural)
    sources = 2 * (((owner & 1) ^ core) * chips + (owner >> 1)) + side
    places = 2 * owner + side

    segments = segment_ids.reshape(total)
    starts = jnp.sum((segments[None, :] < segments[:, None]).astype(jnp.int32), axis=1)
    place = jnp.arange(total, dtype=jnp.int32) - starts
    frequency = theta_base ** (-(jnp.arange(HD // 2, dtype=high) * 2.0) / HD)
    angles = place.astype(high)[:, None] * frequency
    cosine = jnp.cos(angles)
    sine = jnp.sin(angles)
    cosine = jnp.concatenate([cosine, cosine], axis=1)
    sine = jnp.concatenate([-sine, sine], axis=1)
    segment_column = segments.reshape(total, 1)
    segment_row = segments.reshape(1, total)

    normed_parts = []
    for tokens_part in token_parts:
        features = tokens_part.astype(high)
        normed_parts.append((features * rms_factor(features) * gain_attn).astype(low))
    qkv_raw = jnp.concatenate([dot(normed, qkv_w) for normed in normed_parts], axis=0)
    tables = (cosine, sine, query_gain, key_gain, segment_column, segment_row)
    mixed_rel, mixed_abs, query, key, value, logs = attend(
        total, heads, sources, places, qkv_raw, *tables
    )
    mixed = exchange(mixed_abs.reshape(n, own, qw), CTX)
    out_blocks = out_half + [swap(block, "core") for block in out_half]
    mixed = mixed.transpose(1, 0, 2).reshape(own, n * qw)
    own_features = own_tokens.astype(high)
    branch = jnp.zeros((own, width), high)
    for block_owner, block in zip(owners, out_blocks):
        branch = lax.dynamic_update_slice_in_dim(branch, dot(mixed, block), block_owner * out_cols, axis=1)
    middle = own_features + branch
    factor_ffn = rms_factor(middle)
    ffn_own = (middle * factor_ffn * gain_ffn).astype(low)
    ffn_parts = gather(ffn_own)
    upstream_parts = (upstream_half, swap(upstream_half, "core"))

    hidden_parts, gates = [], []
    for ffn_low in ffn_parts:
        gate_up = dot(ffn_low, gate_up_w)
        gate, up = gate_up[:, :hidden], gate_up[:, hidden:]
        sigmoid = jax.nn.sigmoid(gate)
        silu = gate * sigmoid
        hidden_parts.append((silu * up).astype(low))
        gates.append((up * sigmoid * (1.0 + gate * (1.0 - sigmoid)), silu))
    grad_down = own_hidden(sum_parts(hidden_parts, upstream_parts))
    grad_down, down_w = after(grad_down, down_w)
    gate_up_grads = []
    for upstream_low, (gate_slope, silu) in zip(upstream_parts, gates):
        grad_hidden = dot_t(upstream_low, down_w)
        grads = [(grad_hidden * gate_slope).astype(low), (grad_hidden * silu).astype(low)]
        gate_up_grads.append(jnp.concatenate(grads, axis=1))
    grad_ffn = [dot_t(grads, gate_up_w).astype(low) for grads in gate_up_grads]
    grad_gate_up = by_layer(sum_parts(ffn_parts, gate_up_grads))
    grad_ffn = send_chips(sum_cores(grad_ffn[0], grad_ffn[1]))
    grad_down = scatter_rows(grad_down)
    grad_ffn, grad_gate_up = after(grad_ffn, grad_gate_up)
    grad_gate_up = scatter_rows(grad_gate_up)

    grad_middle, middle_low, grad_gain_ffn, mixed_grad = project_back(
        jnp.stack(owners), grad_ffn, middle, own_cotangent, gain_ffn.reshape(1, -1), out_blocks
    )
    mixed_grad, grad_down, *hidden_parts = after(mixed_grad, grad_down, *hidden_parts)
    block_parts = [dot(values, down_w).astype(low) for values in hidden_parts]
    block_half = sum_cores(block_parts[0], block_parts[1])
    mixed_grad, block_half = after(exchange(mixed_grad, CTX), block_half)
    block_sum = sum_chips(block_half)
    mixed_grad = mixed_grad.reshape(total, qw)
    qkv_grad, grad_gains = attend_back(
        total, heads, sources, places, qkv_raw, *tables, query, key, value, logs, mixed_grad
    )
    qkv_grads = halves(qkv_grad)
    grad_attn = [dot_t(grads, qkv_w).astype(low) for grads in qkv_grads]
    attn_half = sum_cores(grad_attn[0], grad_attn[1])
    grad_qkv = sum_parts(normed_parts, qkv_grads).reshape(n, m * strip, -1)
    block_sum, grad_qkv, late_low = after(block_sum, grad_qkv, middle_low)
    late_half = in_order(spread(late_low, "chip"), chip)
    grad_out = sum_parts(halves(mixed_rel), (late_half, swap(late_half, "core")))
    block_out = (middle + block_sum).astype(low).reshape(tokens.shape)
    grad_qkv = exchange(grad_qkv, CTX).reshape(n, m, strip, -1)

    def all_heads(grads):
        return grads.transpose(1, 2, 0, 3).reshape(m, strip, -1)

    def grad_of_kv(grads):
        grads = jnp.sum(grads.reshape(KVH, repeat, m, strip, HD).astype(high), axis=1)
        return all_heads(grads.astype(low))

    grad_late = [
        all_heads(grad_qkv[..., :qw]),
        grad_of_kv(grad_qkv[..., qw : qw + HD]),
        grad_of_kv(grad_qkv[..., qw + HD :]),
        grad_out.reshape(m, strip, width),
    ]
    grad_late = jnp.concatenate(grad_late, axis=2).reshape(m * strip, -1)
    grad_late, attn_half = after(grad_late, attn_half)
    grad_attn = sum_chips(attn_half)
    grad_late = scatter_rows(grad_late)

    grad_attn, grad_gate_up = after(grad_attn, grad_gate_up)
    grad_gate_up = exchange(grad_gate_up.reshape(n, strip, -1), CTX)
    factor_attn = rms_factor(own_features)
    scaled = gain_attn * grad_attn
    inner = mean_last(own_features * scaled)
    input_grad = grad_middle + factor_attn * scaled - own_features * factor_attn**3 * inner
    grad_gain_attn = jnp.sum(grad_attn * own_features * factor_attn, axis=0)
    input_grad = input_grad.reshape(tokens.shape)

    devices = n * m
    partial = jnp.concatenate(
        [
            grad_gain_attn.reshape(devices, -1),
            grad_gain_ffn.reshape(devices, -1),
            grad_gains[0].reshape(devices, -1),
            grad_gains[1].reshape(devices, -1),
        ],
        axis=1,
    )
    grad_gate_up, partial = after(grad_gate_up, partial)
    gains = exchange(partial, CTX + LAYER)
    gains = jnp.sum(gains, axis=0)
    grad_down = grad_down.astype(high)
    grad_gate, grad_up = arrange(grad_gate_up, piece)
    grad_late, gains = after(grad_late, gains)
    ends = [0, n * qw, n * qw + KVH * HD, n * qw + 2 * KVH * HD, grad_late.shape[1]]
    grad_query, grad_key, grad_value, grad_out = [
        grad_late[:, start:end].astype(high) for start, end in zip(ends, ends[1:])
    ]

    end = 2 * strip + HD // devices
    return (
        block_out,
        input_grad,
        gains[:strip],
        grad_query,
        grad_key,
        grad_value,
        gains[2 * strip : end],
        gains[end:],
        grad_out,
        gains[strip : 2 * strip],
        grad_gate,
        grad_up,
        grad_down,
    )


def solution(mesh):
    n, m = mesh.shape["ctx"], mesh.shape["fsdp"]
    mesh = Mesh(mesh.devices.reshape(n // 2, 2, m // 2, 2), CTX + LAYER)
    rows = P(LAYER, None)
    line = P(LAYER)
    blocks = P(LAYER, None, CTX, None, None)
    both = P(CTX + LAYER, None)
    both_line = P(CTX + LAYER)
    in_specs = (blocks, rows, blocks, line, rows, rows, rows, line, line, rows, line, rows, rows, rows)
    out_specs = (
        blocks,
        blocks,
        both_line,
        both,
        both,
        both,
        both_line,
        both_line,
        both,
        both_line,
        both,
        both,
        both,
    )
    return jax.shard_map(local, mesh=mesh, in_specs=in_specs, out_specs=out_specs, check_vma=False)
```

```python
import functools

import jax
import jax.numpy as jnp
from jax import lax
from jax.experimental import pallas as pl
from jax.experimental.pallas import tpu as pltpu
from jax.sharding import Mesh
from jax.sharding import PartitionSpec as P

H = 16
KVH = 8
HD = 128
BLOCK = 64
TILE = 256

epsilon = 1e-06
theta_base = 1000000.0
score_scale = HD ** (-0.5)
low = jnp.bfloat16
high = jnp.float32
vmem_bytes = 48 << 20


def dot(left, right):
    return jnp.dot(left, right, preferred_element_type=high)


def dot_t(left, right):
    return lax.dot_general(left, right, (((1,), (1,)), ((), ())), preferred_element_type=high)


def t_dot(left, right):
    return lax.dot_general(left, right, (((0,), (0,)), ((), ())), preferred_element_type=high)


def mean_last(values):
    return jnp.mean(values, axis=-1, keepdims=True)


def rms_factor(values):
    return lax.rsqrt(mean_last(values * values) + epsilon)


def head_cols(head):
    return slice(head * HD, (head + 1) * HD)


def visible_tile(segc_ref, segr_ref, first, keys):
    rows = lax.broadcasted_iota(jnp.int32, (TILE, keys), 0) + first
    cols = lax.broadcasted_iota(jnp.int32, (TILE, keys), 1)
    same = segc_ref[first : first + TILE, :] == segr_ref[:, :keys]
    return same & (cols <= rows)


def attend_kernel(
    sources_ref,
    places_ref,
    raw_ref,
    cos_ref,
    sin_ref,
    qg_ref,
    kg_ref,
    segc_ref,
    segr_ref,
    rel_ref,
    abs_ref,
    q_ref,
    k_ref,
    v_ref,
    log_ref,
):
    total = q_ref.shape[0]
    heads = q_ref.shape[1] // HD
    blocks = total // BLOCK

    def prepare(index, carry):
        source = pl.multiple_of(sources_ref[index] * BLOCK, BLOCK)
        target = pl.multiple_of(index * BLOCK, BLOCK)
        raw = raw_ref[pl.ds(source, BLOCK), :]
        cosine = cos_ref[pl.ds(target, BLOCK), :]
        sine = sin_ref[pl.ds(target, BLOCK), :]
        for head in range(heads + 1):
            values = raw[:, head_cols(head)]
            gain = qg_ref[...] if head < heads else kg_ref[...]
            normed = values * rms_factor(values) * gain
            turned = (normed * cosine + pltpu.roll(normed, HD // 2, 1) * sine).astype(low)
            if head < heads:
                q_ref[pl.ds(target, BLOCK), head_cols(head)] = turned
            else:
                k_ref[pl.ds(target, BLOCK), :] = turned
        v_ref[pl.ds(target, BLOCK), :] = raw[:, head_cols(heads + 1)].astype(low)
        return carry

    lax.fori_loop(0, blocks, prepare, 0)
    for tile in range(total // TILE):
        first = tile * TILE
        keys = first + TILE
        visible = visible_tile(segc_ref, segr_ref, first, keys)
        for head in range(heads):
            scores = dot_t(q_ref[first : first + TILE, head_cols(head)], k_ref[:keys, :])
            scores = jnp.where(visible, scores * score_scale, -jnp.inf)
            peak = jnp.max(scores, axis=-1, keepdims=True)
            powers = jnp.exp(scores - peak)
            sums = jnp.sum(powers, axis=-1, keepdims=True)
            probs = (powers / sums).astype(low)
            mixed = dot(probs, v_ref[:keys, :]).astype(low)
            log_ref[first : first + TILE, head : head + 1] = peak + jnp.log(sums)
            for part in range(TILE // BLOCK):
                index = first // BLOCK + part
                piece = mixed[part * BLOCK : (part + 1) * BLOCK, :]
                target = pl.multiple_of(sources_ref[index] * BLOCK, BLOCK)
                rel_ref[pl.ds(target, BLOCK), head_cols(head)] = piece
                target = pl.multiple_of(places_ref[index] * BLOCK, BLOCK)
                abs_ref[pl.ds(target, BLOCK), head_cols(head)] = piece


def attend_back_kernel(
    sources_ref,
    places_ref,
    raw_ref,
    cos_ref,
    sin_ref,
    qg_ref,
    kg_ref,
    segc_ref,
    segr_ref,
    q_ref,
    k_ref,
    v_ref,
    log_ref,
    up_ref,
    out_ref,
    gains_ref,
    dq_ref,
    dk_ref,
    dv_ref,
):
    total = q_ref.shape[0]
    heads = q_ref.shape[1] // HD
    blocks = total // BLOCK
    dk_ref[...] = jnp.zeros_like(dk_ref)
    dv_ref[...] = jnp.zeros_like(dv_ref)
    for tile in range(total // TILE):
        first = tile * TILE
        keys = first + TILE
        visible = visible_tile(segc_ref, segr_ref, first, keys)
        for head in range(heads):
            pieces = []
            for part in range(TILE // BLOCK):
                source = pl.multiple_of(places_ref[first // BLOCK + part] * BLOCK, BLOCK)
                pieces.append(up_ref[pl.ds(source, BLOCK), head_cols(head)])
            upstream = jnp.concatenate(pieces, axis=0)
            query = q_ref[first : first + TILE, head_cols(head)]
            key = k_ref[:keys, :]
            scores = dot_t(query, key) * score_scale
            shifted = scores - log_ref[first : first + TILE, head : head + 1]
            probs = jnp.exp(jnp.where(visible, shifted, -jnp.inf))
            dprobs = dot_t(upstream, v_ref[:keys, :])
            inner = jnp.sum(probs * dprobs, axis=-1, keepdims=True)
            dscores = (probs * (dprobs - inner)).astype(low)
            dq_ref[first : first + TILE, head_cols(head)] = dot(dscores, key) * score_scale
            dk_ref[:keys, :] += t_dot(dscores, query) * score_scale
            dv_ref[:keys, :] += t_dot(probs.astype(low), upstream)

    def finish(index, carry):
        target = pl.multiple_of(sources_ref[index] * BLOCK, BLOCK)
        source = pl.multiple_of(index * BLOCK, BLOCK)
        raw = raw_ref[pl.ds(target, BLOCK), :]
        cosine = cos_ref[pl.ds(source, BLOCK), :]
        sine = sin_ref[pl.ds(source, BLOCK), :]
        gains = list(carry)
        for head in range(heads + 1):
            values = raw[:, head_cols(head)]
            if head < heads:
                upstream, gain, slot = dq_ref[pl.ds(source, BLOCK), head_cols(head)], qg_ref[...], 0
            else:
                upstream, gain, slot = dk_ref[pl.ds(source, BLOCK), :], kg_ref[...], 1
            upstream = upstream * cosine - pltpu.roll(upstream, HD // 2, 1) * sine
            factor = rms_factor(values)
            gains[slot] = gains[slot] + jnp.sum(upstream * values * factor, axis=0, keepdims=True)
            scaled = gain * upstream
            inner = mean_last(values * scaled)
            back = factor * scaled - values * (factor * factor * factor) * inner
            out_ref[pl.ds(target, BLOCK), head_cols(head)] = back.astype(low)
        out_ref[pl.ds(target, BLOCK), head_cols(heads + 1)] = dv_ref[pl.ds(source, BLOCK), :].astype(low)
        return tuple(gains)

    zero = jnp.zeros((1, HD), high)
    query_gain, key_gain = lax.fori_loop(0, blocks, finish, (zero, zero))
    gains_ref[0:1, :] = query_gain
    gains_ref[1:2, :] = key_gain


def in_memory(kinds):
    return [pl.BlockSpec(memory_space=kind) for kind in kinds]


def attend(total, heads, *operands):
    shapes = (
        jax.ShapeDtypeStruct((total, heads * HD), low),
        jax.ShapeDtypeStruct((total, heads * HD), low),
        jax.ShapeDtypeStruct((total, heads * HD), low),
        jax.ShapeDtypeStruct((total, HD), low),
        jax.ShapeDtypeStruct((total, HD), low),
        jax.ShapeDtypeStruct((total, HD), high),
    )
    return pl.pallas_call(
        attend_kernel,
        out_shape=shapes,
        in_specs=in_memory([pltpu.SMEM] * 2 + [pltpu.VMEM] * (len(operands) - 2)),
        out_specs=in_memory([pltpu.VMEM] * len(shapes)),
        compiler_params=pltpu.CompilerParams(vmem_limit_bytes=vmem_bytes),
        name="attend",
    )(*operands)


def attend_back(total, heads, *operands):
    shapes = (
        jax.ShapeDtypeStruct((total, (heads + 2) * HD), low),
        jax.ShapeDtypeStruct((2, HD), high),
    )
    return pl.pallas_call(
        attend_back_kernel,
        out_shape=shapes,
        in_specs=in_memory([pltpu.SMEM] * 2 + [pltpu.VMEM] * (len(operands) - 2)),
        out_specs=in_memory([pltpu.VMEM] * len(shapes)),
        scratch_shapes=[
            pltpu.VMEM((total, heads * HD), high),
            pltpu.VMEM((total, HD), high),
            pltpu.VMEM((total, HD), high),
        ],
        compiler_params=pltpu.CompilerParams(vmem_limit_bytes=vmem_bytes),
        name="attend_back",
    )(*operands)


def project_back_kernel(chips, *refs):
    owners_ref, sums_ref, middle_ref, up_ref, gain_ref = refs[:5]
    (grad_ref, low_ref, gain_grad_ref, out_ref, weights_ref, sems) = refs[-6:]
    blocks = refs[5:-6]
    copies = [
        pltpu.make_async_copy(block, weights_ref.at[i], sems.at[i]) for i, block in enumerate(blocks)
    ]
    for copy in copies:
        copy.start()
    upstream = sums_ref[0].astype(high)
    for chip in range(1, chips):
        upstream = upstream + sums_ref[chip].astype(high)
    values = middle_ref[...]
    factor = rms_factor(values)
    gain_grad_ref[...] = jnp.sum(upstream * values * factor, axis=0, keepdims=True)
    scaled = gain_ref[...] * upstream
    inner = mean_last(values * scaled)
    back = factor * scaled - values * (factor * factor * factor) * inner
    grad = up_ref[...].astype(high) + back
    grad_ref[...] = grad
    low_ref[...] = grad.astype(low)
    cols = weights_ref.shape[2]
    total = 0.0
    for i, copy in enumerate(copies):
        start = pl.multiple_of(owners_ref[i] * cols, cols)
        copy.wait()
        total = total + dot_t(low_ref[:, pl.ds(start, cols)], weights_ref[i])
    total = total.astype(low)
    width = out_ref.shape[2]
    for i in range(out_ref.shape[0]):
        out_ref[i] = total[:, i * width : (i + 1) * width]


def project_back(owners, sums, middle, upstream, gain, blocks):
    rows, width = middle.shape
    count = len(blocks)
    depth, cols = blocks[0].shape
    shapes = (
        jax.ShapeDtypeStruct((rows, width), high),
        jax.ShapeDtypeStruct((rows, width), low),
        jax.ShapeDtypeStruct((1, width), high),
        jax.ShapeDtypeStruct((count, rows, depth // count), low),
    )
    return pl.pallas_call(
        functools.partial(project_back_kernel, sums.shape[0]),
        out_shape=shapes,
        in_specs=in_memory([pltpu.SMEM] + [pltpu.VMEM] * 4 + [pl.ANY] * count),
        out_specs=in_memory([pltpu.VMEM] * len(shapes)),
        scratch_shapes=[pltpu.VMEM((count, depth, cols), low), pltpu.SemaphoreType.DMA((count,))],
        compiler_params=pltpu.CompilerParams(vmem_limit_bytes=vmem_bytes),
        name="project_back",
    )(owners, sums, middle, upstream, gain, *blocks)


def arrange_kernel(piece, in_ref, gate_ref, up_ref):
    count, _, width = in_ref.shape
    hidden = width // 2
    for half, out_ref in enumerate((gate_ref, up_ref)):
        for layer in range(hidden // piece):
            start = half * hidden + layer * piece
            parts = [in_ref[i, :, start : start + piece].astype(high) for i in range(count)]
            target = layer * count * piece
            out_ref[:, target : target + count * piece] = jnp.concatenate(parts, axis=1)


def arrange(grads, piece):
    count, rows, width = grads.shape
    shape = jax.ShapeDtypeStruct((rows, count * width // 2), high)
    return pl.pallas_call(
        functools.partial(arrange_kernel, piece),
        out_shape=(shape, shape),
        in_specs=in_memory([pltpu.VMEM]),
        out_specs=in_memory([pltpu.VMEM] * 2),
        compiler_params=pltpu.CompilerParams(vmem_limit_bytes=vmem_bytes),
        name="arrange",
    )(grads)


def widen_kernel(in_ref, *out_refs):
    start = 0
    for out_ref in out_refs:
        end = start + out_ref.shape[1]
        out_ref[...] = in_ref[:, start:end].astype(high)
        start = end


def widen(values, widths):
    rows = values.shape[0]
    return pl.pallas_call(
        widen_kernel,
        out_shape=tuple(jax.ShapeDtypeStruct((rows, width), high) for width in widths),
        in_specs=in_memory([pltpu.VMEM]),
        out_specs=in_memory([pltpu.VMEM] * len(widths)),
        compiler_params=pltpu.CompilerParams(vmem_limit_bytes=vmem_bytes),
        name="widen",
    )(values)


CTX = ("chip", "core")
LAYER = ("hi", "lo")


def swap(values, axis, mask=1):
    size = lax.axis_size(axis)
    return lax.ppermute(values, axis, [(i, i ^ mask) for i in range(size)])


def exchange(values, axis):
    return lax.all_to_all(values, axis, 0, 0, tiled=True)


def gather(values):
    copies = jnp.broadcast_to(values[None], (lax.axis_size("chip"),) + values.shape)
    half = exchange(copies, "chip").reshape(-1, values.shape[-1])
    return half, swap(half, "core")


def sum_cores(keep, give):
    return (keep.astype(high) + swap(give, "core").astype(high)).astype(low)


def sum_chips(half):
    size = lax.axis_size("chip")
    chip = lax.axis_index("chip")
    rows = half.shape[0] // size
    total = rows_of(half, chip, rows).astype(high)
    for mask in range(1, size):
        total = total + swap(rows_of(half, chip ^ mask, rows), "chip", mask).astype(high)
    return total


def send_chips(half):
    size = lax.axis_size("chip")
    return exchange(half.reshape(size, half.shape[0] // size, -1), "chip")


def spread(values, axis):
    return [values] + [swap(values, axis, mask) for mask in range(1, lax.axis_size(axis))]


def in_order(pieces, index):
    rows = pieces[0].shape[0]
    whole = jnp.zeros((len(pieces) * rows,) + pieces[0].shape[1:], pieces[0].dtype)
    for mask, piece in enumerate(pieces):
        whole = lax.dynamic_update_slice_in_dim(whole, piece, (index ^ mask) * rows, axis=0)
    return whole


def halves(values):
    middle = values.shape[0] // 2
    return values[:middle], values[middle:]


def after(values, *others):
    return lax.optimization_barrier((values,) + others)


def columns_of(values, index, width):
    return lax.dynamic_slice_in_dim(values, index * width, width, axis=1)


def rows_of(values, index, height):
    return lax.dynamic_slice_in_dim(values, index * height, height, axis=0)


def sum_parts(lefts, rights):
    return sum(t_dot(left, right) for left, right in zip(lefts, rights)).astype(low)


def gather_rows(values):
    return lax.all_gather(values, LAYER, axis=0, tiled=True)


def scatter_rows(values):
    return lax.psum_scatter(values, LAYER, scatter_dimension=0, tiled=True)


def local(
    tokens,
    segment_ids,
    cotangent,
    norm_attn,
    w_query,
    w_key,
    w_value,
    q_gain,
    k_gain,
    w_out,
    norm_ffn,
    w_gate,
    w_up,
    w_down,
):
    n = lax.axis_size(CTX)
    m = lax.axis_size(LAYER)
    me = lax.axis_index(CTX)
    chip = lax.axis_index("chip")
    core = lax.axis_index("core")
    chips = n // 2
    width = tokens.shape[-1]
    own = 2 * BLOCK
    total = n * own
    heads = H // n
    repeat = n // KVH
    qw = heads * HD
    hidden = w_gate.shape[1] // n
    piece = hidden // m
    strip = width // (n * m)
    assert tokens.shape[0] == 1 and heads * n == H and repeat * KVH == n

    own_tokens = tokens.reshape(own, width)
    own_cotangent = cotangent.reshape(own, width)
    out_cols = width // n
    attn_w = jnp.concatenate(
        [
            columns_of(w_out, me, out_cols),
            columns_of(w_query, me, qw),
            columns_of(w_key, me // repeat, HD),
            columns_of(w_value, me // repeat, HD),
        ],
        axis=1,
    )
    own_tokens, attn_w = after(own_tokens, attn_w)
    layer = lax.axis_index(LAYER)
    attn_w = gather_rows(attn_w)

    small = jnp.concatenate([norm_attn, norm_ffn, q_gain, k_gain]).reshape(1, -1)
    small = in_order(spread(small, LAYER), layer).astype(high)
    part, gain_part = norm_attn.shape[0], q_gain.shape[0]
    gain_attn = small[:, :part].reshape(-1)
    gain_ffn = small[:, part : 2 * part].reshape(-1)
    query_gain = small[:, 2 * part : 2 * part + gain_part].reshape(1, HD)
    key_gain = small[:, 2 * part + gain_part :].reshape(1, HD)

    def hidden_columns(weights):
        starts = [(i * n + me) * piece for i in range(m)]
        return [lax.dynamic_slice_in_dim(weights, start, piece, axis=1) for start in starts]

    gate_up_w = jnp.concatenate(hidden_columns(w_gate) + hidden_columns(w_up), axis=1)
    down_w = rows_of(w_down, me, piece)
    token_half = exchange(jnp.broadcast_to(own_tokens, (chips, own, width)), "chip").reshape(-1, width)
    token_half, own_cotangent, gate_up_w, down_w = after(
        token_half, own_cotangent, gate_up_w, down_w
    )
    upstream_half = in_order(spread(own_cotangent, "chip"), chip)
    upstream_half, attn_w = after(upstream_half, attn_w)
    out_w, qkv_w = attn_w[:, :out_cols], attn_w[:, out_cols:]
    token_parts = (token_half, swap(token_half, "core"))
    gate_up_w = gather_rows(gate_up_w)
    down_w = gather_rows(down_w)

    out_half = spread(out_w, "chip")
    owners = [me ^ (2 * mask) for mask in range(chips)]
    owners = owners + [owner ^ 1 for owner in owners]

    def by_layer(grads):
        return grads.reshape(n, m, strip, -1).transpose(1, 0, 2, 3).reshape(width, -1)

    def own_hidden(grads):
        whole = jnp.zeros_like(grads)
        for step in range(m):
            targets = [(i, ((step + i) % m * n + i) // m) for i in range(n)]
            rows = lax.ppermute(rows_of(grads, (step + me) % m, piece), CTX, targets)
            place = (me // (n // m) - step) % m * piece
            whole = lax.dynamic_update_slice_in_dim(whole, rows, place, axis=0)
        return whole

    natural = jnp.arange(2 * n, dtype=jnp.int32)
    side = (natural >= n).astype(jnp.int32)
    owner = jnp.where(side == 0, natural, 2 * n - 1 - natural)
    sources = 2 * (((owner & 1) ^ core) * chips + (owner >> 1)) + side
    places = 2 * owner + side

    segments = segment_ids.reshape(total)
    starts = jnp.sum((segments[None, :] < segments[:, None]).astype(jnp.int32), axis=1)
    place = jnp.arange(total, dtype=jnp.int32) - starts
    frequency = theta_base ** (-(jnp.arange(HD // 2, dtype=high) * 2.0) / HD)
    angles = place.astype(high)[:, None] * frequency
    cosine = jnp.cos(angles)
    sine = jnp.sin(angles)
    cosine = jnp.concatenate([cosine, cosine], axis=1)
    sine = jnp.concatenate([-sine, sine], axis=1)
    segment_column = segments.reshape(total, 1)
    segment_row = segments.reshape(1, total)

    normed_parts = []
    for tokens_part in token_parts:
        features = tokens_part.astype(high)
        normed_parts.append((features * rms_factor(features) * gain_attn).astype(low))
    qkv_raw = jnp.concatenate([dot(normed, qkv_w) for normed in normed_parts], axis=0)
    tables = (cosine, sine, query_gain, key_gain, segment_column, segment_row)
    mixed_rel, mixed_abs, query, key, value, logs = attend(
        total, heads, sources, places, qkv_raw, *tables
    )
    mixed = exchange(mixed_abs.reshape(n, own, qw), CTX)
    out_blocks = out_half + [swap(block, "core") for block in out_half]
    mixed = mixed.transpose(1, 0, 2).reshape(own, n * qw)
    own_features = own_tokens.astype(high)
    branch = jnp.zeros((own, width), high)
    for block_owner, block in zip(owners, out_blocks):
        branch = lax.dynamic_update_slice_in_dim(branch, dot(mixed, block), block_owner * out_cols, axis=1)
    middle = own_features + branch
    factor_ffn = rms_factor(middle)
    ffn_own = (middle * factor_ffn * gain_ffn).astype(low)
    ffn_parts = gather(ffn_own)
    upstream_parts = (upstream_half, swap(upstream_half, "core"))

    hidden_parts, gates = [], []
    for ffn_low in ffn_parts:
        gate_up = dot(ffn_low, gate_up_w)
        gate, up = gate_up[:, :hidden], gate_up[:, hidden:]
        sigmoid = jax.nn.sigmoid(gate)
        silu = gate * sigmoid
        hidden_parts.append((silu * up).astype(low))
        gates.append((up * sigmoid * (1.0 + gate * (1.0 - sigmoid)), silu))
    grad_down = own_hidden(sum_parts(hidden_parts, upstream_parts))
    grad_down, down_w = after(grad_down, down_w)
    gate_up_grads = []
    for upstream_low, (gate_slope, silu) in zip(upstream_parts, gates):
        grad_hidden = dot_t(upstream_low, down_w)
        grads = [(grad_hidden * gate_slope).astype(low), (grad_hidden * silu).astype(low)]
        gate_up_grads.append(jnp.concatenate(grads, axis=1))
    grad_ffn = [dot_t(grads, gate_up_w).astype(low) for grads in gate_up_grads]
    grad_gate_up = by_layer(sum_parts(ffn_parts, gate_up_grads))
    grad_ffn = send_chips(sum_cores(grad_ffn[0], grad_ffn[1]))
    grad_down = scatter_rows(grad_down)
    grad_ffn, grad_gate_up = after(grad_ffn, grad_gate_up)
    grad_gate_up = scatter_rows(grad_gate_up)

    grad_middle, middle_low, grad_gain_ffn, mixed_grad = project_back(
        jnp.stack(owners), grad_ffn, middle, own_cotangent, gain_ffn.reshape(1, -1), out_blocks
    )
    mixed_grad, grad_down, *hidden_parts = after(mixed_grad, grad_down, *hidden_parts)
    block_parts = [dot(values, down_w).astype(low) for values in hidden_parts]
    block_half = sum_cores(block_parts[0], block_parts[1])
    mixed_grad, block_half = after(exchange(mixed_grad, CTX), block_half)
    block_sum = sum_chips(block_half)
    mixed_grad = mixed_grad.reshape(total, qw)
    qkv_grad, grad_gains = attend_back(
        total, heads, sources, places, qkv_raw, *tables, query, key, value, logs, mixed_grad
    )
    qkv_grads = halves(qkv_grad)
    grad_attn = [dot_t(grads, qkv_w).astype(low) for grads in qkv_grads]
    attn_half = sum_cores(grad_attn[0], grad_attn[1])
    grad_qkv = sum_parts(normed_parts, qkv_grads).reshape(n, m * strip, -1)
    block_sum, grad_qkv, late_low = after(block_sum, grad_qkv, middle_low)
    late_half = in_order(spread(late_low, "chip"), chip)
    grad_out = sum_parts(halves(mixed_rel), (late_half, swap(late_half, "core")))
    block_out = (middle + block_sum).astype(low).reshape(tokens.shape)
    grad_qkv = exchange(grad_qkv, CTX).reshape(n, m, strip, -1)

    def all_heads(grads):
        return grads.transpose(1, 2, 0, 3).reshape(m, strip, -1)

    def grad_of_kv(grads):
        grads = jnp.sum(grads.reshape(KVH, repeat, m, strip, HD).astype(high), axis=1)
        return all_heads(grads.astype(low))

    grad_late = [
        all_heads(grad_qkv[..., :qw]),
        grad_of_kv(grad_qkv[..., qw : qw + HD]),
        grad_of_kv(grad_qkv[..., qw + HD :]),
        grad_out.reshape(m, strip, width),
    ]
    grad_late = jnp.concatenate(grad_late, axis=2).reshape(m * strip, -1)
    grad_late, attn_half = after(grad_late, attn_half)
    grad_attn = sum_chips(attn_half)
    grad_late = scatter_rows(grad_late)

    grad_attn, grad_gate_up = after(grad_attn, grad_gate_up)
    grad_gate_up = exchange(grad_gate_up.reshape(n, strip, -1), CTX)
    factor_attn = rms_factor(own_features)
    scaled = gain_attn * grad_attn
    inner = mean_last(own_features * scaled)
    input_grad = grad_middle + factor_attn * scaled - own_features * factor_attn**3 * inner
    grad_gain_attn = jnp.sum(grad_attn * own_features * factor_attn, axis=0)
    input_grad = input_grad.reshape(tokens.shape)

    devices = n * m
    partial = jnp.concatenate(
        [
            grad_gain_attn.reshape(devices, -1),
            grad_gain_ffn.reshape(devices, -1),
            grad_gains[0].reshape(devices, -1),
            grad_gains[1].reshape(devices, -1),
        ],
        axis=1,
    )
    grad_gate_up, partial = after(grad_gate_up, partial)
    gains = exchange(partial, CTX + LAYER)
    gains = jnp.sum(gains, axis=0)
    grad_down = grad_down.astype(high)
    grad_gate, grad_up = arrange(grad_gate_up, piece)
    end = 2 * strip + HD // devices
    gains = (gains[:strip], gains[strip : 2 * strip], gains[2 * strip : end], gains[end:])
    grad_late, *gains = after(grad_late, *gains)
    widths = (n * qw, KVH * HD, KVH * HD, width)
    grad_query, grad_key, grad_value, grad_out = widen(grad_late, widths)

    return (
        block_out,
        input_grad,
        gains[0],
        grad_query,
        grad_key,
        grad_value,
        gains[2],
        gains[3],
        grad_out,
        gains[1],
        grad_gate,
        grad_up,
        grad_down,
    )


def solution(mesh):
    n, m = mesh.shape["ctx"], mesh.shape["fsdp"]
    mesh = Mesh(mesh.devices.reshape(n // 2, 2, m // 2, 2), CTX + LAYER)
    rows = P(LAYER, None)
    line = P(LAYER)
    blocks = P(LAYER, None, CTX, None, None)
    both = P(CTX + LAYER, None)
    both_line = P(CTX + LAYER)
    in_specs = (blocks, rows, blocks, line, rows, rows, rows, line, line, rows, line, rows, rows, rows)
    out_specs = (
        blocks,
        blocks,
        both_line,
        both,
        both,
        both,
        both_line,
        both_line,
        both,
        both_line,
        both,
        both,
        both,
    )
    return jax.shard_map(local, mesh=mesh, in_specs=in_specs, out_specs=out_specs, check_vma=False)
```

```python
import functools

import jax
import jax.numpy as jnp
from jax import lax
from jax.experimental import pallas as pl
from jax.experimental.pallas import tpu as pltpu
from jax.sharding import Mesh
from jax.sharding import PartitionSpec as P

H = 16
KVH = 8
HD = 128
BLOCK = 64
TILE = 256
WIDEN_ROWS = 16

epsilon = 1e-06
theta_base = 1000000.0
score_scale = HD ** (-0.5)
low = jnp.bfloat16
high = jnp.float32
vmem_bytes = 48 << 20


def dot(left, right):
    return jnp.dot(left, right, preferred_element_type=high)


def dot_t(left, right):
    return lax.dot_general(left, right, (((1,), (1,)), ((), ())), preferred_element_type=high)


def t_dot(left, right):
    return lax.dot_general(left, right, (((0,), (0,)), ((), ())), preferred_element_type=high)


def mean_last(values):
    return jnp.mean(values, axis=-1, keepdims=True)


def rms_factor(values):
    return lax.rsqrt(mean_last(values * values) + epsilon)


def head_cols(head):
    return slice(head * HD, (head + 1) * HD)


def visible_tile(segc_ref, segr_ref, first, keys):
    rows = lax.broadcasted_iota(jnp.int32, (TILE, keys), 0) + first
    cols = lax.broadcasted_iota(jnp.int32, (TILE, keys), 1)
    same = segc_ref[first : first + TILE, :] == segr_ref[:, :keys]
    return same & (cols <= rows)


def attend_kernel(
    sources_ref,
    places_ref,
    raw_ref,
    cos_ref,
    sin_ref,
    qg_ref,
    kg_ref,
    segc_ref,
    segr_ref,
    rel_ref,
    abs_ref,
    q_ref,
    k_ref,
    v_ref,
    log_ref,
):
    total = q_ref.shape[0]
    heads = q_ref.shape[1] // HD
    blocks = total // BLOCK

    def prepare(index, carry):
        source = pl.multiple_of(sources_ref[index] * BLOCK, BLOCK)
        target = pl.multiple_of(index * BLOCK, BLOCK)
        raw = raw_ref[pl.ds(source, BLOCK), :]
        cosine = cos_ref[pl.ds(target, BLOCK), :]
        sine = sin_ref[pl.ds(target, BLOCK), :]
        for head in range(heads + 1):
            values = raw[:, head_cols(head)]
            gain = qg_ref[...] if head < heads else kg_ref[...]
            normed = values * rms_factor(values) * gain
            turned = (normed * cosine + pltpu.roll(normed, HD // 2, 1) * sine).astype(low)
            if head < heads:
                q_ref[pl.ds(target, BLOCK), head_cols(head)] = turned
            else:
                k_ref[pl.ds(target, BLOCK), :] = turned
        v_ref[pl.ds(target, BLOCK), :] = raw[:, head_cols(heads + 1)].astype(low)
        return carry

    lax.fori_loop(0, blocks, prepare, 0)
    for tile in range(total // TILE):
        first = tile * TILE
        keys = first + TILE
        visible = visible_tile(segc_ref, segr_ref, first, keys)
        for head in range(heads):
            scores = dot_t(q_ref[first : first + TILE, head_cols(head)], k_ref[:keys, :])
            scores = jnp.where(visible, scores * score_scale, -jnp.inf)
            peak = jnp.max(scores, axis=-1, keepdims=True)
            powers = jnp.exp(scores - peak)
            sums = jnp.sum(powers, axis=-1, keepdims=True)
            probs = (powers / sums).astype(low)
            mixed = dot(probs, v_ref[:keys, :]).astype(low)
            log_ref[first : first + TILE, head : head + 1] = peak + jnp.log(sums)
            for part in range(TILE // BLOCK):
                index = first // BLOCK + part
                piece = mixed[part * BLOCK : (part + 1) * BLOCK, :]
                target = pl.multiple_of(sources_ref[index] * BLOCK, BLOCK)
                rel_ref[pl.ds(target, BLOCK), head_cols(head)] = piece
                target = pl.multiple_of(places_ref[index] * BLOCK, BLOCK)
                abs_ref[pl.ds(target, BLOCK), head_cols(head)] = piece


def attend_back_kernel(
    sources_ref,
    places_ref,
    raw_ref,
    cos_ref,
    sin_ref,
    qg_ref,
    kg_ref,
    segc_ref,
    segr_ref,
    q_ref,
    k_ref,
    v_ref,
    log_ref,
    up_ref,
    out_ref,
    gains_ref,
    dq_ref,
    dk_ref,
    dv_ref,
):
    total = q_ref.shape[0]
    heads = q_ref.shape[1] // HD
    blocks = total // BLOCK
    dk_ref[...] = jnp.zeros_like(dk_ref)
    dv_ref[...] = jnp.zeros_like(dv_ref)
    for tile in range(total // TILE):
        first = tile * TILE
        keys = first + TILE
        visible = visible_tile(segc_ref, segr_ref, first, keys)
        for head in range(heads):
            pieces = []
            for part in range(TILE // BLOCK):
                source = pl.multiple_of(places_ref[first // BLOCK + part] * BLOCK, BLOCK)
                pieces.append(up_ref[pl.ds(source, BLOCK), head_cols(head)])
            upstream = jnp.concatenate(pieces, axis=0)
            query = q_ref[first : first + TILE, head_cols(head)]
            key = k_ref[:keys, :]
            scores = dot_t(query, key) * score_scale
            shifted = scores - log_ref[first : first + TILE, head : head + 1]
            probs = jnp.exp(jnp.where(visible, shifted, -jnp.inf))
            dprobs = dot_t(upstream, v_ref[:keys, :])
            inner = jnp.sum(probs * dprobs, axis=-1, keepdims=True)
            dscores = (probs * (dprobs - inner)).astype(low)
            dq_ref[first : first + TILE, head_cols(head)] = dot(dscores, key) * score_scale
            dk_ref[:keys, :] += t_dot(dscores, query) * score_scale
            dv_ref[:keys, :] += t_dot(probs.astype(low), upstream)

    def finish(index, carry):
        target = pl.multiple_of(sources_ref[index] * BLOCK, BLOCK)
        source = pl.multiple_of(index * BLOCK, BLOCK)
        raw = raw_ref[pl.ds(target, BLOCK), :]
        cosine = cos_ref[pl.ds(source, BLOCK), :]
        sine = sin_ref[pl.ds(source, BLOCK), :]
        gains = list(carry)
        for head in range(heads + 1):
            values = raw[:, head_cols(head)]
            if head < heads:
                upstream, gain, slot = dq_ref[pl.ds(source, BLOCK), head_cols(head)], qg_ref[...], 0
            else:
                upstream, gain, slot = dk_ref[pl.ds(source, BLOCK), :], kg_ref[...], 1
            upstream = upstream * cosine - pltpu.roll(upstream, HD // 2, 1) * sine
            factor = rms_factor(values)
            gains[slot] = gains[slot] + jnp.sum(upstream * values * factor, axis=0, keepdims=True)
            scaled = gain * upstream
            inner = mean_last(values * scaled)
            back = factor * scaled - values * (factor * factor * factor) * inner
            out_ref[pl.ds(target, BLOCK), head_cols(head)] = back.astype(low)
        out_ref[pl.ds(target, BLOCK), head_cols(heads + 1)] = dv_ref[pl.ds(source, BLOCK), :].astype(low)
        return tuple(gains)

    zero = jnp.zeros((1, HD), high)
    query_gain, key_gain = lax.fori_loop(0, blocks, finish, (zero, zero))
    gains_ref[0:1, :] = query_gain
    gains_ref[1:2, :] = key_gain


def in_memory(kinds):
    return [pl.BlockSpec(memory_space=kind) for kind in kinds]


def attend(total, heads, *operands):
    shapes = (
        jax.ShapeDtypeStruct((total, heads * HD), low),
        jax.ShapeDtypeStruct((total, heads * HD), low),
        jax.ShapeDtypeStruct((total, heads * HD), low),
        jax.ShapeDtypeStruct((total, HD), low),
        jax.ShapeDtypeStruct((total, HD), low),
        jax.ShapeDtypeStruct((total, HD), high),
    )
    return pl.pallas_call(
        attend_kernel,
        out_shape=shapes,
        in_specs=in_memory([pltpu.SMEM] * 2 + [pltpu.VMEM] * (len(operands) - 2)),
        out_specs=in_memory([pltpu.VMEM] * len(shapes)),
        compiler_params=pltpu.CompilerParams(vmem_limit_bytes=vmem_bytes),
        name="attend",
    )(*operands)


def attend_back(total, heads, *operands):
    shapes = (
        jax.ShapeDtypeStruct((total, (heads + 2) * HD), low),
        jax.ShapeDtypeStruct((2, HD), high),
    )
    return pl.pallas_call(
        attend_back_kernel,
        out_shape=shapes,
        in_specs=in_memory([pltpu.SMEM] * 2 + [pltpu.VMEM] * (len(operands) - 2)),
        out_specs=in_memory([pltpu.VMEM] * len(shapes)),
        scratch_shapes=[
            pltpu.VMEM((total, heads * HD), high),
            pltpu.VMEM((total, HD), high),
            pltpu.VMEM((total, HD), high),
        ],
        compiler_params=pltpu.CompilerParams(vmem_limit_bytes=vmem_bytes),
        name="attend_back",
    )(*operands)


def project_back_kernel(chips, *refs):
    owners_ref, sums_ref, middle_ref, up_ref, gain_ref = refs[:5]
    (grad_ref, low_ref, gain_grad_ref, out_ref, weights_ref, sems) = refs[-6:]
    blocks = refs[5:-6]
    copies = [
        pltpu.make_async_copy(block, weights_ref.at[i], sems.at[i]) for i, block in enumerate(blocks)
    ]
    for copy in copies:
        copy.start()
    upstream = sums_ref[0].astype(high)
    for chip in range(1, chips):
        upstream = upstream + sums_ref[chip].astype(high)
    values = middle_ref[...]
    factor = rms_factor(values)
    gain_grad_ref[...] = jnp.sum(upstream * values * factor, axis=0, keepdims=True)
    scaled = gain_ref[...] * upstream
    inner = mean_last(values * scaled)
    back = factor * scaled - values * (factor * factor * factor) * inner
    grad = up_ref[...].astype(high) + back
    grad_ref[...] = grad
    low_ref[...] = grad.astype(low)
    cols = weights_ref.shape[2]
    total = 0.0
    for i, copy in enumerate(copies):
        start = pl.multiple_of(owners_ref[i] * cols, cols)
        copy.wait()
        total = total + dot_t(low_ref[:, pl.ds(start, cols)], weights_ref[i])
    total = total.astype(low)
    width = out_ref.shape[2]
    for i in range(out_ref.shape[0]):
        out_ref[i] = total[:, i * width : (i + 1) * width]


def project_back(owners, sums, middle, upstream, gain, blocks):
    rows, width = middle.shape
    count = len(blocks)
    depth, cols = blocks[0].shape
    shapes = (
        jax.ShapeDtypeStruct((rows, width), high),
        jax.ShapeDtypeStruct((rows, width), low),
        jax.ShapeDtypeStruct((1, width), high),
        jax.ShapeDtypeStruct((count, rows, depth // count), low),
    )
    return pl.pallas_call(
        functools.partial(project_back_kernel, sums.shape[0]),
        out_shape=shapes,
        in_specs=in_memory([pltpu.SMEM] + [pltpu.VMEM] * 4 + [pl.ANY] * count),
        out_specs=in_memory([pltpu.VMEM] * len(shapes)),
        scratch_shapes=[pltpu.VMEM((count, depth, cols), low), pltpu.SemaphoreType.DMA((count,))],
        compiler_params=pltpu.CompilerParams(vmem_limit_bytes=vmem_bytes),
        name="project_back",
    )(owners, sums, middle, upstream, gain, *blocks)


def arrange_kernel(piece, in_ref, gate_ref, up_ref):
    count, _, width = in_ref.shape
    hidden = width // 2
    for half, out_ref in enumerate((gate_ref, up_ref)):
        for layer in range(hidden // piece):
            start = half * hidden + layer * piece
            parts = [in_ref[i, :, start : start + piece].astype(high) for i in range(count)]
            target = layer * count * piece
            out_ref[:, target : target + count * piece] = jnp.concatenate(parts, axis=1)


def arrange(grads, piece):
    count, rows, width = grads.shape
    shape = jax.ShapeDtypeStruct((rows, count * width // 2), high)
    return pl.pallas_call(
        functools.partial(arrange_kernel, piece),
        out_shape=(shape, shape),
        in_specs=in_memory([pltpu.VMEM]),
        out_specs=in_memory([pltpu.VMEM] * 2),
        compiler_params=pltpu.CompilerParams(vmem_limit_bytes=vmem_bytes),
        name="arrange",
    )(grads)


def widen_kernel(in_ref, *out_refs):
    start = 0
    for out_ref in out_refs:
        end = start + out_ref.shape[1]
        out_ref[...] = in_ref[:, start:end].astype(high)
        start = end


def widen(values, widths):
    rows = values.shape[0]
    return pl.pallas_call(
        widen_kernel,
        out_shape=tuple(jax.ShapeDtypeStruct((rows, width), high) for width in widths),
        grid=(rows // WIDEN_ROWS,),
        in_specs=[pl.BlockSpec((WIDEN_ROWS, sum(widths)), lambda i: (i, 0))],
        out_specs=[pl.BlockSpec((WIDEN_ROWS, width), lambda i: (i, 0)) for width in widths],
        compiler_params=pltpu.CompilerParams(vmem_limit_bytes=vmem_bytes),
        name="widen",
    )(values)


CTX = ("chip", "core")
LAYER = ("hi", "lo")


def swap(values, axis, mask=1):
    size = lax.axis_size(axis)
    return lax.ppermute(values, axis, [(i, i ^ mask) for i in range(size)])


def exchange(values, axis):
    return lax.all_to_all(values, axis, 0, 0, tiled=True)


def gather(values):
    copies = jnp.broadcast_to(values[None], (lax.axis_size("chip"),) + values.shape)
    half = exchange(copies, "chip").reshape(-1, values.shape[-1])
    return half, swap(half, "core")


def sum_cores(keep, give):
    return (keep.astype(high) + swap(give, "core").astype(high)).astype(low)


def sum_chips(half):
    size = lax.axis_size("chip")
    chip = lax.axis_index("chip")
    rows = half.shape[0] // size
    total = rows_of(half, chip, rows).astype(high)
    for mask in range(1, size):
        total = total + swap(rows_of(half, chip ^ mask, rows), "chip", mask).astype(high)
    return total


def send_chips(half):
    size = lax.axis_size("chip")
    return exchange(half.reshape(size, half.shape[0] // size, -1), "chip")


def spread(values, axis):
    return [values] + [swap(values, axis, mask) for mask in range(1, lax.axis_size(axis))]


def in_order(pieces, index):
    rows = pieces[0].shape[0]
    whole = jnp.zeros((len(pieces) * rows,) + pieces[0].shape[1:], pieces[0].dtype)
    for mask, piece in enumerate(pieces):
        whole = lax.dynamic_update_slice_in_dim(whole, piece, (index ^ mask) * rows, axis=0)
    return whole


def halves(values):
    middle = values.shape[0] // 2
    return values[:middle], values[middle:]


def after(values, *others):
    return lax.optimization_barrier((values,) + others)


def columns_of(values, index, width):
    return lax.dynamic_slice_in_dim(values, index * width, width, axis=1)


def rows_of(values, index, height):
    return lax.dynamic_slice_in_dim(values, index * height, height, axis=0)


def sum_parts(lefts, rights):
    return sum(t_dot(left, right) for left, right in zip(lefts, rights)).astype(low)


def gather_rows(values):
    return lax.all_gather(values, LAYER, axis=0, tiled=True)


def scatter_rows(values):
    return lax.psum_scatter(values, LAYER, scatter_dimension=0, tiled=True)


def local(
    tokens,
    segment_ids,
    cotangent,
    norm_attn,
    w_query,
    w_key,
    w_value,
    q_gain,
    k_gain,
    w_out,
    norm_ffn,
    w_gate,
    w_up,
    w_down,
):
    n = lax.axis_size(CTX)
    m = lax.axis_size(LAYER)
    me = lax.axis_index(CTX)
    chip = lax.axis_index("chip")
    core = lax.axis_index("core")
    chips = n // 2
    width = tokens.shape[-1]
    own = 2 * BLOCK
    total = n * own
    heads = H // n
    repeat = n // KVH
    qw = heads * HD
    hidden = w_gate.shape[1] // n
    piece = hidden // m
    strip = width // (n * m)
    assert tokens.shape[0] == 1 and heads * n == H and repeat * KVH == n

    own_tokens = tokens.reshape(own, width)
    own_cotangent = cotangent.reshape(own, width)
    out_cols = width // n
    attn_w = jnp.concatenate(
        [
            columns_of(w_out, me, out_cols),
            columns_of(w_query, me, qw),
            columns_of(w_key, me // repeat, HD),
            columns_of(w_value, me // repeat, HD),
        ],
        axis=1,
    )
    own_tokens, attn_w = after(own_tokens, attn_w)
    layer = lax.axis_index(LAYER)
    attn_w = gather_rows(attn_w)

    small = jnp.concatenate([norm_attn, norm_ffn, q_gain, k_gain]).reshape(1, -1)
    small = in_order(spread(small, LAYER), layer).astype(high)
    part, gain_part = norm_attn.shape[0], q_gain.shape[0]
    gain_attn = small[:, :part].reshape(-1)
    gain_ffn = small[:, part : 2 * part].reshape(-1)
    query_gain = small[:, 2 * part : 2 * part + gain_part].reshape(1, HD)
    key_gain = small[:, 2 * part + gain_part :].reshape(1, HD)

    def hidden_columns(weights):
        starts = [(i * n + me) * piece for i in range(m)]
        return [lax.dynamic_slice_in_dim(weights, start, piece, axis=1) for start in starts]

    gate_up_w = jnp.concatenate(hidden_columns(w_gate) + hidden_columns(w_up), axis=1)
    down_w = rows_of(w_down, me, piece)
    token_half = exchange(jnp.broadcast_to(own_tokens, (chips, own, width)), "chip").reshape(-1, width)
    token_half, own_cotangent, gate_up_w, down_w = after(
        token_half, own_cotangent, gate_up_w, down_w
    )
    upstream_half = in_order(spread(own_cotangent, "chip"), chip)
    upstream_half, attn_w = after(upstream_half, attn_w)
    out_w, qkv_w = attn_w[:, :out_cols], attn_w[:, out_cols:]
    token_parts = (token_half, swap(token_half, "core"))
    gate_up_w = gather_rows(gate_up_w)
    down_w = gather_rows(down_w)

    out_half = spread(out_w, "chip")
    owners = [me ^ (2 * mask) for mask in range(chips)]
    owners = owners + [owner ^ 1 for owner in owners]

    def by_layer(grads):
        return grads.reshape(n, m, strip, -1).transpose(1, 0, 2, 3).reshape(width, -1)

    def own_hidden(grads):
        whole = jnp.zeros_like(grads)
        for step in range(m):
            targets = [(i, ((step + i) % m * n + i) // m) for i in range(n)]
            rows = lax.ppermute(rows_of(grads, (step + me) % m, piece), CTX, targets)
            place = (me // (n // m) - step) % m * piece
            whole = lax.dynamic_update_slice_in_dim(whole, rows, place, axis=0)
        return whole

    natural = jnp.arange(2 * n, dtype=jnp.int32)
    side = (natural >= n).astype(jnp.int32)
    owner = jnp.where(side == 0, natural, 2 * n - 1 - natural)
    sources = 2 * (((owner & 1) ^ core) * chips + (owner >> 1)) + side
    places = 2 * owner + side

    segments = segment_ids.reshape(total)
    starts = jnp.sum((segments[None, :] < segments[:, None]).astype(jnp.int32), axis=1)
    place = jnp.arange(total, dtype=jnp.int32) - starts
    frequency = theta_base ** (-(jnp.arange(HD // 2, dtype=high) * 2.0) / HD)
    angles = place.astype(high)[:, None] * frequency
    cosine = jnp.cos(angles)
    sine = jnp.sin(angles)
    cosine = jnp.concatenate([cosine, cosine], axis=1)
    sine = jnp.concatenate([-sine, sine], axis=1)
    segment_column = segments.reshape(total, 1)
    segment_row = segments.reshape(1, total)

    normed_parts = []
    for tokens_part in token_parts:
        features = tokens_part.astype(high)
        normed_parts.append((features * rms_factor(features) * gain_attn).astype(low))
    qkv_raw = jnp.concatenate([dot(normed, qkv_w) for normed in normed_parts], axis=0)
    tables = (cosine, sine, query_gain, key_gain, segment_column, segment_row)
    mixed_rel, mixed_abs, query, key, value, logs = attend(
        total, heads, sources, places, qkv_raw, *tables
    )
    mixed = exchange(mixed_abs.reshape(n, own, qw), CTX)
    out_blocks = out_half + [swap(block, "core") for block in out_half]
    mixed = mixed.transpose(1, 0, 2).reshape(own, n * qw)
    own_features = own_tokens.astype(high)
    branch = jnp.zeros((own, width), high)
    for block_owner, block in zip(owners, out_blocks):
        branch = lax.dynamic_update_slice_in_dim(branch, dot(mixed, block), block_owner * out_cols, axis=1)
    middle = own_features + branch
    factor_ffn = rms_factor(middle)
    ffn_own = (middle * factor_ffn * gain_ffn).astype(low)
    ffn_parts = gather(ffn_own)
    upstream_parts = (upstream_half, swap(upstream_half, "core"))

    hidden_parts, gates = [], []
    for ffn_low in ffn_parts:
        gate_up = dot(ffn_low, gate_up_w)
        gate, up = gate_up[:, :hidden], gate_up[:, hidden:]
        sigmoid = jax.nn.sigmoid(gate)
        silu = gate * sigmoid
        hidden_parts.append((silu * up).astype(low))
        gates.append((up * sigmoid * (1.0 + gate * (1.0 - sigmoid)), silu))
    grad_down = own_hidden(sum_parts(hidden_parts, upstream_parts))
    grad_down, down_w = after(grad_down, down_w)
    gate_up_grads = []
    for upstream_low, (gate_slope, silu) in zip(upstream_parts, gates):
        grad_hidden = dot_t(upstream_low, down_w)
        grads = [(grad_hidden * gate_slope).astype(low), (grad_hidden * silu).astype(low)]
        gate_up_grads.append(jnp.concatenate(grads, axis=1))
    grad_ffn = [dot_t(grads, gate_up_w).astype(low) for grads in gate_up_grads]
    grad_gate_up = by_layer(sum_parts(ffn_parts, gate_up_grads))
    grad_ffn = send_chips(sum_cores(grad_ffn[0], grad_ffn[1]))
    grad_down = scatter_rows(grad_down)
    grad_ffn, grad_gate_up = after(grad_ffn, grad_gate_up)
    grad_gate_up = scatter_rows(grad_gate_up)

    grad_middle, middle_low, grad_gain_ffn, mixed_grad = project_back(
        jnp.stack(owners), grad_ffn, middle, own_cotangent, gain_ffn.reshape(1, -1), out_blocks
    )
    mixed_grad, grad_down, *hidden_parts = after(mixed_grad, grad_down, *hidden_parts)
    block_parts = [dot(values, down_w).astype(low) for values in hidden_parts]
    block_half = sum_cores(block_parts[0], block_parts[1])
    mixed_grad, block_half = after(exchange(mixed_grad, CTX), block_half)
    block_sum = sum_chips(block_half)
    mixed_grad = mixed_grad.reshape(total, qw)
    qkv_grad, grad_gains = attend_back(
        total, heads, sources, places, qkv_raw, *tables, query, key, value, logs, mixed_grad
    )
    qkv_grads = halves(qkv_grad)
    grad_attn = [dot_t(grads, qkv_w).astype(low) for grads in qkv_grads]
    attn_half = sum_cores(grad_attn[0], grad_attn[1])
    grad_qkv = sum_parts(normed_parts, qkv_grads).reshape(n, m * strip, -1)
    block_sum, grad_qkv, late_low = after(block_sum, grad_qkv, middle_low)
    late_half = in_order(spread(late_low, "chip"), chip)
    grad_out = sum_parts(halves(mixed_rel), (late_half, swap(late_half, "core")))
    block_out = (middle + block_sum).astype(low).reshape(tokens.shape)
    grad_qkv = exchange(grad_qkv, CTX).reshape(n, m, strip, -1)

    def all_heads(grads):
        return grads.transpose(1, 2, 0, 3).reshape(m, strip, -1)

    def grad_of_kv(grads):
        grads = jnp.sum(grads.reshape(KVH, repeat, m, strip, HD).astype(high), axis=1)
        return all_heads(grads.astype(low))

    grad_late = [
        all_heads(grad_qkv[..., :qw]),
        grad_of_kv(grad_qkv[..., qw : qw + HD]),
        grad_of_kv(grad_qkv[..., qw + HD :]),
        grad_out.reshape(m, strip, width),
    ]
    grad_late = jnp.concatenate(grad_late, axis=2).reshape(m * strip, -1)
    grad_late, attn_half = after(grad_late, attn_half)
    grad_attn = sum_chips(attn_half)
    grad_late = scatter_rows(grad_late)

    grad_attn, grad_gate_up = after(grad_attn, grad_gate_up)
    grad_gate_up = exchange(grad_gate_up.reshape(n, strip, -1), CTX)
    factor_attn = rms_factor(own_features)
    scaled = gain_attn * grad_attn
    inner = mean_last(own_features * scaled)
    input_grad = grad_middle + factor_attn * scaled - own_features * factor_attn**3 * inner
    grad_gain_attn = jnp.sum(grad_attn * own_features * factor_attn, axis=0)
    input_grad = input_grad.reshape(tokens.shape)

    devices = n * m
    partial = jnp.concatenate(
        [
            grad_gain_attn.reshape(devices, -1),
            grad_gain_ffn.reshape(devices, -1),
            grad_gains[0].reshape(devices, -1),
            grad_gains[1].reshape(devices, -1),
        ],
        axis=1,
    )
    grad_gate_up, partial = after(grad_gate_up, partial)
    gains = exchange(partial, CTX + LAYER)
    gains = jnp.sum(gains, axis=0)
    grad_down = grad_down.astype(high)
    grad_gate, grad_up = arrange(grad_gate_up, piece)
    end = 2 * strip + HD // devices
    gains = (gains[:strip], gains[strip : 2 * strip], gains[2 * strip : end], gains[end:])
    grad_late, *gains = after(grad_late, *gains)
    widths = (n * qw, KVH * HD, KVH * HD, width)
    grad_query, grad_key, grad_value, grad_out = widen(grad_late, widths)

    return (
        block_out,
        input_grad,
        gains[0],
        grad_query,
        grad_key,
        grad_value,
        gains[2],
        gains[3],
        grad_out,
        gains[1],
        grad_gate,
        grad_up,
        grad_down,
    )


def solution(mesh):
    n, m = mesh.shape["ctx"], mesh.shape["fsdp"]
    mesh = Mesh(mesh.devices.reshape(n // 2, 2, m // 2, 2), CTX + LAYER)
    rows = P(LAYER, None)
    line = P(LAYER)
    blocks = P(LAYER, None, CTX, None, None)
    both = P(CTX + LAYER, None)
    both_line = P(CTX + LAYER)
    in_specs = (blocks, rows, blocks, line, rows, rows, rows, line, line, rows, line, rows, rows, rows)
    out_specs = (
        blocks,
        blocks,
        both_line,
        both,
        both,
        both,
        both_line,
        both_line,
        both,
        both_line,
        both,
        both,
        both,
    )
    return jax.shard_map(local, mesh=mesh, in_specs=in_specs, out_specs=out_specs, check_vma=False)
```
